32 devices in a mesh: dp: 32 (over z, y, x, core).
Axes of the slice: x: 2, y: 2, z: 4, core: 2. Of those that a mesh axis runs over, the one named last changes fastest.
Arguments:
- tokens: bfloat16 [16384, 384], P('dp'), may hold values from -6 to 6
- gain_attn: bfloat16 [384], P('dp'), may hold values from 0.5 to 1.5
- w_qkv: bfloat16 [384, 1152], P('dp'), may hold values from -0.3125 to 0.3125
- w_proj: bfloat16 [384, 384], P('dp'), may hold values from -0.875 to 0.875
- gain_moe: bfloat16 [384], P('dp'), may hold values from 0.5 to 1.5
- w_router: bfloat16 [384, 8], P('dp'), may hold values from -0.3125 to 0.3125
- w_in: bfloat16 [32, 384, 384], P('dp'), may hold values from -0.3125 to 0.3125
- w_out: bfloat16 [32, 384, 384], P('dp'), may hold values from -1.25 to 1.25
- cotangent: bfloat16 [16384, 384], P('dp'), may hold values from -6 to 6
- image_ids: int32 [16384], P('dp'), may hold values from 0 to 109, never falling along the last dimension, each value on 1 to 197 neighbouring positions
- expert_ids: int32 [16384, 2], P('dp'), may hold values from 0 to 7, as said below
- slots: int32 [16384, 2], P('dp'), may hold values from -1 to 159, as said below
Outputs:
- mixed: bfloat16 [16384, 384], P('dp')
- grad_tokens: bfloat16 [16384, 384], P('dp')
- grad_gain_attn: float32 [384], P('dp')
- grad_w_qkv: float32 [384, 1152], P('dp')
- grad_w_proj: float32 [384, 384], P('dp')
- grad_gain_moe: float32 [384], P('dp')
- grad_w_router: float32 [384, 8], P('dp')
- grad_w_in: float32 [32, 384, 384], P('dp')
- grad_w_out: float32 [32, 384, 384], P('dp')
The draws below stay inside these ranges and needn't reach their ends.
Inputs may be any that keep to these rules, and one draw needn't show every extreme that they name: `image_ids`: image numbers never fall along the rows; an image has 1 to 197 rows, and some image has exactly 197. `expert_ids`: the two experts of a row differ. Within one device's 512 rows, the choices naming an expert take slots 0, 1, 2, ... in the order of all first choices by row, then all second choices by row; choices beyond 160 get -1; in every draw some expert gets all 160 slots from every device.
All inputs are finite; a program needn't handle non-finite values.
Results may differ from the reference program's by a relative error of at most 0.017.
Values may be sent and summed in bfloat16 or wider, within the bound.
No kernel may reach another device: no remote copies, remote signals or barrier semaphores. Data moves between devices by JAX's collectives and lax.ppermute only.
A program may use at most 128 MiB of HBM per device.

```python
import math
import jax
import jax.numpy as jnp
import numpy as np
from jax import lax

D = 384
HEADS = 6
HEAD_DIM = 64
FF = 1536
LEN = 197
TOK_DEV = 512
EXPERTS = 8
CAP = 160
TOKENS = 16384
IMAGES = 110
N_DP = 32


def block_order(key):
    return jax.random.permutation(key, TOK_DEV)


def routing(key):
    blocks = TOKENS // TOK_DEV
    hot = jax.random.randint(jax.random.fold_in(key, 11), (), 0, EXPERTS)
    random_first = jax.random.randint(jax.random.fold_in(key, 12), (TOKENS,), 0, EXPERTS)
    offset = jax.random.randint(jax.random.fold_in(key, 13), (TOKENS,), 1, EXPERTS)
    block_keys = jax.random.split(jax.random.fold_in(key, 14), blocks)
    ranks = jax.vmap(block_order)(block_keys).reshape(TOKENS)
    first = jnp.where(ranks < CAP, hot, jnp.where(ranks == CAP, (hot + offset) % EXPERTS, random_first))
    second = jnp.where(ranks == CAP, hot, (first + offset) % EXPERTS)
    expert_ids = jnp.stack([first, second], axis=1).astype(jnp.int32)
    ordered = jnp.stack([first, second], axis=0).reshape(2, blocks, TOK_DEV).transpose(1, 0, 2).reshape(blocks, 2 * TOK_DEV)
    onehot = (ordered[:, :, None] == jnp.arange(EXPERTS)[None, None, :]).astype(jnp.int32)
    before = jnp.cumsum(onehot, axis=1) - onehot
    position = jnp.sum(before * onehot, axis=2)
    slot_values = jnp.where(position < CAP, position, -1)
    slots = slot_values.reshape(blocks, 2, TOK_DEV).transpose(1, 0, 2).reshape(2, TOKENS).T
    return (expert_ids, slots.astype(jnp.int32))


def draw_expert_ids(key, part):
    return routing(key)[0]


def draw_slots(key, part):
    return routing(key)[1]


def block_scale(key, shape, cuts, least, largest):
    loudness = 1.0
    for dim, blocks in cuts:
        steps = jax.random.uniform(jax.random.fold_in(jax.random.fold_in(key, 6), dim), (blocks,), jnp.float32, least / len(cuts), largest / len(cuts))
        loudness = loudness * jnp.repeat(jnp.exp(steps), shape[dim] // blocks).reshape((-1,) + (1,) * (len(shape) - 1 - dim))
    return loudness


def length_profile(number_of, total, reach, slope):
    weights = [(1 << 20) // math.isqrt(standing ** slope) + 1 for standing in range(2, number_of + 1)]
    spare, holding = total - reach - (number_of - 1), [1] * (number_of - 1)
    while spare > 0:
        movable = [i for i in range(number_of - 1) if holding[i] < reach]
        mass, left = sum([weights[i] for i in movable]), spare
        for i in movable:
            extra = min(reach - holding[i], max(1, left * weights[i] // mass), spare)
            holding[i] = holding[i] + extra
            spare = spare - extra
    return np.array([reach] + holding)


def uneven(key, count, total, most, lean):
    if count == 2:
        one = jax.random.randint(key, (), max(1, total - most), min(most, total - 1) + 1)
        return jnp.stack([one, total - one])
    lengths = jnp.asarray(length_profile(count, total, most, lean), jnp.int32)
    couples = (count - 1) // 2
    donor, receiver = lengths[1:1 + 2 * couples:2], lengths[2:2 + 2 * couples:2]
    room = jnp.minimum(donor - 1, most - receiver)
    passed = jax.random.randint(jax.random.fold_in(key, 1), (couples,), 0, 1 << 20) % (room + 1)
    lengths = lengths.at[1:1 + 2 * couples:2].set(donor - passed).at[2:2 + 2 * couples:2].set(receiver + passed)
    return lengths[jax.random.permutation(jax.random.fold_in(key, 2), count)]


def gaussian(stream_key, dims, spread, bound, cuts=(), held_as=jnp.bfloat16):
    level = block_scale(stream_key, dims, cuts, -0.22, 0.18) if cuts else 1.0
    values = jax.random.normal(stream_key, dims, jnp.float32) * spread * level
    return jnp.minimum(jnp.maximum(values, -bound), bound).astype(held_as)


def setup_inputs(seed: int = 0) -> dict:
    streams_of = jax.random.split(jax.random.key(seed), 13)
    return {
        "tokens": gaussian(streams_of[0], (TOKENS, D), 1.0, 6.0, ((0, 32),)),
        "gain_attn": jnp.clip(1.0 + 0.1 * jax.random.normal(streams_of[1], (D,), jnp.float32), 0.5, 1.5).astype(jnp.bfloat16),
        "w_qkv": gaussian(streams_of[2], (D, 3 * D), D ** -0.5, 0.3125, ((0, 32),)),
        "w_proj": gaussian(streams_of[3], (D, D), (D // 8) ** -0.5, 0.875, ((0, 32),)),
        "gain_moe": jnp.clip(1.0 + 0.1 * jax.random.normal(streams_of[4], (D,), jnp.float32), 0.5, 1.5).astype(jnp.bfloat16),
        "w_router": gaussian(streams_of[5], (D, EXPERTS), D ** -0.5, 0.3125, ((0, 32),)),
        "w_in": gaussian(streams_of[6], (N_DP, D, FF // 4), D ** -0.5, 0.3125, ((0, 32),)),
        "w_out": gaussian(streams_of[7], (N_DP, FF // 4, D), (max(1, FF // (EXPERTS * EXPERTS))) ** -0.5, 1.25, ((0, 32),)),
        "cotangent": gaussian(streams_of[8], (TOKENS, D), 1.0, 6.0, ((0, 32),)),
        "image_ids": jnp.searchsorted(jnp.cumsum(uneven(streams_of[9], IMAGES, TOKENS, LEN, 1)), jnp.arange(TOKENS), side="right").astype(jnp.int32),
        "expert_ids": draw_expert_ids(jax.random.fold_in(streams_of[12], 71), 0),
        "slots": draw_slots(jax.random.fold_in(streams_of[12], 71), 0),
    }


@jax.custom_vjp
def low(v):
    return lax.optimization_barrier(v.astype(jnp.bfloat16)).astype(jnp.float32)

@jax.custom_vjp
def low_back(v):
    return v

def low_keep(v):
    return (low(v), None)

def low_pass(kept, grad):
    return (grad,)

def back_keep(v):
    return (v, None)

def back_low(kept, grad):
    return (low(grad),)
low.defvjp(low_keep, low_pass)
low_back.defvjp(back_keep, back_low)
EPSILON = 1e-06
MASKED = -1e+30

def layer_norm(values, gain):
    centered = values - lax.optimization_barrier(jnp.mean(values, axis=-1, keepdims=True))
    variance = lax.optimization_barrier(jnp.mean(centered * centered, axis=-1, keepdims=True))
    return centered * lax.rsqrt(variance + EPSILON) * gain

def matmul(left, right):
    return jnp.dot(left, right, precision=lax.Precision.HIGHEST, preferred_element_type=jnp.float32)

def attend(qkv, image_ids):
    rim_width = LEN - 1
    queries = qkv[:, :D]
    keys = jnp.pad(qkv[:, D:2 * D], ((rim_width, rim_width), (0, 0)))
    values = jnp.pad(qkv[:, 2 * D:], ((rim_width, rim_width), (0, 0)))
    key_ids = jnp.pad(image_ids, (rim_width, rim_width), constant_values=-1)
    key_count = TOK_DEV + 2 * rim_width
    scale = HEAD_DIM ** (-0.5)

    def one_block(index):
        start = index * TOK_DEV
        query_block = lax.dynamic_slice_in_dim(queries, start, TOK_DEV, 0).reshape(TOK_DEV, HEADS, HEAD_DIM)
        key_block = lax.dynamic_slice_in_dim(keys, start, key_count, 0).reshape(key_count, HEADS, HEAD_DIM)
        value_block = lax.dynamic_slice_in_dim(values, start, key_count, 0).reshape(key_count, HEADS, HEAD_DIM)
        query_ids = lax.dynamic_slice_in_dim(image_ids, start, TOK_DEV, 0)
        block_ids = lax.dynamic_slice_in_dim(key_ids, start, key_count, 0)
        scores = low_back(jnp.einsum('qhd,khd->hqk', query_block, key_block, precision=lax.Precision.HIGHEST) * scale)
        same_image = query_ids[:, None] == block_ids[None, :]
        masked = jnp.where(same_image[None], scores, MASKED)
        total = jax.nn.logsumexp(masked, axis=-1, keepdims=True)
        weights = low(jnp.exp(masked - total))
        result = jnp.einsum('hqk,khd->qhd', weights, value_block, precision=lax.Precision.HIGHEST)
        return result.reshape(TOK_DEV, D)
    blocks = lax.map(jax.checkpoint(one_block), jnp.arange(TOKENS // TOK_DEV, dtype=jnp.int32))
    return blocks.reshape(TOKENS, D)

def expert_block(items):
    rows_in, first, second = items
    total = jnp.zeros(rows_in.shape, jnp.float32)
    for quarter in range(4):
        pre = low_back(matmul(rows_in, first[quarter]))
        hidden = low(jax.nn.gelu(pre))
        total = total + low(matmul(hidden, second[quarter]))
    return low_back(total)

def forward(tokens, gain_attn, w_qkv, w_proj, gain_moe, w_router, w_in, w_out, image_ids, expert_ids, slots):
    normed_one = low(layer_norm(tokens, gain_attn))
    qkv = low_back(low(matmul(normed_one, w_qkv)))
    attended = low_back(low(attend(qkv, image_ids)))
    middle = tokens + low_back(matmul(attended, w_proj))
    normed_two = low(layer_norm(middle, gain_moe))
    logits = low_back(matmul(normed_two, w_router))
    router_probs = jax.nn.softmax(logits, axis=-1)
    gates = jnp.take_along_axis(router_probs, expert_ids, axis=1)
    kept = slots >= 0
    source = jnp.arange(TOKENS, dtype=jnp.int32) // TOK_DEV
    buffer_rows = EXPERTS * N_DP * CAP
    place = jnp.where(kept, (expert_ids * N_DP + source[:, None]) * CAP + slots, buffer_rows).astype(jnp.int32)
    rows_in = jnp.broadcast_to(normed_two[:, None, :], (TOKENS, 2, D)).reshape(2 * TOKENS, D)
    filled = jnp.zeros((buffer_rows, D), jnp.float32).at[place.reshape(-1)].set(rows_in, mode='drop')
    grouped = filled.reshape(EXPERTS, N_DP * CAP, D)
    outputs = lax.map(jax.checkpoint(expert_block), (grouped, w_in.reshape(EXPERTS, 4, D, FF // 4), w_out.reshape(EXPERTS, 4, FF // 4, D)))
    picked = outputs.reshape(buffer_rows, D)[jnp.minimum(place, buffer_rows - 1)]
    pair_gates = jnp.where(kept, gates, 0.0)
    return middle + lax.optimization_barrier(jnp.sum(picked * pair_gates[:, :, None], axis=1))

def reference(tokens, gain_attn, w_qkv, w_proj, gain_moe, w_router, w_in, w_out, cotangent, image_ids, expert_ids, slots):
    floats = (tokens, gain_attn, w_qkv, w_proj, gain_moe, w_router, w_in, w_out)
    floats = tuple((item.astype(jnp.float32) for item in floats))

    def apply(*params):
        return forward(*params, image_ids, expert_ids, slots)
    result, pullback = jax.vjp(apply, *floats)
    grads = pullback(cotangent.astype(jnp.float32))
    return (result.astype(jnp.bfloat16), grads[0].astype(jnp.bfloat16), grads[1], grads[2], grads[3], grads[4], grads[5], grads[6], grads[7])
```

```python
import functools

import jax
import jax.numpy as jnp
import numpy as np
from jax import lax
from jax.experimental import pallas as pl
from jax.experimental.pallas import tpu as pltpu
from jax.sharding import PartitionSpec as P

HEAD_DIM = 64
LEN = 197
EPSILON = 1e-06
MASKED = -1e30
HALO = 256
BLOCK = 128
WINDOW = BLOCK + 2 * HALO
LANES = 128
SCALE = HEAD_DIM ** (-0.5)
BF = jnp.bfloat16
F32 = jnp.float32
GELU_C = (2.0 / np.pi) ** 0.5
GELU_A = 0.044715


def dot(left, right, left_dim=1, right_dim=0):
    return lax.dot_general(
        left,
        right,
        (((left_dim,), (right_dim,)), ((), ())),
        preferred_element_type=F32,
    )


def call(body, outs, ins, scratch=(), flops=0, name=None, vmem_mib=12, fetch=False):
    vmem = pl.BlockSpec(memory_space=pltpu.VMEM)
    spec = pl.BlockSpec(memory_space=pl.ANY) if fetch else vmem
    return pl.pallas_call(
        body,
        out_shape=tuple(outs),
        in_specs=[spec] * len(ins),
        out_specs=tuple([vmem] * len(outs)),
        scratch_shapes=list(scratch),
        compiler_params=pltpu.CompilerParams(vmem_limit_bytes=vmem_mib * 1024 * 1024),
        cost_estimate=pl.CostEstimate(flops=int(flops), bytes_accessed=1024, transcendentals=0),
        name=name,
    )(*ins)


def shape(dims, dtype):
    return jax.ShapeDtypeStruct(dims, dtype)


def lane_iota(rows, lanes=LANES):
    return lax.broadcasted_iota(jnp.int32, (rows, lanes), 1)


def fetched(refs, held, sems):
    copies = [
        pltpu.make_async_copy(ref, into, sems.at[index])
        for index, (ref, into) in enumerate(zip(refs, held))
    ]
    for copy in copies:
        copy.start()
    for copy in copies:
        copy.wait()


def pack_body(experts, *refs):
    out, held, sems = refs[5], refs[6:11], refs[11]
    fetched(refs[:5], held, sems)
    w_qkv, w_proj, router_turned, gain_attn, gain_moe = held
    share, cols = w_qkv.shape
    width = cols // 3
    out[:, :cols] = w_qkv[...]
    out[:, cols : 4 * width] = w_proj[...]
    lanes = lane_iota(share)
    diagonal = lax.broadcasted_iota(jnp.int32, (share, share), 0) == lane_iota(share, share)
    pick = lax.broadcasted_iota(jnp.int32, (experts, LANES), 0) == lane_iota(experts)
    tail = dot(router_turned[...], pick.astype(F32).astype(BF), 0, 0)
    for index, gain in enumerate((gain_attn, gain_moe)):
        column = jnp.sum(
            jnp.where(diagonal, gain[...].astype(F32), 0.0), axis=1, keepdims=True
        )
        tail = jnp.where(lanes == experts + index, column, tail)
    out[:, 4 * width :] = tail.astype(BF)


def front_body(width, tokens_ref, ids_ref, own, low, high, tokens, ids, sems):
    fetched((tokens_ref, ids_ref), (tokens, ids), sems)
    rows = tokens.shape[0]
    own[:, :width] = tokens[...]
    for index in range(rows // BLOCK):
        line = (ids[index : index + 1, :] + 1).astype(F32)
        column = jnp.broadcast_to(line, (BLOCK, BLOCK)).T
        upper = jnp.floor(column * (1.0 / 256.0))
        lower = column - 256.0 * upper
        own[index * BLOCK : (index + 1) * BLOCK, width:] = jnp.where(
            lane_iota(BLOCK) == 0, upper, lower
        ).astype(BF)
    low[...] = own[rows - HALO :, :]
    high[...] = own[:HALO, :]


def quarter_body(width, w_in, w_out, quarter, sems):
    fetched(
        (w_in.at[0], w_out.at[0]), (quarter.at[:width, :], quarter.at[width:, :]), sems
    )


def join_body(parts, *refs):
    pieces, outs = refs[:-parts], refs[-parts:]
    whole = jnp.concatenate([piece[...].astype(F32) for piece in pieces], axis=0).astype(BF)
    size = whole.shape[0] // parts
    for index, out in enumerate(outs):
        out[...] = whole[index * size : (index + 1) * size, :]


def prepare_body(
    width,
    experts,
    capacity,
    own,
    low,
    high,
    order,
    experts_row,
    slots_row,
    xhat,
    rstd_out,
    select,
    idcol,
    idrow,
    routes,
    place_row,
):
    me = lax.axis_index("dp")
    devices = 4 * experts
    share = width // devices
    target = (me ^ order[0:1, :]) * share + order[1:2, :]
    sel = (lax.broadcasted_iota(jnp.int32, (width, width), 0) == target).astype(F32).astype(BF)
    select[...] = sel
    start = 0
    for ref in (low, own, high):
        rows = ref.shape[0]
        values = dot(ref[:, :width], sel)
        mean = jnp.mean(values, axis=1, keepdims=True)
        centered = values - mean
        rstd = lax.rsqrt(jnp.mean(centered * centered, axis=1, keepdims=True) + EPSILON)
        xhat[start : start + rows, :] = centered * rstd
        rstd_out[start : start + rows, :] = jnp.broadcast_to(rstd, (rows, LANES))
        marks = ref[:, width : width + LANES].astype(F32)
        column = marks[:, 0:1] * 256.0 + marks[:, 1:2]
        idcol[start : start + rows, :] = jnp.broadcast_to(column, (rows, LANES))
        turned = marks.T
        line = turned[0:1, :] * 256.0 + turned[1:2, :]
        idrow[:, start : start + rows] = jnp.broadcast_to(line, (8, rows))
        start += rows
    rows = own.shape[0]
    group = (((me >> 2) & (experts // 2 - 1)) << 1) | (me & 1)
    half_bits = (experts // 2).bit_length() - 1
    expert = experts_row[...]
    slot = slots_row[...]
    holder = ((expert & (experts // 2 - 1)) << 1) | (expert >> half_bits)
    place = jnp.where(slot >= 0, (group ^ holder) * capacity + slot, -1).astype(F32)
    lines = jnp.concatenate(
        [place, expert.astype(F32), jnp.zeros((4, rows), F32)], axis=0
    )
    place_row[...] = lines
    routes[...] = jnp.concatenate([lines] * (LANES // 8), axis=0).T


def stacked(values, half):
    zero = jnp.zeros_like(values)
    return jnp.concatenate(
        [jnp.where(half, values, zero), jnp.where(half, zero, values)], axis=0
    )


def forward_body(
    width,
    experts,
    capacity,
    xhat,
    idcol,
    idrow,
    select,
    own,
    cotangent,
    routes,
    place_row,
    near_one,
    near_two,
    far_one,
    far_two,
    *outs,
):
    chunks = outs[:experts]
    qkv, attended, lse, middle, normed_two, probs, normed, weights, weights_tail, gain = outs[
        experts:
    ]
    rows = own.shape[0]
    span = xhat.shape[0]
    cols = 3 * width
    parts = (near_one, near_two, far_one, far_two)
    size = width // 4
    for index, part in enumerate(parts):
        weights[index * size : (index + 1) * size, :] = part[:, :cols]
    sel = select[...]
    tail = jnp.concatenate([part[:, cols:] for part in parts], axis=0)
    gain_row = tail[:, width:].astype(F32).T[experts : experts + 1, :]
    gain[...] = jnp.broadcast_to(gain_row, (8, width))
    natural = dot(sel, tail)
    weights_tail[...] = natural.astype(BF)
    gain_two = natural[:, width:].T[experts + 1 : experts + 2, :]
    normed[...] = (xhat[...] * gain_row).astype(BF)
    qkv[HALO : HALO + rows, :] = dot(normed[HALO : HALO + rows, :], weights[...]).astype(BF)
    for first in (0, HALO + rows):
        qkv[first : first + HALO, width:] = dot(
            normed[first : first + HALO, :], weights[:, width:]
        ).astype(BF)
    half = lane_iota(BLOCK) < HEAD_DIM

    def attend(block, carry):
        base = pl.multiple_of(block * BLOCK, BLOCK)
        marks = idcol[pl.ds(base + HALO, BLOCK), 0:1]
        same = marks == idrow[0:1, pl.ds(base, WINDOW)]
        same = jnp.concatenate([same, same], axis=0)
        totals = jnp.zeros((BLOCK, LANES), F32)
        for pair in range(width // LANES):
            start = pair * LANES
            queries = qkv[pl.ds(base + HALO, BLOCK), start : start + LANES]
            queries = stacked((queries.astype(F32) * SCALE).astype(BF), half)
            keys = qkv[pl.ds(base, WINDOW), width + start : width + start + LANES]
            values = qkv[pl.ds(base, WINDOW), 2 * width + start : 2 * width + start + LANES]
            scores = jnp.where(same, dot(queries, keys, 1, 1), MASKED)
            peak = jnp.max(scores, axis=1, keepdims=True)
            raised = jnp.exp(scores - peak)
            total = jnp.sum(raised, axis=1, keepdims=True)
            result = dot(raised.astype(BF), values) / total
            attended[pl.ds(base, BLOCK), start : start + LANES] = jnp.where(
                half, result[:BLOCK], result[BLOCK:]
            ).astype(BF)
            logs = peak + jnp.log(total)
            lanes = lane_iota(BLOCK)
            totals = jnp.where(lanes == 2 * pair, logs[:BLOCK], totals)
            totals = jnp.where(lanes == 2 * pair + 1, logs[BLOCK:], totals)
        lse[pl.ds(base, BLOCK), :] = totals
        return carry

    lax.fori_loop(0, rows // BLOCK, attend, 0)
    mid = own[:, :width].astype(F32) + dot(attended[...], weights_tail[:, :width])
    middle[...] = mid
    centered = mid - jnp.mean(mid, axis=1, keepdims=True)
    variance = jnp.mean(centered * centered, axis=1, keepdims=True)
    low_two = (centered * lax.rsqrt(variance + EPSILON) * gain_two).astype(BF)
    normed_two[...] = low_two
    lanes = lane_iota(rows)
    logits = jnp.where(lanes < experts, dot(low_two, weights_tail[:, width:]), MASKED)
    raised = jnp.exp(logits - jnp.max(logits, axis=1, keepdims=True))
    share = raised / jnp.sum(raised, axis=1, keepdims=True)
    probs[...] = share
    upstream = cotangent[...].astype(F32)
    scaled = []
    wide_lanes = lanes.astype(F32)
    for choice in range(2):
        gate = jnp.sum(
            jnp.where(wide_lanes == routes[:, 2 + choice : 3 + choice], share, 0.0),
            axis=1,
            keepdims=True,
        )
        scaled.append((gate * upstream).astype(BF))
    scaled = jnp.concatenate(scaled, axis=0)
    for index, chunk in enumerate(chunks):
        slot = (
            lax.broadcasted_iota(jnp.int32, (capacity, rows), 0) + index * capacity
        ).astype(F32)
        first = (slot == place_row[0:1, :]).astype(F32)
        second = (slot == place_row[1:2, :]).astype(F32)
        chunk[:, :width] = dot((first + second).astype(BF), low_two).astype(BF)
        chunk[:, width:] = dot(
            jnp.concatenate([first, second], axis=1).astype(BF), scaled
        ).astype(BF)


def joined(pieces, held):
    capacity = pieces[0].shape[0]
    for index, piece in enumerate(pieces):
        held[index * capacity : (index + 1) * capacity, :] = piece[...]


def expert_body(width, tile, count, *refs):
    pieces, (kept, sent), rest = refs[:count], refs[count : count + 2], refs[count + 2 :]
    returns, (hidden_out, grad_out, arrived, back) = rest[:count], rest[count:]
    joined(pieces, arrived)
    size = 2 * width
    weights = [pair.at[at : at + size, :] for pair in (kept, sent) for at in (0, size)]

    def step(index, carry):
        at = pl.ds(pl.multiple_of(index * tile, tile), tile)
        rows = arrived[at, :width]
        grads = arrived[at, width:]
        total = jnp.zeros((tile, width), F32)
        total_grad = jnp.zeros((tile, width), F32)
        for quarter, weight in enumerate(weights):
            first, second = weight[:width, :], weight[width:, :]
            columns = slice(quarter * width, (quarter + 1) * width)
            pre = dot(rows, first)
            square = pre * pre
            bend = jnp.tanh(GELU_C * pre * (1.0 + GELU_A * square))
            hidden = (0.5 * pre * (1.0 + bend)).astype(BF)
            slope = 0.5 * (1.0 + bend) + 0.5 * pre * (1.0 - bend * bend) * (
                GELU_C * (1.0 + 3.0 * GELU_A * square)
            )
            pre_grad = (dot(grads, second, 1, 1) * slope).astype(BF)
            total = total + dot(hidden, second)
            total_grad = total_grad + dot(pre_grad, first, 1, 1)
            hidden_out[at, columns] = hidden
            grad_out[at, columns] = pre_grad
        back[at, :width] = total.astype(BF)
        back[at, width:] = total_grad.astype(BF)
        return carry

    lax.fori_loop(0, arrived.shape[0] // tile, step, 0)
    capacity = pieces[0].shape[0]
    for index, out in enumerate(returns):
        out[...] = back[index * capacity : (index + 1) * capacity, :]


def expert_grad_body(width, count, *refs):
    hidden, pre_grad, kept, sent, arrived = refs[count:]
    joined(refs[:count], arrived)
    size = 2 * width
    outs = (kept.at[:size, :], kept.at[size:, :], sent.at[:size, :], sent.at[size:, :])
    for quarter, out in enumerate(outs):
        columns = slice(quarter * width, (quarter + 1) * width)
        out[:width, :] = dot(arrived[:, :width], pre_grad[:, columns], 0, 0).astype(out.dtype)
        out[width:, :] = dot(hidden[:, columns], arrived[:, width:], 0, 0).astype(out.dtype)


def at_home(half):
    me = lax.axis_index("dp")
    return (me >= half) == ((me & 1) == 1)


def choose_body(half, size, near_one, near_two, far_one, far_two, kept, sent):
    home = at_home(half)

    @pl.when(home)
    def _():
        kept[:size, :], kept[size:, :] = near_one[...], near_two[...]
        sent[:size, :], sent[size:, :] = far_one[...], far_two[...]

    @pl.when(jnp.logical_not(home))
    def _():
        kept[:size, :], kept[size:, :] = far_one[...], far_two[...]
        sent[:size, :], sent[size:, :] = near_one[...], near_two[...]


def split_body(half, size, mine, theirs, home_one, home_two, away_one, away_two):
    home = at_home(half)

    @pl.when(home)
    def _():
        home_one[...], home_two[...] = mine[:size, :], mine[size:, :]
        away_one[...], away_two[...] = theirs[:size, :], theirs[size:, :]

    @pl.when(jnp.logical_not(home))
    def _():
        home_one[...], home_two[...] = theirs[:size, :], theirs[size:, :]
        away_one[...], away_two[...] = mine[:size, :], mine[size:, :]


def combine_body(
    width,
    experts,
    capacity,
    middle,
    normed_two,
    probs,
    cotangent,
    routes,
    attended,
    weights_tail,
    select,
    *refs,
):
    mixed, middle_grad, attended_grad, tail_grad, held = refs[experts:]
    joined(refs[:experts], held)
    rows = middle.shape[0]
    slots = experts * capacity
    gain_two = weights_tail[:, width:].astype(F32).T[experts + 1 : experts + 2, :]
    gain_grad = jnp.zeros((1, width), F32)
    router_rows = []
    branch_rows = []
    tile = 128
    for start in range(0, rows, tile):
        at = slice(start, start + tile)
        lanes = lane_iota(tile).astype(F32)
        wide = lax.broadcasted_iota(jnp.int32, (tile, slots), 1).astype(F32)
        first = (wide == routes[at, 0:1]).astype(F32)
        second = (wide == routes[at, 1:2]).astype(F32)
        picked = dot(
            jnp.concatenate([first, second], axis=0).astype(BF), held[:, :width]
        )
        grad_two = dot((first + second).astype(BF), held[:, width:])
        upstream = cotangent[at, :].astype(F32)
        share = probs[at, :]
        mid = middle[at, :]
        total = mid
        probs_grad = jnp.zeros((tile, LANES), F32)
        for choice in range(2):
            chosen = lanes == routes[at, 2 + choice : 3 + choice]
            gate = jnp.sum(jnp.where(chosen, share, 0.0), axis=1, keepdims=True)
            one = picked[choice * tile : (choice + 1) * tile, :]
            total = total + gate * one
            gate_grad = jnp.sum(one * upstream, axis=1, keepdims=True)
            probs_grad = probs_grad + jnp.where(chosen, gate_grad, 0.0)
        mixed[at, :] = total.astype(BF)
        logits_grad = (
            share * (probs_grad - jnp.sum(share * probs_grad, axis=1, keepdims=True))
        ).astype(BF)
        router_rows.append(logits_grad)
        grad_two = grad_two + dot(logits_grad, weights_tail[:, width:], 1, 1)
        centered = mid - jnp.mean(mid, axis=1, keepdims=True)
        variance = jnp.mean(centered * centered, axis=1, keepdims=True)
        rstd = lax.rsqrt(variance + EPSILON)
        xhat = centered * rstd
        gain_grad = gain_grad + jnp.sum(grad_two * xhat, axis=0, keepdims=True)
        inner = grad_two * gain_two
        inner_grad = rstd * (
            inner
            - jnp.mean(inner, axis=1, keepdims=True)
            - xhat * jnp.mean(inner * xhat, axis=1, keepdims=True)
        )
        through = upstream + inner_grad
        middle_grad[at, :] = through
        branch = through.astype(BF)
        branch_rows.append(branch)
        attended_grad[at, :] = dot(branch, weights_tail[:, :width], 1, 1).astype(BF)
    sel = select[...]
    logits_grad = jnp.concatenate(router_rows, axis=0)
    branch = jnp.concatenate(branch_rows, axis=0)
    attended_turned = dot(attended[...], sel).astype(BF)
    normed_turned = dot(normed_two[...], sel).astype(BF)
    tail_grad[:, :width] = dot(attended_turned, branch, 0, 0).astype(BF)
    gain_line = jnp.broadcast_to(gain_grad, (8, width))
    upper = gain_line.astype(BF)
    lower = (gain_line - upper.astype(F32)).astype(BF)
    gain_turned = dot(upper, sel) + dot(lower, sel)
    gain_column = jnp.broadcast_to(gain_turned[0:1, :], (LANES, width)).T
    router_grad = dot(normed_turned, logits_grad, 0, 0)
    tail_grad[:, width:] = jnp.where(
        lane_iota(width) == experts + 1, gain_column, router_grad
    ).astype(BF)


def backward_body(
    width,
    qkv,
    lse,
    attended_grad,
    idcol,
    idrow,
    normed,
    tail_grad,
    dq,
    rims_low,
    rims_high,
    inner,
    kept,
    sent_one,
    sent_two,
    acc,
):
    rows = attended_grad.shape[0]
    half_rows = width // 2
    half = lane_iota(BLOCK) < HEAD_DIM
    acc[...] = jnp.zeros_like(acc)

    def attend(block, carry):
        base = pl.multiple_of(block * BLOCK, BLOCK)
        marks = idcol[pl.ds(base + HALO, BLOCK), 0:1]
        same = marks == idrow[0:1, pl.ds(base, WINDOW)]
        same = jnp.concatenate([same, same], axis=0)
        totals = lse[pl.ds(base, BLOCK), :]
        for pair in range(width // LANES):
            start = pair * LANES
            queries = qkv[pl.ds(base + HALO, BLOCK), start : start + LANES]
            queries = stacked((queries.astype(F32) * SCALE).astype(BF), half)
            grads = stacked(attended_grad[pl.ds(base, BLOCK), start : start + LANES], half)
            keys = qkv[pl.ds(base, WINDOW), width + start : width + start + LANES]
            values = qkv[pl.ds(base, WINDOW), 2 * width + start : 2 * width + start + LANES]
            logs = jnp.concatenate(
                [totals[:, 2 * pair : 2 * pair + 1], totals[:, 2 * pair + 1 : 2 * pair + 2]], axis=0
            )
            scores = jnp.where(same, dot(queries, keys, 1, 1), MASKED)
            weights = jnp.exp(scores - logs)
            weights_grad = dot(grads, values, 1, 1)
            product = weights * weights_grad
            delta = jnp.sum(product, axis=1, keepdims=True)
            scores_grad = (product - weights * delta).astype(BF)
            low_weights = weights.astype(BF)
            window = pl.ds(base, WINDOW)
            acc[window, start : start + LANES] += dot(scores_grad, queries, 0, 0)
            acc[window, width + start : width + start + LANES] += dot(low_weights, grads, 0, 0)
            result = dot(scores_grad, keys)
            dq[pl.ds(base, BLOCK), start : start + LANES] = (
                jnp.where(half, result[:BLOCK], result[BLOCK:]) * SCALE
            ).astype(BF)
        return carry

    lax.fori_loop(0, rows // BLOCK, attend, 0)
    rims_low[...] = acc[:HALO, :].astype(BF)
    rims_high[...] = acc[HALO + rows :, :].astype(BF)
    inner[...] = acc[HALO : HALO + rows, :]
    own = normed[HALO : HALO + rows, :]
    query_part = dot(own, dq[...], 0, 0)
    kept[:, :width] = query_part[:half_rows]
    other_part = dot(normed[...], acc[...].astype(BF), 0, 0)
    kept[:, width : 3 * width] = other_part[:half_rows]
    kept[:, 3 * width :] = tail_grad[:half_rows, :].astype(F32)
    size = half_rows // 2
    for start, sent in ((half_rows, sent_one), (half_rows + size, sent_two)):
        at = slice(start, start + size)
        sent[:, :width] = query_part[at].astype(BF)
        sent[:, width : 3 * width] = other_part[at].astype(BF)
        sent[:, 3 * width :] = tail_grad[at, :]


def finish_body(
    width, dq, inner, from_low, from_high, weights, normed_gain, xhat, rstd, select, middle_grad, out, grad
):
    rows = dq.shape[0]
    experts_lane = 0
    grad[...] = inner[...]
    grad[:HALO, :] += from_low[...].astype(F32)
    grad[rows - HALO :, :] += from_high[...].astype(F32)
    values = dot(dq[...], weights[:, :width], 1, 1) + dot(
        grad[...].astype(BF), weights[:, width:], 1, 1
    )
    hat = xhat[HALO : HALO + rows, :]
    values = values * normed_gain[0:1, :]
    part = rstd[HALO : HALO + rows, 0:1] * (
        values
        - jnp.mean(values, axis=1, keepdims=True)
        - hat * jnp.mean(values * hat, axis=1, keepdims=True)
    )
    upper = part.astype(BF)
    lower = (part - upper.astype(F32)).astype(BF)
    sel = select[...]
    out[...] = (middle_grad[...] + dot(upper, sel, 1, 1) + dot(lower, sel, 1, 1)).astype(BF)


def sum_body(parts, own, *refs):
    arrived, outs = refs[: len(refs) - parts], refs[len(refs) - parts :]
    total = own[...].astype(F32)
    if arrived[0].shape[0] < total.shape[0]:
        total = total + jnp.concatenate([ref[...].astype(F32) for ref in arrived], axis=0)
    else:
        for ref in arrived:
            total = total + ref[...].astype(F32)
    size = total.shape[0] // parts
    for index, out in enumerate(outs):
        out[...] = total[index * size : (index + 1) * size, :].astype(out.dtype)


def final_body(width, experts, own, *refs):
    arrived, rest = refs[:-12], refs[-12:]
    w_qkv, gain, *parts, qkv_grad, proj_grad, router_grad, one, two, in_grad, out_grad = rest
    total = own[...]
    for ref in arrived:
        total = total + ref[...].astype(F32)
    qkv = total[:, : 3 * width]
    qkv_grad[...] = qkv
    proj_grad[...] = total[:, 3 * width : 4 * width]
    gain_grad = jnp.sum(qkv * w_qkv[...].astype(F32), axis=1, keepdims=True)
    tail = total[:, 4 * width :]
    share = own.shape[0]
    diagonal = lax.broadcasted_iota(jnp.int32, (share, share), 0) == lane_iota(share, share)

    def turned(column):
        return jnp.sum(jnp.where(diagonal, column, 0.0), axis=0, keepdims=True)

    one[...] = turned(gain_grad) / gain[...].astype(F32)
    two[...] = turned(tail[:, experts + 1 : experts + 2])
    for index in range(experts):
        router_grad[index : index + 1, :] = turned(tail[:, index : index + 1])
    for out, at in ((in_grad, slice(0, width)), (out_grad, slice(width, 2 * width))):
        first, second, third = (part[at, :].astype(F32) for part in parts)
        out[0] = first + second + third


def gather_stages(devices):
    bits = devices.bit_length() - 1
    stages = []
    top = bits - 1
    while top >= 1:
        if top >= 2:
            low, high = 1 << (top - 1), 1 << top
            stages.append([low, high, low | high])
            top -= 2
        else:
            stages.append([1 << top])
            top -= 1
    stages.append([1])
    return stages


def swap(value, devices, mask):
    return lax.ppermute(value, "dp", [(i, i ^ mask) for i in range(devices)])


def reduce_scattered(kept, sent, devices, stages, before):
    total = kept
    arrived = [swap(part, devices, stages[-1][0]) for part in sent]
    for level in range(len(stages) - 1, 0, -1):
        masks = stages[level - 1]
        parts = 1 + len(masks)
        dims = (total.shape[0] // parts, total.shape[1])
        outs = [shape(dims, F32)] + [shape(dims, BF)] * (parts - 1)
        if level == 2:
            arrived, before = lax.optimization_barrier((arrived, before))
        pieces = call(
            functools.partial(sum_body, parts), outs, [total] + arrived, name=f"sum{level}"
        )
        total = pieces[0]
        arrived = [swap(piece, devices, mask) for piece, mask in zip(pieces[1:], masks)]
    return total, arrived, before


def per_device(
    tokens,
    gain_attn,
    w_qkv,
    w_proj,
    gain_moe,
    w_router,
    w_in,
    w_out,
    cotangent,
    image_ids,
    expert_ids,
    slots,
):
    devices = lax.axis_size("dp")
    experts = devices // 4
    rows, width = tokens.shape
    capacity = max(2, 5 * rows // (2 * experts))
    share = width // devices
    span = rows + 2 * HALO
    stages = gather_stages(devices)
    everyone = range(devices)
    half = devices // 2

    ins = [w_qkv, w_proj, w_router.T, gain_attn[None, :], gain_moe[None, :]]
    packed = call(
        functools.partial(pack_body, experts),
        [shape((share, 4 * width + LANES), BF)],
        ins,
        scratch=[pltpu.VMEM(x.shape, x.dtype) for x in ins]
        + [pltpu.SemaphoreType.DMA((len(ins),))],
        name="pack",
        fetch=True,
    )[0]
    ins = [tokens, image_ids.reshape(rows // BLOCK, BLOCK)]
    own, low, high = call(
        functools.partial(front_body, width),
        [
            shape((rows, width + LANES), BF),
            shape((HALO, width + LANES), BF),
            shape((HALO, width + LANES), BF),
        ],
        ins,
        scratch=[pltpu.VMEM(x.shape, x.dtype) for x in ins]
        + [pltpu.SemaphoreType.DMA((len(ins),))],
        name="front",
        fetch=True,
    )
    up = [(i, i + 1) for i in range(devices - 1)]
    down = [(i + 1, i) for i in range(devices - 1)]
    low = lax.ppermute(low, "dp", up)
    high = lax.ppermute(high, "dp", down)
    quarter = call(
        functools.partial(quarter_body, width),
        [shape((2 * width, width), BF)],
        [w_in, w_out],
        scratch=[pltpu.SemaphoreType.DMA((2,))],
        name="quarter",
        fetch=True,
    )[0]
    order = [0]
    near = [packed]
    far = None
    for stage in stages:
        order = [a ^ mask for mask in [0] + stage for a in order]
        arrived = [swap(part, devices, mask) for mask in stage for part in near]
        if stage is stages[0]:
            quarter_far, arrived, low, high = lax.optimization_barrier(
                (quarter, arrived, low, high)
            )
        if stage is stages[-2]:
            quarter_near, arrived = lax.optimization_barrier((quarter, arrived))
        if stage is stages[-1]:
            far = arrived
        else:
            parts = 2 if stage is stages[-2] else 1
            size = near[0].shape[0] * (1 + len(stage)) // parts
            near = call(
                functools.partial(join_body, parts),
                [shape((size, near[0].shape[1]), BF)] * parts,
                [*near, *arrived],
                name="join",
            )
    order = np.stack(
        [
            np.repeat(np.array(order, np.int32), share),
            np.tile(np.arange(share, dtype=np.int32), devices),
        ]
    )

    near_half = [quarter, swap(quarter_near, devices, 2)]
    far_quarter = swap(quarter_far, devices, half)

    masks = [((p >> 1) << 2) | (p & 1) for p in range(experts)]

    def exchange(parts):
        return [parts[0]] + [swap(parts[p], devices, masks[p]) for p in range(1, experts)]

    xhat, rstd, select, idcol, idrow, routes, place_row = call(
        functools.partial(prepare_body, width, experts, capacity),
        [
            shape((span, width), F32),
            shape((span, LANES), F32),
            shape((width, width), BF),
            shape((span, LANES), F32),
            shape((8, span), F32),
            shape((rows, LANES), F32),
            shape((8, rows), F32),
        ],
        [own, low, high, jnp.asarray(order), expert_ids.T, slots.T],
        flops=2 * span * width * width,
        name="prepare",
    )
    outs = call(
        functools.partial(forward_body, width, experts, capacity),
        [shape((capacity, 2 * width), BF)] * experts
        + [
            shape((span, 3 * width), BF),
            shape((rows, width), BF),
            shape((rows, LANES), F32),
            shape((rows, width), F32),
            shape((rows, width), BF),
            shape((rows, LANES), F32),
            shape((span, width), BF),
            shape((width, 3 * width), BF),
            shape((width, width + LANES), BF),
            shape((8, width), F32),
        ],
        [xhat, idcol, idrow, select, own, cotangent, routes, place_row, *near, *far],
        name="forward",
    )
    chunks = outs[:experts]
    qkv, attended, lse, middle, normed_two, probs, normed, weights, weights_tail, gain = outs[
        experts:
    ]

    far_quarter, lse = lax.optimization_barrier((far_quarter, lse))
    far_half = [far_quarter, swap(far_quarter, devices, 2)]
    arrived = exchange(chunks)
    slot_count = experts * capacity
    pair = shape((4 * width, width), BF)
    far_half[1], *arrived[1:-1] = lax.optimization_barrier((far_half[1], *arrived[1:-1]))
    kept_pair, sent_pair = call(
        functools.partial(choose_body, half, 2 * width),
        [pair, pair],
        [*near_half, *far_half],
        name="choose",
    )
    expert_weights = [kept_pair, swap(sent_pair, devices, 1)]
    tile = slot_count // 4
    held = pltpu.VMEM((slot_count, 2 * width), BF)
    outs = call(
        functools.partial(expert_body, width, tile, experts),
        [shape((capacity, 2 * width), BF)] * experts
        + [shape((slot_count, 4 * width), BF)] * 2,
        [*arrived, *expert_weights],
        scratch=[held, held],
        flops=8 * slot_count * width * 4 * width,
        name="expert",
    )
    back, hidden, pre_grad = outs[:experts], outs[experts], outs[experts + 1]
    returned = exchange(back)

    kept_pair, sent_pair = call(
        functools.partial(expert_grad_body, width, experts),
        [pair, pair],
        [*arrived, hidden, pre_grad],
        scratch=[held],
        flops=4 * slot_count * width * 4 * width,
        name="expert_grad",
    )
    other_pair = swap(sent_pair, devices, 1)
    single = shape((2 * width, width), BF)
    home_kept, home_sent, away_kept, away_sent = call(
        functools.partial(split_body, half, 2 * width),
        [single] * 4,
        [kept_pair, other_pair],
        name="split",
    )
    away_came = swap(away_sent, devices, 2)
    home_came = swap(home_sent, devices, 2)
    away = call(
        functools.partial(sum_body, 1), [single], [away_kept, away_came], name="away"
    )[0]

    mixed, middle_grad, attended_grad, tail_grad = call(
        functools.partial(combine_body, width, experts, capacity),
        [
            shape((rows, width), BF),
            shape((rows, width), F32),
            shape((rows, width), BF),
            shape((width, width + LANES), BF),
        ],
        [
            middle,
            normed_two,
            probs,
            cotangent,
            routes,
            attended,
            weights_tail,
            select,
            *returned,
        ],
        scratch=[pltpu.VMEM((slot_count, 2 * width), BF)],
        flops=6 * rows * slot_count * width,
        name="combine",
    )
    attended_grad, away = lax.optimization_barrier((attended_grad, away))
    expert_parts = [home_kept, home_came, swap(away, devices, half)]
    half_rows = width // 2

    dq, rims_low, rims_high, inner, kept, *sent = call(
        functools.partial(backward_body, width),
        [
            shape((rows, width), BF),
            shape((HALO, 2 * width), BF),
            shape((HALO, 2 * width), BF),
            shape((rows, 2 * width), F32),
            shape((half_rows, 4 * width + LANES), F32),
            shape((half_rows // 2, 4 * width + LANES), BF),
            shape((half_rows // 2, 4 * width + LANES), BF),
        ],
        [qkv, lse, attended_grad, idcol, idrow, normed, tail_grad],
        scratch=[pltpu.VMEM((span, 2 * width), F32)],
        name="backward",
    )
    from_high = lax.ppermute(rims_low, "dp", down)
    from_low = lax.ppermute(rims_high, "dp", up)
    total, last, expert_parts = reduce_scattered(kept, sent, devices, stages, expert_parts)
    qkv_grad, proj_grad, router_grad, gain_one_grad, gain_two_grad, in_grad, out_grad = call(
        functools.partial(final_body, width, experts),
        [
            shape((share, 3 * width), F32),
            shape((share, width), F32),
            shape((experts, share), F32),
            shape((1, share), F32),
            shape((1, share), F32),
            shape((1, width, width), F32),
            shape((1, width, width), F32),
        ],
        [total, *last, w_qkv, gain_attn[None, :], *expert_parts],
        name="final",
    )
    grad_tokens = call(
        functools.partial(finish_body, width),
        [shape((rows, width), BF)],
        [dq, inner, from_low, from_high, weights, gain, xhat, rstd, select, middle_grad],
        scratch=[pltpu.VMEM((rows, 2 * width), F32)],
        flops=2 * rows * width * 5 * width,
        name="finish",
    )[0]

    return (
        mixed,
        grad_tokens,
        gain_one_grad.reshape(share),
        qkv_grad,
        proj_grad,
        gain_two_grad.reshape(share),
        router_grad.T,
        in_grad,
        out_grad,
    )


def solution(mesh):
    row, line, cube = P("dp", None), P("dp"), P("dp", None, None)
    return jax.shard_map(
        per_device,
        mesh=mesh,
        in_specs=(row, line, row, row, line, row, cube, cube, row, line, row, row),
        out_specs=(row, row, line, row, row, line, row, cube, cube),
        check_vma=False,
    )
```

```python
import functools

import jax
import jax.numpy as jnp
import numpy as np
from jax import lax
from jax.experimental import pallas as pl
from jax.experimental.pallas import tpu as pltpu
from jax.sharding import PartitionSpec as P

HEAD_DIM = 64
LEN = 197
EPSILON = 1e-06
MASKED = -1e30
HALO = 256
BLOCK = 128
WINDOW = BLOCK + 2 * HALO
LANES = 128
SCALE = HEAD_DIM ** (-0.5)
BF = jnp.bfloat16
F32 = jnp.float32
GELU_C = (2.0 / np.pi) ** 0.5
GELU_A = 0.044715


def dot(left, right, left_dim=1, right_dim=0):
    return lax.dot_general(
        left,
        right,
        (((left_dim,), (right_dim,)), ((), ())),
        preferred_element_type=F32,
    )


def call(body, outs, ins, scratch=(), flops=0, name=None, vmem_mib=12, fetch=False):
    vmem = pl.BlockSpec(memory_space=pltpu.VMEM)
    spec = pl.BlockSpec(memory_space=pltpu.HBM) if fetch else vmem
    if fetch:
        ins = [pltpu.with_memory_space_constraint(x, pltpu.HBM) for x in ins]
    return pl.pallas_call(
        body,
        out_shape=tuple(outs),
        in_specs=[spec] * len(ins),
        out_specs=tuple([vmem] * len(outs)),
        scratch_shapes=list(scratch),
        compiler_params=pltpu.CompilerParams(vmem_limit_bytes=vmem_mib * 1024 * 1024),
        cost_estimate=pl.CostEstimate(flops=int(flops), bytes_accessed=1024, transcendentals=0),
        name=name,
    )(*ins)


def shape(dims, dtype):
    return jax.ShapeDtypeStruct(dims, dtype)


def lane_iota(rows, lanes=LANES):
    return lax.broadcasted_iota(jnp.int32, (rows, lanes), 1)


def fetched(refs, held, sems):
    copies = [
        pltpu.make_async_copy(ref, into, sems.at[index])
        for index, (ref, into) in enumerate(zip(refs, held))
    ]
    for copy in copies:
        copy.start()
    for copy in copies:
        copy.wait()


def pack_body(experts, *refs):
    out, held, sems = refs[5], refs[6:11], refs[11]
    fetched(refs[:5], held, sems)
    w_qkv, w_proj, router_turned, gain_attn, gain_moe = held
    share, cols = w_qkv.shape
    width = cols // 3
    out[:, :cols] = w_qkv[...]
    out[:, cols : 4 * width] = w_proj[...]
    lanes = lane_iota(share)
    diagonal = lax.broadcasted_iota(jnp.int32, (share, share), 0) == lane_iota(share, share)
    pick = lax.broadcasted_iota(jnp.int32, (experts, LANES), 0) == lane_iota(experts)
    tail = dot(router_turned[...], pick.astype(F32).astype(BF), 0, 0)
    for index, gain in enumerate((gain_attn, gain_moe)):
        column = jnp.sum(
            jnp.where(diagonal, gain[...].astype(F32), 0.0), axis=1, keepdims=True
        )
        tail = jnp.where(lanes == experts + index, column, tail)
    out[:, 4 * width :] = tail.astype(BF)


def front_body(width, tokens_ref, ids_ref, own, low, high, tokens, ids, sems):
    fetched((tokens_ref, ids_ref), (tokens, ids), sems)
    rows = tokens.shape[0]
    own[:, :width] = tokens[...]
    for index in range(rows // BLOCK):
        line = (ids[index : index + 1, :] + 1).astype(F32)
        column = jnp.broadcast_to(line, (BLOCK, BLOCK)).T
        upper = jnp.floor(column * (1.0 / 256.0))
        lower = column - 256.0 * upper
        own[index * BLOCK : (index + 1) * BLOCK, width:] = jnp.where(
            lane_iota(BLOCK) == 0, upper, lower
        ).astype(BF)
    low[...] = own[rows - HALO :, :]
    high[...] = own[:HALO, :]


def quarter_body(width, w_in, w_out, quarter, sems):
    fetched(
        (w_in.at[0], w_out.at[0]), (quarter.at[:width, :], quarter.at[width:, :]), sems
    )


def join_body(parts, *refs):
    pieces, outs = refs[:-parts], refs[-parts:]
    whole = jnp.concatenate([piece[...].astype(F32) for piece in pieces], axis=0).astype(BF)
    size = whole.shape[0] // parts
    for index, out in enumerate(outs):
        out[...] = whole[index * size : (index + 1) * size, :]


def prepare_body(
    width,
    experts,
    capacity,
    own,
    low,
    high,
    order,
    experts_row,
    slots_row,
    xhat,
    rstd_out,
    select,
    idcol,
    idrow,
    routes,
    place_row,
):
    me = lax.axis_index("dp")
    devices = 4 * experts
    share = width // devices
    target = (me ^ order[0:1, :]) * share + order[1:2, :]
    sel = (lax.broadcasted_iota(jnp.int32, (width, width), 0) == target).astype(F32).astype(BF)
    select[...] = sel
    start = 0
    for ref in (low, own, high):
        rows = ref.shape[0]
        values = dot(ref[:, :width], sel)
        mean = jnp.mean(values, axis=1, keepdims=True)
        centered = values - mean
        rstd = lax.rsqrt(jnp.mean(centered * centered, axis=1, keepdims=True) + EPSILON)
        xhat[start : start + rows, :] = centered * rstd
        rstd_out[start : start + rows, :] = jnp.broadcast_to(rstd, (rows, LANES))
        marks = ref[:, width : width + LANES].astype(F32)
        column = marks[:, 0:1] * 256.0 + marks[:, 1:2]
        idcol[start : start + rows, :] = jnp.broadcast_to(column, (rows, LANES))
        turned = marks.T
        line = turned[0:1, :] * 256.0 + turned[1:2, :]
        idrow[:, start : start + rows] = jnp.broadcast_to(line, (8, rows))
        start += rows
    rows = own.shape[0]
    group = (((me >> 2) & (experts // 2 - 1)) << 1) | (me & 1)
    half_bits = (experts // 2).bit_length() - 1
    expert = experts_row[...]
    slot = slots_row[...]
    holder = ((expert & (experts // 2 - 1)) << 1) | (expert >> half_bits)
    apart = group ^ holder
    index = (apart & 1) * (experts // 2) + (apart >> 1)
    place = jnp.where(slot >= 0, index * capacity + slot, -1).astype(F32)
    lines = jnp.concatenate(
        [place, expert.astype(F32), jnp.zeros((4, rows), F32)], axis=0
    )
    place_row[...] = lines
    routes[...] = jnp.concatenate([lines] * (LANES // 8), axis=0).T


def stacked(values, half):
    zero = jnp.zeros_like(values)
    return jnp.concatenate(
        [jnp.where(half, values, zero), jnp.where(half, zero, values)], axis=0
    )


def forward_body(
    width,
    experts,
    capacity,
    xhat,
    idcol,
    idrow,
    select,
    own,
    cotangent,
    routes,
    place_row,
    near_one,
    near_two,
    far_one,
    far_two,
    *outs,
):
    same_core, other_core, outs = outs[0], outs[1 : 1 + experts // 2], outs[1 + experts // 2 :]
    qkv, attended, lse, middle, normed_two, probs, normed, weights, weights_tail, gain = outs
    rows = own.shape[0]
    span = xhat.shape[0]
    cols = 3 * width
    parts = (near_one, near_two, far_one, far_two)
    size = width // 4
    for index, part in enumerate(parts):
        weights[index * size : (index + 1) * size, :] = part[:, :cols]
    sel = select[...]
    tail = jnp.concatenate([part[:, cols:] for part in parts], axis=0)
    gain_row = tail[:, width:].astype(F32).T[experts : experts + 1, :]
    gain[...] = jnp.broadcast_to(gain_row, (8, width))
    natural = dot(sel, tail)
    weights_tail[...] = natural.astype(BF)
    gain_two = natural[:, width:].T[experts + 1 : experts + 2, :]
    normed[...] = (xhat[...] * gain_row).astype(BF)
    qkv[HALO : HALO + rows, :] = dot(normed[HALO : HALO + rows, :], weights[...]).astype(BF)
    for first in (0, HALO + rows):
        qkv[first : first + HALO, width:] = dot(
            normed[first : first + HALO, :], weights[:, width:]
        ).astype(BF)
    half = lane_iota(BLOCK) < HEAD_DIM

    def attend(block, carry):
        base = pl.multiple_of(block * BLOCK, BLOCK)
        window = pl.ds(base, WINDOW)
        here = pl.ds(base, BLOCK)
        marks = idrow[0:1, pl.ds(base + HALO, BLOCK)]
        same = idcol[window, 0:1] == jnp.concatenate([marks, marks], axis=1)
        for pair in range(width // LANES):
            start = pair * LANES
            queries = qkv[pl.ds(base + HALO, BLOCK), start : start + LANES]
            queries = stacked((queries.astype(F32) * SCALE).astype(BF), half)
            keys = qkv[window, width + start : width + start + LANES]
            values = qkv[window, 2 * width + start : 2 * width + start + LANES]
            scores = jnp.where(same, dot(keys, queries, 1, 1), MASKED)
            peak = jnp.max(scores, axis=0, keepdims=True)
            raised = jnp.exp(scores - peak)
            total = jnp.sum(raised, axis=0, keepdims=True)
            result = dot(raised.astype(BF), values, 0, 0)
            column = jnp.broadcast_to(1.0 / total, (8, 2 * BLOCK)).T[:, 0:1]
            result = result * column
            attended[here, start : start + LANES] = jnp.where(
                half, result[:BLOCK], result[BLOCK:]
            ).astype(BF)
            logs = peak + jnp.log(total)
            lse[2 * pair : 2 * pair + 1, here] = logs[:, :BLOCK]
            lse[2 * pair + 1 : 2 * pair + 2, here] = logs[:, BLOCK:]
        return carry

    lax.fori_loop(0, rows // BLOCK, attend, 0, unroll=4)
    mid = own[:, :width].astype(F32) + dot(attended[...], weights_tail[:, :width])
    middle[...] = mid
    centered = mid - jnp.mean(mid, axis=1, keepdims=True)
    variance = jnp.mean(centered * centered, axis=1, keepdims=True)
    low_two = (centered * lax.rsqrt(variance + EPSILON) * gain_two).astype(BF)
    normed_two[...] = low_two
    lanes = lane_iota(rows)
    logits = jnp.where(lanes < experts, dot(low_two, weights_tail[:, width:]), MASKED)
    raised = jnp.exp(logits - jnp.max(logits, axis=1, keepdims=True))
    share = raised / jnp.sum(raised, axis=1, keepdims=True)
    probs[...] = share
    upstream = cotangent[...].astype(F32)
    wide_lanes = lanes.astype(F32)
    gates = []
    for choice in range(2):
        gate = jnp.sum(
            jnp.where(wide_lanes == routes[:, 2 + choice : 3 + choice], share, 0.0),
            axis=1,
            keepdims=True,
        )
        gates.append(jnp.broadcast_to(gate, (rows, 8)))
    gates = jnp.concatenate(gates + [jnp.zeros((rows, LANES - 16), F32)], axis=1).T
    source = jnp.concatenate([low_two, cotangent[...]], axis=1)
    for index in range(experts):
        if index < experts // 2:
            chunk = same_core.at[index * capacity : (index + 1) * capacity, :]
        else:
            chunk = other_core[index - experts // 2]
        slot = (
            lax.broadcasted_iota(jnp.int32, (capacity, rows), 0) + index * capacity
        ).astype(F32)
        first = slot == place_row[0:1, :]
        second = slot == place_row[1:2, :]
        weight = jnp.where(first, gates[0:1, :], jnp.where(second, gates[8:9, :], 0.0))
        taken = jnp.where(first | second, 1.0, 0.0)
        moved = dot(taken.astype(BF), source)
        chunk[:, :width] = moved[:, :width].astype(BF)
        chunk[:, width:] = (
            moved[:, width:] * jnp.sum(weight, axis=1, keepdims=True)
        ).astype(BF)


def joined(pieces, held):
    capacity = pieces[0].shape[0]
    for index, piece in enumerate(pieces):
        held[index * capacity : (index + 1) * capacity, :] = piece[...]


def expert_body(width, tile, count, *refs):
    pieces, kept, sent, rest = (
        refs[:count],
        refs[count],
        refs[count + 1 : count + 5],
        refs[count + 5 :],
    )
    returns, (hidden_out, grad_out, arrived, back, w_in, w_out) = rest[:count], rest[count:]
    joined(pieces, arrived)
    w_ins = [kept.at[:width, :], kept.at[2 * width : 3 * width, :], sent[0], sent[2]]
    w_outs = [kept.at[width : 2 * width, :], kept.at[3 * width :, :], sent[1], sent[3]]
    for quarter, (first, second) in enumerate(zip(w_ins, w_outs)):
        at = slice(quarter * width, (quarter + 1) * width)
        w_in[:, at] = first[...]
        w_out[at, :] = second[...]
    step_width = 2 * width // 3

    def step(index, carry):
        at = pl.ds(pl.multiple_of(index * tile, tile), tile)
        for start in range(0, 4 * width, step_width):
            columns = slice(start, start + step_width)
            pre = dot(arrived[at, :width], w_in[:, columns])
            hidden_grad = dot(arrived[at, width:], w_out[columns, :], 1, 1)
            square = pre * pre
            bend = jnp.tanh(pre * (GELU_C + (GELU_C * GELU_A) * square))
            scaled = 0.5 * pre
            hidden_out[at, columns] = (scaled + scaled * bend).astype(BF)
            slope = (0.5 + 0.5 * bend) + (
                scaled * (GELU_C + (3.0 * GELU_C * GELU_A) * square)
            ) * (1.0 - bend * bend)
            grad_out[at, columns] = (hidden_grad * slope).astype(BF)
        back[at, :width] = dot(hidden_out[at, :], w_out[...]).astype(BF)
        back[at, width:] = dot(grad_out[at, :], w_in[...], 1, 1).astype(BF)
        return carry

    lax.fori_loop(0, arrived.shape[0] // tile, step, 0)
    capacity = pieces[0].shape[0]
    for index, out in enumerate(returns):
        out[...] = back[index * capacity : (index + 1) * capacity, :]


def expert_grad_body(width, count, *refs):
    hidden, pre_grad, kept, sent, arrived = refs[count:]
    joined(refs[:count], arrived)
    size = 2 * width
    outs = (kept.at[:size, :], kept.at[size:, :], sent.at[:size, :], sent.at[size:, :])
    grad_in = dot(arrived[:, :width], pre_grad[...], 0, 0)
    for quarter, out in enumerate(outs):
        out[:width, :] = grad_in[:, quarter * width : (quarter + 1) * width].astype(BF)
    grad_out = dot(arrived[:, width:], hidden[...], 0, 0)
    for quarter, out in enumerate(outs):
        out[width:, :] = grad_out[:, quarter * width : (quarter + 1) * width].T.astype(BF)


def at_home(half):
    me = lax.axis_index("dp")
    return (me >= half) == ((me & 1) == 1)


def halve_body(whole, upper, lower):
    size = upper.shape[0]
    upper[...] = whole[:size, :]
    lower[...] = whole[size:, :]


def choose_body(half, size, near_one, near_in, near_out, *refs):
    far, kept, sent = refs[:4], refs[4], refs[5:]
    near = (near_one.at[:size, :], near_one.at[size:, :], near_in, near_out)

    def place(mine, theirs):
        for index, (one, two) in enumerate(zip(mine, theirs)):
            kept[index * size : (index + 1) * size, :] = one[...]
            sent[index][...] = two[...]

    @pl.when(at_home(half))
    def _():
        place(near, far)

    @pl.when(jnp.logical_not(at_home(half)))
    def _():
        place(far, near)


def mix_body(capacity, mine, *refs):
    theirs, outs = refs[: len(refs) // 2], refs[len(refs) // 2 :]
    for index, (part, out) in enumerate(zip(theirs, outs)):
        out[:capacity, :] = mine[index * capacity : (index + 1) * capacity, :]
        out[capacity:, :] = part[...]


def unmix_body(capacity, *refs):
    count = len(refs) // 2
    pieces, mine, theirs = refs[:count], refs[count], refs[count + 1 :]
    for index, (piece, out) in enumerate(zip(pieces, theirs)):
        mine[index * capacity : (index + 1) * capacity, :] = piece[:capacity, :]
        out[...] = piece[capacity:, :]


def split_body(half, size, mine, theirs, weights, normed, *outs):
    home_one, home_two, home_three, *away, keys_turned = outs
    width = size // 2
    keys_turned[...] = dot(weights[:, width : 2 * width], normed[...], 0, 1).astype(BF)

    def place(home, other):
        home_one[...] = home[:size, :]
        home_two[...], home_three[...] = home[size : 3 * size // 2, :], home[3 * size // 2 :, :]
        away[0][...] = other[:size, :]
        away[1][...], away[2][...] = other[size : 3 * size // 2, :], other[3 * size // 2 :, :]

    @pl.when(at_home(half))
    def _():
        place(mine, theirs)

    @pl.when(jnp.logical_not(at_home(half)))
    def _():
        place(theirs, mine)


def combine_body(
    width,
    experts,
    capacity,
    middle,
    normed_two,
    probs,
    cotangent,
    routes,
    attended,
    weights_tail,
    select,
    *refs,
):
    mixed, middle_grad, attended_grad, tail_grad, held = refs[-5:]
    start = 0
    for ref in refs[:-5]:
        held[start : start + ref.shape[0], :] = ref[...]
        start += ref.shape[0]
    rows = middle.shape[0]
    slots = experts * capacity
    gain_two = weights_tail[:, width:].astype(F32).T[experts + 1 : experts + 2, :]
    gain_grad = jnp.zeros((1, width), F32)
    router_rows = []
    branch_rows = []
    tile = rows
    for start in range(0, rows, tile):
        at = slice(start, start + tile)
        lanes = lane_iota(tile).astype(F32)
        wide = lax.broadcasted_iota(jnp.int32, (tile, slots), 1).astype(F32)
        first = (wide == routes[at, 0:1]).astype(F32)
        second = (wide == routes[at, 1:2]).astype(F32)
        picked = dot(
            jnp.concatenate([first, second], axis=0).astype(BF), held[:, :width]
        )
        grad_two = dot((first + second).astype(BF), held[:, width:])
        upstream = cotangent[at, :].astype(F32)
        share = probs[at, :]
        mid = middle[at, :]
        total = mid
        probs_grad = jnp.zeros((tile, LANES), F32)
        for choice in range(2):
            chosen = lanes == routes[at, 2 + choice : 3 + choice]
            gate = jnp.sum(jnp.where(chosen, share, 0.0), axis=1, keepdims=True)
            one = picked[choice * tile : (choice + 1) * tile, :]
            total = total + gate * one
            gate_grad = jnp.sum(one * upstream, axis=1, keepdims=True)
            probs_grad = probs_grad + jnp.where(chosen, gate_grad, 0.0)
        mixed[at, :] = total.astype(BF)
        logits_grad = (
            share * (probs_grad - jnp.sum(share * probs_grad, axis=1, keepdims=True))
        ).astype(BF)
        router_rows.append(logits_grad)
        grad_two = grad_two + dot(logits_grad, weights_tail[:, width:], 1, 1)
        centered = mid - jnp.mean(mid, axis=1, keepdims=True)
        variance = jnp.mean(centered * centered, axis=1, keepdims=True)
        rstd = lax.rsqrt(variance + EPSILON)
        xhat = centered * rstd
        gain_grad = gain_grad + jnp.sum(grad_two * xhat, axis=0, keepdims=True)
        inner = grad_two * gain_two
        inner_grad = rstd * (
            inner
            - jnp.mean(inner, axis=1, keepdims=True)
            - xhat * jnp.mean(inner * xhat, axis=1, keepdims=True)
        )
        through = upstream + inner_grad
        middle_grad[at, :] = through
        branch = through.astype(BF)
        branch_rows.append(branch)
        attended_grad[at, :] = dot(branch, weights_tail[:, :width], 1, 1).astype(BF)
    sel = select[...]
    logits_grad = jnp.concatenate(router_rows, axis=0)
    branch = jnp.concatenate(branch_rows, axis=0)
    attended_turned = dot(attended[...], sel).astype(BF)
    normed_turned = dot(normed_two[...], sel).astype(BF)
    tail_grad[:, :width] = dot(attended_turned, branch, 0, 0).astype(BF)
    gain_line = jnp.broadcast_to(gain_grad, (8, width))
    upper = gain_line.astype(BF)
    lower = (gain_line - upper.astype(F32)).astype(BF)
    gain_turned = dot(upper, sel) + dot(lower, sel)
    gain_column = jnp.broadcast_to(gain_turned[0:1, :], (LANES, width)).T
    router_grad = dot(normed_turned, logits_grad, 0, 0)
    tail_grad[:, width:] = jnp.where(
        lane_iota(width) == experts + 1, gain_column, router_grad
    ).astype(BF)


def backward_body(
    width,
    qkv,
    keys_turned,
    lse,
    attended_grad,
    idcol,
    idrow,
    normed,
    tail_grad,
    dq,
    rims_low,
    rims_high,
    inner,
    kept,
    *sents,
):
    rows = attended_grad.shape[0]
    half_rows = width // 2
    *sents, acc = sents
    half = lane_iota(BLOCK) < HEAD_DIM
    upper = lax.broadcasted_iota(jnp.int32, (LANES, BLOCK), 0) < HEAD_DIM
    acc[...] = jnp.zeros_like(acc)

    def attend(block, carry):
        base = pl.multiple_of(block * BLOCK, BLOCK)
        window = pl.ds(base, WINDOW)
        here = pl.ds(base, BLOCK)
        marks = idrow[0:1, pl.ds(base + HALO, BLOCK)]
        same = idcol[window, 0:1] == jnp.concatenate([marks, marks], axis=1)
        for pair in range(width // LANES):
            start = pair * LANES
            queries = qkv[pl.ds(base + HALO, BLOCK), start : start + LANES]
            queries = stacked((queries.astype(F32) * SCALE).astype(BF), half)
            grads = stacked(attended_grad[here, start : start + LANES], half)
            keys = qkv[window, width + start : width + start + LANES]
            values = qkv[window, 2 * width + start : 2 * width + start + LANES]
            logs = jnp.concatenate(
                [lse[2 * pair : 2 * pair + 1, here], lse[2 * pair + 1 : 2 * pair + 2, here]], axis=1
            )
            scores = jnp.where(same, dot(keys, queries, 1, 1), MASKED)
            weights = jnp.exp(scores - logs)
            weights_grad = dot(values, grads, 1, 1)
            delta = jnp.sum(weights * weights_grad, axis=0, keepdims=True)
            scores_grad = (weights * (weights_grad - delta)).astype(BF)
            acc[window, start : start + LANES] += dot(scores_grad, queries)
            acc[window, width + start : width + start + LANES] += dot(weights.astype(BF), grads)
            result = dot(keys_turned[start : start + LANES, window], scores_grad) * SCALE
            dq[here, start : start + LANES] = (
                jnp.where(upper, result[:, :BLOCK], result[:, BLOCK:]).T.astype(BF)
            )
        return carry

    lax.fori_loop(0, rows // BLOCK, attend, 0, unroll=4)
    rims_low[...] = acc[:HALO, :].astype(BF)
    rims_high[...] = acc[HALO + rows :, :].astype(BF)
    inner[...] = acc[HALO : HALO + rows, :]
    own = normed[HALO : HALO + rows, :]
    query_part = dot(own, dq[...], 0, 0)
    kept[:, :width] = query_part[:half_rows]
    other_part = dot(normed[...], acc[...].astype(BF), 0, 0)
    kept[:, width : 3 * width] = other_part[:half_rows]
    kept[:, 3 * width :] = tail_grad[:half_rows, :].astype(F32)
    size = half_rows // len(sents)
    for index, sent in enumerate(sents):
        at = slice(half_rows + index * size, half_rows + (index + 1) * size)
        sent[:, :width] = query_part[at].astype(BF)
        sent[:, width : 3 * width] = other_part[at].astype(BF)
        sent[:, 3 * width :] = tail_grad[at, :]


def finish_body(
    width, dq, inner, from_low, from_high, weights, normed_gain, xhat, rstd, select, middle_grad, out, grad
):
    rows = dq.shape[0]
    experts_lane = 0
    grad[...] = inner[...]
    grad[:HALO, :] += from_low[...].astype(F32)
    grad[rows - HALO :, :] += from_high[...].astype(F32)
    values = dot(dq[...], weights[:, :width], 1, 1) + dot(
        grad[...].astype(BF), weights[:, width:], 1, 1
    )
    hat = xhat[HALO : HALO + rows, :]
    values = values * normed_gain[0:1, :]
    part = rstd[HALO : HALO + rows, 0:1] * (
        values
        - jnp.mean(values, axis=1, keepdims=True)
        - hat * jnp.mean(values * hat, axis=1, keepdims=True)
    )
    upper = part.astype(BF)
    lower = (part - upper.astype(F32)).astype(BF)
    sel = select[...]
    out[...] = (middle_grad[...] + dot(upper, sel, 1, 1) + dot(lower, sel, 1, 1)).astype(BF)


def sum_body(parts, own, *refs):
    arrived, outs = refs[: len(refs) - parts], refs[len(refs) - parts :]
    total = own[...].astype(F32)
    if arrived[0].shape[0] < total.shape[0]:
        total = total + jnp.concatenate([ref[...].astype(F32) for ref in arrived], axis=0)
    else:
        for ref in arrived:
            total = total + ref[...].astype(F32)
    size = total.shape[0] // parts
    for index, out in enumerate(outs):
        out[...] = total[index * size : (index + 1) * size, :].astype(out.dtype)


def final_body(width, experts, own, *refs):
    arrived, rest = refs[:-13], refs[-13:]
    w_qkv, gain, *parts, qkv_grad, proj_grad, router_grad, one, two, in_grad, out_grad = rest
    total = own[...]
    for ref in arrived:
        total = total + ref[...].astype(F32)
    qkv = total[:, : 3 * width]
    qkv_grad[...] = qkv
    proj_grad[...] = total[:, 3 * width : 4 * width]
    gain_grad = jnp.sum(qkv * w_qkv[...].astype(F32), axis=1, keepdims=True)
    tail = total[:, 4 * width :]
    share = own.shape[0]
    diagonal = lax.broadcasted_iota(jnp.int32, (share, share), 0) == lane_iota(share, share)

    def turned(column):
        return jnp.sum(jnp.where(diagonal, column, 0.0), axis=0, keepdims=True)

    one[...] = turned(gain_grad) / gain[...].astype(F32)
    two[...] = turned(tail[:, experts + 1 : experts + 2])
    for index in range(experts):
        router_grad[index : index + 1, :] = turned(tail[:, index : index + 1])
    mine, upper, lower, other = parts
    for out, at, beside in (
        (in_grad, slice(0, width), upper),
        (out_grad, slice(width, 2 * width), lower),
    ):
        out[0] = mine[at, :].astype(F32) + beside[...].astype(F32) + other[at, :].astype(F32)


def gather_stages(devices):
    bits = devices.bit_length() - 1
    stages = []
    top = bits - 1
    while top >= 1:
        if top >= 2:
            low, high = 1 << (top - 1), 1 << top
            stages.append([low, high, low | high])
            top -= 2
        else:
            stages.append([1 << top])
            top -= 1
    stages.append([1])
    return stages


def swap(value, devices, mask):
    return lax.ppermute(value, "dp", [(i, i ^ mask) for i in range(devices)])


def reduce_scattered(kept, sent, devices, stages, before):
    total = kept
    arrived = [swap(part, devices, stages[-1][0]) for part in sent]
    for level in range(len(stages) - 1, 0, -1):
        masks = stages[level - 1]
        parts = 1 + len(masks)
        dims = (total.shape[0] // parts, total.shape[1])
        outs = [shape(dims, F32)] + [shape(dims, BF)] * (parts - 1)
        if level == 2:
            arrived, before = lax.optimization_barrier((arrived, before))
        pieces = call(
            functools.partial(sum_body, parts), outs, [total] + arrived, name=f"sum{level}"
        )
        total = pieces[0]
        arrived = [swap(piece, devices, mask) for piece, mask in zip(pieces[1:], masks)]
    return total, arrived, before


def per_device(
    tokens,
    gain_attn,
    w_qkv,
    w_proj,
    gain_moe,
    w_router,
    w_in,
    w_out,
    cotangent,
    image_ids,
    expert_ids,
    slots,
):
    devices = lax.axis_size("dp")
    experts = devices // 4
    rows, width = tokens.shape
    capacity = max(2, 5 * rows // (2 * experts))
    share = width // devices
    span = rows + 2 * HALO
    stages = gather_stages(devices)
    everyone = range(devices)
    half = devices // 2

    ins = [w_qkv, w_proj, w_router.T, gain_attn[None, :], gain_moe[None, :]]
    packed = call(
        functools.partial(pack_body, experts),
        [shape((share, 4 * width + LANES), BF)],
        ins,
        scratch=[pltpu.VMEM(x.shape, x.dtype) for x in ins]
        + [pltpu.SemaphoreType.DMA((len(ins),))],
        name="pack",
        fetch=True,
    )[0]
    first_arrived = [swap(packed, devices, mask) for mask in stages[0]]
    first_arrived[0], tokens = lax.optimization_barrier((first_arrived[0], tokens))
    packed, w_in, w_out = lax.optimization_barrier((packed, w_in, w_out))
    near_in = swap(w_in[0], devices, 2)
    near_out = swap(w_out[0], devices, 2)
    quarter = call(
        functools.partial(quarter_body, width),
        [shape((2 * width, width), BF)],
        [w_in, w_out],
        scratch=[pltpu.SemaphoreType.DMA((2,))],
        name="quarter",
        fetch=True,
    )[0]
    ins = [tokens, image_ids.reshape(rows // BLOCK, BLOCK)]
    own, low, high = call(
        functools.partial(front_body, width),
        [
            shape((rows, width + LANES), BF),
            shape((HALO, width + LANES), BF),
            shape((HALO, width + LANES), BF),
        ],
        ins,
        scratch=[pltpu.VMEM(x.shape, x.dtype) for x in ins]
        + [pltpu.SemaphoreType.DMA((len(ins),))],
        name="front",
        fetch=True,
    )
    up = [(i, i + 1) for i in range(devices - 1)]
    down = [(i + 1, i) for i in range(devices - 1)]
    low = lax.ppermute(low, "dp", up)
    high = lax.ppermute(high, "dp", down)
    order = [0]
    near = [packed]
    far = None
    for stage in stages:
        order = [a ^ mask for mask in [0] + stage for a in order]
        if stage is stages[0]:
            arrived = first_arrived
        else:
            arrived = [swap(part, devices, mask) for mask in stage for part in near]
        if stage is stages[0]:
            arrived[1], quarter, near_in = lax.optimization_barrier(
                (arrived[1], quarter, near_in)
            )
            quarter_far, low, high = lax.optimization_barrier((quarter, low, high))
        if stage is stages[-2]:
            arrived[1], near_out = lax.optimization_barrier((arrived[1], near_out))
        if stage is stages[-1]:
            far = arrived
        else:
            parts = 2 if stage is stages[-2] else 1
            size = near[0].shape[0] * (1 + len(stage)) // parts
            near = call(
                functools.partial(join_body, parts),
                [shape((size, near[0].shape[1]), BF)] * parts,
                [*near, *arrived],
                name="join",
            )
    order = np.stack(
        [
            np.repeat(np.array(order, np.int32), share),
            np.tile(np.arange(share, dtype=np.int32), devices),
        ]
    )

    far_quarter = swap(quarter_far, devices, half)

    def exchange(parts):
        return [parts[0]] + [
            swap(part, devices, 4 * index) for index, part in enumerate(parts) if index
        ]

    xhat, rstd, select, idcol, idrow, routes, place_row = call(
        functools.partial(prepare_body, width, experts, capacity),
        [
            shape((span, width), F32),
            shape((span, LANES), F32),
            shape((width, width), BF),
            shape((span, LANES), F32),
            shape((8, span), F32),
            shape((rows, LANES), F32),
            shape((8, rows), F32),
        ],
        [own, low, high, jnp.asarray(order), expert_ids.T, slots.T],
        flops=2 * span * width * width,
        name="prepare",
    )
    chips = experts // 2
    half_slots = chips * capacity
    outs = call(
        functools.partial(forward_body, width, experts, capacity),
        [shape((half_slots, 2 * width), BF)]
        + [shape((capacity, 2 * width), BF)] * chips
        + [
            shape((span, 3 * width), BF),
            shape((rows, width), BF),
            shape((8, rows), F32),
            shape((rows, width), F32),
            shape((rows, width), BF),
            shape((rows, LANES), F32),
            shape((span, width), BF),
            shape((width, 3 * width), BF),
            shape((width, width + LANES), BF),
            shape((8, width), F32),
        ],
        [xhat, idcol, idrow, select, own, cotangent, routes, place_row, *near, *far],
        name="forward",
    )
    same_core, other_core, outs = outs[0], outs[1 : 1 + chips], outs[1 + chips :]
    qkv, attended, lse, middle, normed_two, probs, normed, weights, weights_tail, gain = outs

    both = shape((2 * capacity, 2 * width), BF)
    pieces = call(
        functools.partial(mix_body, capacity),
        [both] * chips,
        [same_core, *[swap(part, devices, 1) for part in other_core]],
        name="mix",
    )
    far_quarter, piece = lax.optimization_barrier((far_quarter, pieces[0]))
    arrived = exchange([piece, *pieces[1:]])
    far_half = call(
        halve_body, [shape((width, width), BF)] * 2, [far_quarter], name="halve"
    )
    far_half = [*far_half] + [swap(part, devices, 2) for part in far_half]
    slot_count = experts * capacity
    pair = shape((4 * width, width), BF)
    far_half[-1], *arrived[1:] = lax.optimization_barrier((far_half[-1], *arrived[1:]))
    kept_pair, *sent_parts = call(
        functools.partial(choose_body, half, width),
        [pair] + [shape((width, width), BF)] * 4,
        [quarter, near_in, near_out, *far_half],
        name="choose",
    )
    expert_weights = [kept_pair] + [swap(part, devices, 1) for part in sent_parts]
    tile = slot_count // 4
    held = pltpu.VMEM((slot_count, 2 * width), BF)
    outs = call(
        functools.partial(expert_body, width, tile, chips),
        [both] * chips + [shape((slot_count, 4 * width), BF)] * 2,
        [*arrived, *expert_weights],
        scratch=[
            held,
            held,
            pltpu.VMEM((width, 4 * width), BF),
            pltpu.VMEM((4 * width, width), BF),
        ],
        vmem_mib=16,
        flops=8 * slot_count * width * 4 * width,
        name="expert",
    )
    back, hidden, pre_grad = outs[:chips], outs[chips], outs[chips + 1]
    returned = exchange(back)
    kept_pair, sent_pair = call(
        functools.partial(expert_grad_body, width, chips),
        [pair, pair],
        [*arrived, hidden, pre_grad],
        scratch=[held],
        vmem_mib=16,
        flops=4 * slot_count * width * 4 * width,
        name="expert_grad",
    )
    other_pair = swap(sent_pair, devices, 1)
    single = shape((2 * width, width), BF)
    square = shape((width, width), BF)
    home_kept, *home_sent = call(
        functools.partial(split_body, half, 2 * width),
        [single, square, square] * 2 + [shape((width, span), BF)],
        [kept_pair, other_pair, weights, normed],
        name="split",
    )
    home_sent, (away_kept, *away_sent, keys_turned) = home_sent[:2], home_sent[2:]
    away_came = [swap(part, devices, 2) for part in away_sent]
    *home_sent, returned[1] = lax.optimization_barrier((*home_sent, returned[1]))
    home_came = [swap(part, devices, 2) for part in home_sent]
    away = call(
        functools.partial(sum_body, 1), [single], [away_kept, *away_came], name="away"
    )[0]

    returned[-1], away = lax.optimization_barrier((returned[-1], away))
    mine, *theirs = call(
        functools.partial(unmix_body, capacity),
        [shape((half_slots, 2 * width), BF)] + [shape((capacity, 2 * width), BF)] * chips,
        returned,
        name="unmix",
    )
    theirs = [swap(part, devices, 1) for part in theirs]
    mixed, middle_grad, attended_grad, tail_grad = call(
        functools.partial(combine_body, width, experts, capacity),
        [
            shape((rows, width), BF),
            shape((rows, width), F32),
            shape((rows, width), BF),
            shape((width, width + LANES), BF),
        ],
        [
            middle,
            normed_two,
            probs,
            cotangent,
            routes,
            attended,
            weights_tail,
            select,
            mine,
            *theirs,
        ],
        scratch=[pltpu.VMEM((slot_count, 2 * width), BF)],
        flops=6 * rows * slot_count * width,
        name="combine",
    )
    expert_parts = [home_kept, *home_came, swap(away, devices, half)]
    half_rows = width // 2

    dq, rims_low, rims_high, inner, kept, *sent = call(
        functools.partial(backward_body, width),
        [
            shape((rows, width), BF),
            shape((HALO, 2 * width), BF),
            shape((HALO, 2 * width), BF),
            shape((rows, 2 * width), F32),
            shape((half_rows, 4 * width + LANES), F32),
        ]
        + [shape((half_rows // 2, 4 * width + LANES), BF)] * 2,
        [qkv, keys_turned, lse, attended_grad, idcol, idrow, normed, tail_grad],
        scratch=[pltpu.VMEM((span, 2 * width), F32)],
        name="backward",
    )
    from_high = lax.ppermute(rims_low, "dp", down)
    from_low = lax.ppermute(rims_high, "dp", up)
    total, last, expert_parts = reduce_scattered(kept, sent, devices, stages, expert_parts)
    qkv_grad, proj_grad, router_grad, gain_one_grad, gain_two_grad, in_grad, out_grad = call(
        functools.partial(final_body, width, experts),
        [
            shape((share, 3 * width), F32),
            shape((share, width), F32),
            shape((experts, share), F32),
            shape((1, share), F32),
            shape((1, share), F32),
            shape((1, width, width), F32),
            shape((1, width, width), F32),
        ],
        [total, *last, w_qkv, gain_attn[None, :], *expert_parts],
        name="final",
    )
    grad_tokens = call(
        functools.partial(finish_body, width),
        [shape((rows, width), BF)],
        [dq, inner, from_low, from_high, weights, gain, xhat, rstd, select, middle_grad],
        scratch=[pltpu.VMEM((rows, 2 * width), F32)],
        flops=2 * rows * width * 5 * width,
        name="finish",
    )[0]

    return (
        mixed,
        grad_tokens,
        gain_one_grad.reshape(share),
        qkv_grad,
        proj_grad,
        gain_two_grad.reshape(share),
        router_grad.T,
        in_grad,
        out_grad,
    )


def solution(mesh):
    row, line, cube = P("dp", None), P("dp"), P("dp", None, None)
    return jax.shard_map(
        per_device,
        mesh=mesh,
        in_specs=(row, line, row, row, line, row, cube, cube, row, line, row, row),
        out_specs=(row, row, line, row, row, line, row, cube, cube),
        check_vma=False,
    )
```

```python
import functools

import jax
import jax.numpy as jnp
import numpy as np
from jax import lax
from jax.experimental import pallas as pl
from jax.experimental.pallas import tpu as pltpu
from jax.sharding import PartitionSpec as P

HEAD_DIM = 64
LEN = 197
EPSILON = 1e-06
MASKED = -1e30
HALO = 256
BLOCK = 128
WINDOW = BLOCK + 2 * HALO
LANES = 128
SCALE = HEAD_DIM ** (-0.5)
BF = jnp.bfloat16
F32 = jnp.float32
GELU_C = (2.0 / np.pi) ** 0.5
GELU_A = 0.044715


def dot(left, right, left_dim=1, right_dim=0):
    return lax.dot_general(
        left,
        right,
        (((left_dim,), (right_dim,)), ((), ())),
        preferred_element_type=F32,
    )


def call(body, outs, ins, scratch=(), flops=0, name=None, vmem_mib=12, fetch=False):
    vmem = pl.BlockSpec(memory_space=pltpu.VMEM)
    spec = pl.BlockSpec(memory_space=pltpu.HBM) if fetch else vmem
    if fetch:
        ins = [pltpu.with_memory_space_constraint(x, pltpu.HBM) for x in ins]
    return pl.pallas_call(
        body,
        out_shape=tuple(outs),
        in_specs=[spec] * len(ins),
        out_specs=tuple([vmem] * len(outs)),
        scratch_shapes=list(scratch),
        compiler_params=pltpu.CompilerParams(vmem_limit_bytes=vmem_mib * 1024 * 1024),
        cost_estimate=pl.CostEstimate(flops=int(flops), bytes_accessed=1024, transcendentals=0),
        name=name,
    )(*ins)


def shape(dims, dtype):
    return jax.ShapeDtypeStruct(dims, dtype)


def lane_iota(rows, lanes=LANES):
    return lax.broadcasted_iota(jnp.int32, (rows, lanes), 1)


def fetched(refs, held, sems):
    copies = [
        pltpu.make_async_copy(ref, into, sems.at[index])
        for index, (ref, into) in enumerate(zip(refs, held))
    ]
    for copy in copies:
        copy.start()
    for copy in copies:
        copy.wait()


def pack_body(experts, *refs):
    count = 7
    (out, own, low, high), held, sems = refs[count : count + 4], refs[count + 4 : -1], refs[-1]
    fetched(refs[:count], held, sems)
    w_qkv, w_proj, router_turned, gain_attn, gain_moe, tokens, ids = held
    share, cols = w_qkv.shape
    width = cols // 3
    out[:, :cols] = w_qkv[...]
    out[:, cols : 4 * width] = w_proj[...]
    lanes = lane_iota(share)
    diagonal = lax.broadcasted_iota(jnp.int32, (share, share), 0) == lane_iota(share, share)
    pick = lax.broadcasted_iota(jnp.int32, (experts, LANES), 0) == lane_iota(experts)
    tail = dot(router_turned[...], pick.astype(F32).astype(BF), 0, 0)
    for index, gain in enumerate((gain_attn, gain_moe)):
        column = jnp.sum(
            jnp.where(diagonal, gain[...].astype(F32), 0.0), axis=1, keepdims=True
        )
        tail = jnp.where(lanes == experts + index, column, tail)
    out[:, 4 * width :] = tail.astype(BF)
    rows = tokens.shape[0]
    own[:, :width] = tokens[...]
    for index in range(rows // BLOCK):
        line = (ids[index : index + 1, :] + 1).astype(F32)
        column = jnp.broadcast_to(line, (BLOCK, BLOCK)).T
        upper = jnp.floor(column * (1.0 / 256.0))
        lower = column - 256.0 * upper
        own[index * BLOCK : (index + 1) * BLOCK, width:] = jnp.where(
            lane_iota(BLOCK) == 0, upper, lower
        ).astype(BF)
    low[...] = own[rows - HALO :, :]
    high[...] = own[:HALO, :]


def quarter_body(width, w_in, w_out, quarter, sems):
    fetched(
        (w_in.at[0], w_out.at[0]), (quarter.at[:width, :], quarter.at[width:, :]), sems
    )


def join_body(parts, *refs):
    pieces, outs = refs[:-parts], refs[-parts:]
    whole = jnp.concatenate([piece[...].astype(F32) for piece in pieces], axis=0).astype(BF)
    size = whole.shape[0] // parts
    for index, out in enumerate(outs):
        out[...] = whole[index * size : (index + 1) * size, :]


def prepare_body(
    width,
    experts,
    capacity,
    own,
    low,
    high,
    order,
    experts_row,
    slots_row,
    xhat,
    rstd_out,
    select,
    idcol,
    idrow,
    routes,
    place_row,
):
    me = lax.axis_index("dp")
    devices = 4 * experts
    share = width // devices
    target = (me ^ order[0:1, :]) * share + order[1:2, :]
    sel = (lax.broadcasted_iota(jnp.int32, (width, width), 0) == target).astype(F32).astype(BF)
    select[...] = sel
    start = 0
    for ref in (low, own, high):
        rows = ref.shape[0]
        values = dot(ref[:, :width], sel)
        mean = jnp.mean(values, axis=1, keepdims=True)
        centered = values - mean
        rstd = lax.rsqrt(jnp.mean(centered * centered, axis=1, keepdims=True) + EPSILON)
        xhat[start : start + rows, :] = centered * rstd
        rstd_out[start : start + rows, :] = jnp.broadcast_to(rstd, (rows, LANES))
        marks = ref[:, width : width + LANES].astype(F32)
        column = marks[:, 0:1] * 256.0 + marks[:, 1:2]
        idcol[start : start + rows, :] = jnp.broadcast_to(column, (rows, LANES))
        turned = marks.T
        line = turned[0:1, :] * 256.0 + turned[1:2, :]
        idrow[:, start : start + rows] = jnp.broadcast_to(line, (8, rows))
        start += rows
    rows = own.shape[0]
    group = (((me >> 2) & (experts // 2 - 1)) << 1) | (me & 1)
    half_bits = (experts // 2).bit_length() - 1
    expert = experts_row[...]
    slot = slots_row[...]
    holder = ((expert & (experts // 2 - 1)) << 1) | (expert >> half_bits)
    apart = group ^ holder
    index = (apart & 1) * (experts // 2) + (apart >> 1)
    place = jnp.where(slot >= 0, index * capacity + slot, -1).astype(F32)
    lines = jnp.concatenate(
        [place, expert.astype(F32), jnp.zeros((4, rows), F32)], axis=0
    )
    place_row[...] = lines
    routes[...] = jnp.concatenate([lines] * (LANES // 8), axis=0).T


def stacked(values, half):
    zero = jnp.zeros_like(values)
    return jnp.concatenate(
        [jnp.where(half, values, zero), jnp.where(half, zero, values)], axis=0
    )


def forward_body(
    width,
    experts,
    capacity,
    xhat,
    idcol,
    idrow,
    select,
    own,
    cotangent,
    routes,
    place_row,
    near_one,
    near_two,
    far_one,
    far_two,
    *outs,
):
    same_core, other_core, outs = outs[0], outs[1 : 1 + experts // 2], outs[1 + experts // 2 :]
    qkv, attended, lse, middle, normed_two, probs, normed, weights, weights_tail, gain = outs
    rows = own.shape[0]
    span = xhat.shape[0]
    cols = 3 * width
    parts = (near_one, near_two, far_one, far_two)
    size = width // 4
    for index, part in enumerate(parts):
        weights[index * size : (index + 1) * size, :] = part[:, :cols]
    sel = select[...]
    tail = jnp.concatenate([part[:, cols:] for part in parts], axis=0)
    gain_row = tail[:, width:].astype(F32).T[experts : experts + 1, :]
    gain[...] = jnp.broadcast_to(gain_row, (8, width))
    natural = dot(sel, tail)
    weights_tail[...] = natural.astype(BF)
    gain_two = natural[:, width:].T[experts + 1 : experts + 2, :]
    normed[...] = (xhat[...] * gain_row).astype(BF)
    qkv[HALO : HALO + rows, :] = dot(normed[HALO : HALO + rows, :], weights[...]).astype(BF)
    for first in (0, HALO + rows):
        qkv[first : first + HALO, width:] = dot(
            normed[first : first + HALO, :], weights[:, width:]
        ).astype(BF)
    half = lane_iota(BLOCK) < HEAD_DIM

    def attend(block, carry):
        base = pl.multiple_of(block * BLOCK, BLOCK)
        window = pl.ds(base, WINDOW)
        here = pl.ds(base, BLOCK)
        marks = idrow[0:1, pl.ds(base + HALO, BLOCK)]
        same = idcol[window, 0:1] == jnp.concatenate([marks, marks], axis=1)
        for pair in range(width // LANES):
            start = pair * LANES
            queries = qkv[pl.ds(base + HALO, BLOCK), start : start + LANES]
            queries = stacked((queries.astype(F32) * SCALE).astype(BF), half)
            keys = qkv[window, width + start : width + start + LANES]
            values = qkv[window, 2 * width + start : 2 * width + start + LANES]
            scores = jnp.where(same, dot(keys, queries, 1, 1), MASKED)
            peak = jnp.max(scores, axis=0, keepdims=True)
            raised = jnp.exp(scores - peak)
            total = jnp.sum(raised, axis=0, keepdims=True)
            result = dot(raised.astype(BF), values, 0, 0)
            column = jnp.broadcast_to(1.0 / total, (8, 2 * BLOCK)).T[:, 0:1]
            result = result * column
            attended[here, start : start + LANES] = jnp.where(
                half, result[:BLOCK], result[BLOCK:]
            ).astype(BF)
            logs = peak + jnp.log(total)
            lse[2 * pair : 2 * pair + 1, here] = logs[:, :BLOCK]
            lse[2 * pair + 1 : 2 * pair + 2, here] = logs[:, BLOCK:]
        return carry

    lax.fori_loop(0, rows // BLOCK, attend, 0, unroll=4)
    mid = own[:, :width].astype(F32) + dot(attended[...], weights_tail[:, :width])
    middle[...] = mid
    centered = mid - jnp.mean(mid, axis=1, keepdims=True)
    variance = jnp.mean(centered * centered, axis=1, keepdims=True)
    low_two = (centered * lax.rsqrt(variance + EPSILON) * gain_two).astype(BF)
    normed_two[...] = low_two
    lanes = lane_iota(rows)
    logits = jnp.where(lanes < experts, dot(low_two, weights_tail[:, width:]), MASKED)
    raised = jnp.exp(logits - jnp.max(logits, axis=1, keepdims=True))
    share = raised / jnp.sum(raised, axis=1, keepdims=True)
    probs[...] = share
    upstream = cotangent[...].astype(F32)
    wide_lanes = lanes.astype(F32)
    gates = []
    for choice in range(2):
        gate = jnp.sum(
            jnp.where(wide_lanes == routes[:, 2 + choice : 3 + choice], share, 0.0),
            axis=1,
            keepdims=True,
        )
        gates.append(jnp.broadcast_to(gate, (rows, 8)))
    gates = jnp.concatenate(gates + [jnp.zeros((rows, LANES - 16), F32)], axis=1).T
    source = jnp.concatenate([low_two, cotangent[...]], axis=1)
    for index in range(experts):
        if index < experts // 2:
            chunk = same_core.at[index * capacity : (index + 1) * capacity, :]
        else:
            chunk = other_core[index - experts // 2]
        slot = (
            lax.broadcasted_iota(jnp.int32, (capacity, rows), 0) + index * capacity
        ).astype(F32)
        first = slot == place_row[0:1, :]
        second = slot == place_row[1:2, :]
        weight = jnp.where(first, gates[0:1, :], jnp.where(second, gates[8:9, :], 0.0))
        taken = jnp.where(first | second, 1.0, 0.0)
        moved = dot(taken.astype(BF), source)
        chunk[:, :width] = moved[:, :width].astype(BF)
        chunk[:, width:] = (
            moved[:, width:] * jnp.sum(weight, axis=1, keepdims=True)
        ).astype(BF)


def joined(pieces, held):
    capacity = pieces[0].shape[0]
    for index, piece in enumerate(pieces):
        held[index * capacity : (index + 1) * capacity, :] = piece[...]


def expert_body(width, tile, count, *refs):
    pieces, kept, sent, rest = (
        refs[:count],
        refs[count],
        refs[count + 1 : count + 5],
        refs[count + 5 :],
    )
    returns, (hidden_out, grad_out, arrived, back, w_in, w_out) = rest[:count], rest[count:]
    joined(pieces, arrived)
    w_ins = [kept.at[:width, :], kept.at[2 * width : 3 * width, :], sent[0], sent[2]]
    w_outs = [kept.at[width : 2 * width, :], kept.at[3 * width :, :], sent[1], sent[3]]
    for quarter, (first, second) in enumerate(zip(w_ins, w_outs)):
        at = slice(quarter * width, (quarter + 1) * width)
        w_in[:, at] = first[...]
        w_out[at, :] = second[...]
    step_width = 2 * width // 3

    def step(index, carry):
        at = pl.ds(pl.multiple_of(index * tile, tile), tile)
        for start in range(0, 4 * width, step_width):
            columns = slice(start, start + step_width)
            pre = dot(arrived[at, :width], w_in[:, columns])
            hidden_grad = dot(arrived[at, width:], w_out[columns, :], 1, 1)
            square = pre * pre
            bend = jnp.tanh(pre * (GELU_C + (GELU_C * GELU_A) * square))
            scaled = 0.5 * pre
            hidden_out[at, columns] = (scaled + scaled * bend).astype(BF)
            slope = (0.5 + 0.5 * bend) + (
                scaled * (GELU_C + (3.0 * GELU_C * GELU_A) * square)
            ) * (1.0 - bend * bend)
            grad_out[at, columns] = (hidden_grad * slope).astype(BF)
        back[at, :width] = dot(hidden_out[at, :], w_out[...]).astype(BF)
        back[at, width:] = dot(grad_out[at, :], w_in[...], 1, 1).astype(BF)
        return carry

    lax.fori_loop(0, arrived.shape[0] // tile, step, 0)
    capacity = pieces[0].shape[0]
    for index, out in enumerate(returns):
        out[...] = back[index * capacity : (index + 1) * capacity, :]


def expert_grad_body(width, count, *refs):
    pieces, (hidden_one, hidden_two, pre_one, pre_two, kept, sent) = refs[:count], refs[count:]
    size = 2 * width
    outs = (kept.at[:size, :], kept.at[size:, :], sent.at[:size, :], sent.at[size:, :])
    grad_in = grad_out = 0.0
    for part, hidden, pre_grad in (
        (pieces[: count // 2], hidden_one, pre_one),
        (pieces[count // 2 :], hidden_two, pre_two),
    ):
        rows = jnp.concatenate([piece[:, :width] for piece in part], axis=0)
        grads = jnp.concatenate([piece[:, width:] for piece in part], axis=0)
        grad_in = grad_in + dot(rows, pre_grad[...], 0, 0)
        grad_out = grad_out + dot(grads, hidden[...], 0, 0)
    for quarter, out in enumerate(outs):
        columns = slice(quarter * width, (quarter + 1) * width)
        out[:width, :] = grad_in[:, columns].astype(BF)
        out[width:, :] = grad_out[:, columns].T.astype(BF)


def at_home(half):
    me = lax.axis_index("dp")
    return (me >= half) == ((me & 1) == 1)


def halve_body(whole, upper, lower):
    size = upper.shape[0]
    upper[...] = whole[:size, :]
    lower[...] = whole[size:, :]


def choose_body(half, size, near_one, near_in, near_out, *refs):
    far, kept, sent = refs[:4], refs[4], refs[5:]
    near = (near_one.at[:size, :], near_one.at[size:, :], near_in, near_out)

    def place(mine, theirs):
        for index, (one, two) in enumerate(zip(mine, theirs)):
            kept[index * size : (index + 1) * size, :] = one[...]
            sent[index][...] = two[...]

    @pl.when(at_home(half))
    def _():
        place(near, far)

    @pl.when(jnp.logical_not(at_home(half)))
    def _():
        place(far, near)


def mix_body(capacity, mine, *refs):
    theirs, outs = refs[: len(refs) // 2], refs[len(refs) // 2 :]
    for index, (part, out) in enumerate(zip(theirs, outs)):
        out[:capacity, :] = mine[index * capacity : (index + 1) * capacity, :]
        out[capacity:, :] = part[...]


def unmix_body(capacity, *refs):
    count = len(refs) // 2
    pieces, mine, theirs = refs[:count], refs[count], refs[count + 1 :]
    for index, (piece, out) in enumerate(zip(pieces, theirs)):
        mine[index * capacity : (index + 1) * capacity, :] = piece[:capacity, :]
        out[...] = piece[capacity:, :]


def split_body(half, size, mine, theirs, weights, normed, *outs):
    home_one, home_two, home_three, *away, keys_turned = outs
    width = size // 2
    keys_turned[...] = dot(weights[:, width : 2 * width], normed[...], 0, 1).astype(BF)

    def place(home, other):
        home_one[...] = home[:size, :]
        home_two[...], home_three[...] = home[size : 3 * size // 2, :], home[3 * size // 2 :, :]
        away[0][...] = other[:size, :]
        away[1][...], away[2][...] = other[size : 3 * size // 2, :], other[3 * size // 2 :, :]

    @pl.when(at_home(half))
    def _():
        place(mine, theirs)

    @pl.when(jnp.logical_not(at_home(half)))
    def _():
        place(theirs, mine)


def combine_body(
    width,
    experts,
    capacity,
    middle,
    normed_two,
    probs,
    cotangent,
    routes,
    attended,
    weights_tail,
    select,
    *refs,
):
    mixed, middle_grad, attended_grad, tail_grad, held = refs[-5:]
    start = 0
    for ref in refs[:-5]:
        held[start : start + ref.shape[0], :] = ref[...]
        start += ref.shape[0]
    rows = middle.shape[0]
    slots = experts * capacity
    gain_two = weights_tail[:, width:].astype(F32).T[experts + 1 : experts + 2, :]
    gain_grad = jnp.zeros((1, width), F32)
    router_rows = []
    branch_rows = []
    tile = rows
    for start in range(0, rows, tile):
        at = slice(start, start + tile)
        lanes = lane_iota(tile).astype(F32)
        wide = lax.broadcasted_iota(jnp.int32, (tile, slots), 1).astype(F32)
        first = (wide == routes[at, 0:1]).astype(F32)
        second = (wide == routes[at, 1:2]).astype(F32)
        picked = dot(
            jnp.concatenate([first, second], axis=0).astype(BF), held[:, :width]
        )
        grad_two = dot((first + second).astype(BF), held[:, width:])
        upstream = cotangent[at, :].astype(F32)
        share = probs[at, :]
        mid = middle[at, :]
        total = mid
        probs_grad = jnp.zeros((tile, LANES), F32)
        for choice in range(2):
            chosen = lanes == routes[at, 2 + choice : 3 + choice]
            gate = jnp.sum(jnp.where(chosen, share, 0.0), axis=1, keepdims=True)
            one = picked[choice * tile : (choice + 1) * tile, :]
            total = total + gate * one
            gate_grad = jnp.sum(one * upstream, axis=1, keepdims=True)
            probs_grad = probs_grad + jnp.where(chosen, gate_grad, 0.0)
        mixed[at, :] = total.astype(BF)
        logits_grad = (
            share * (probs_grad - jnp.sum(share * probs_grad, axis=1, keepdims=True))
        ).astype(BF)
        router_rows.append(logits_grad)
        grad_two = grad_two + dot(logits_grad, weights_tail[:, width:], 1, 1)
        centered = mid - jnp.mean(mid, axis=1, keepdims=True)
        variance = jnp.mean(centered * centered, axis=1, keepdims=True)
        rstd = lax.rsqrt(variance + EPSILON)
        xhat = centered * rstd
        gain_grad = gain_grad + jnp.sum(grad_two * xhat, axis=0, keepdims=True)
        inner = grad_two * gain_two
        inner_grad = rstd * (
            inner
            - jnp.mean(inner, axis=1, keepdims=True)
            - xhat * jnp.mean(inner * xhat, axis=1, keepdims=True)
        )
        through = upstream + inner_grad
        middle_grad[at, :] = through
        branch = through.astype(BF)
        branch_rows.append(branch)
        attended_grad[at, :] = dot(branch, weights_tail[:, :width], 1, 1).astype(BF)
    sel = select[...]
    logits_grad = jnp.concatenate(router_rows, axis=0)
    branch = jnp.concatenate(branch_rows, axis=0)
    attended_turned = dot(attended[...], sel).astype(BF)
    normed_turned = dot(normed_two[...], sel).astype(BF)
    tail_grad[:, :width] = dot(attended_turned, branch, 0, 0).astype(BF)
    gain_line = jnp.broadcast_to(gain_grad, (8, width))
    upper = gain_line.astype(BF)
    lower = (gain_line - upper.astype(F32)).astype(BF)
    gain_turned = dot(upper, sel) + dot(lower, sel)
    gain_column = jnp.broadcast_to(gain_turned[0:1, :], (LANES, width)).T
    router_grad = dot(normed_turned, logits_grad, 0, 0)
    tail_grad[:, width:] = jnp.where(
        lane_iota(width) == experts + 1, gain_column, router_grad
    ).astype(BF)


def backward_body(
    width,
    qkv,
    keys_turned,
    lse,
    attended_grad,
    idcol,
    idrow,
    normed,
    tail_grad,
    dq,
    rims_low,
    rims_high,
    inner,
    kept,
    *sents,
):
    rows = attended_grad.shape[0]
    half_rows = width // 2
    *sents, acc = sents
    half = lane_iota(BLOCK) < HEAD_DIM
    upper = lax.broadcasted_iota(jnp.int32, (LANES, BLOCK), 0) < HEAD_DIM
    acc[...] = jnp.zeros_like(acc)

    def attend(block, carry):
        base = pl.multiple_of(block * BLOCK, BLOCK)
        window = pl.ds(base, WINDOW)
        here = pl.ds(base, BLOCK)
        marks = idrow[0:1, pl.ds(base + HALO, BLOCK)]
        same = idcol[window, 0:1] == jnp.concatenate([marks, marks], axis=1)
        for pair in range(width // LANES):
            start = pair * LANES
            queries = qkv[pl.ds(base + HALO, BLOCK), start : start + LANES]
            queries = stacked((queries.astype(F32) * SCALE).astype(BF), half)
            grads = stacked(attended_grad[here, start : start + LANES], half)
            keys = qkv[window, width + start : width + start + LANES]
            values = qkv[window, 2 * width + start : 2 * width + start + LANES]
            logs = jnp.concatenate(
                [lse[2 * pair : 2 * pair + 1, here], lse[2 * pair + 1 : 2 * pair + 2, here]], axis=1
            )
            scores = jnp.where(same, dot(keys, queries, 1, 1), MASKED)
            weights = jnp.exp(scores - logs)
            weights_grad = dot(values, grads, 1, 1)
            delta = jnp.sum(weights * weights_grad, axis=0, keepdims=True)
            scores_grad = (weights * (weights_grad - delta)).astype(BF)
            acc[window, start : start + LANES] += dot(scores_grad, queries)
            acc[window, width + start : width + start + LANES] += dot(weights.astype(BF), grads)
            result = dot(keys_turned[start : start + LANES, window], scores_grad) * SCALE
            dq[here, start : start + LANES] = (
                jnp.where(upper, result[:, :BLOCK], result[:, BLOCK:]).T.astype(BF)
            )
        return carry

    lax.fori_loop(0, rows // BLOCK, attend, 0, unroll=4)
    rims_low[...] = acc[:HALO, :].astype(BF)
    rims_high[...] = acc[HALO + rows :, :].astype(BF)
    inner[...] = acc[HALO : HALO + rows, :]
    own = normed[HALO : HALO + rows, :]
    query_part = dot(own, dq[...], 0, 0)
    kept[:, :width] = query_part[:half_rows]
    other_part = dot(normed[...], acc[...].astype(BF), 0, 0)
    kept[:, width : 3 * width] = other_part[:half_rows]
    kept[:, 3 * width :] = tail_grad[:half_rows, :].astype(F32)
    size = half_rows // len(sents)
    for index, sent in enumerate(sents):
        at = slice(half_rows + index * size, half_rows + (index + 1) * size)
        sent[:, :width] = query_part[at].astype(BF)
        sent[:, width : 3 * width] = other_part[at].astype(BF)
        sent[:, 3 * width :] = tail_grad[at, :]


def finish_body(
    width, dq, inner, from_low, from_high, weights, normed_gain, xhat, rstd, select, middle_grad, out, grad
):
    rows = dq.shape[0]
    experts_lane = 0
    grad[...] = inner[...]
    grad[:HALO, :] += from_low[...].astype(F32)
    grad[rows - HALO :, :] += from_high[...].astype(F32)
    values = dot(dq[...], weights[:, :width], 1, 1) + dot(
        grad[...].astype(BF), weights[:, width:], 1, 1
    )
    hat = xhat[HALO : HALO + rows, :]
    values = values * normed_gain[0:1, :]
    part = rstd[HALO : HALO + rows, 0:1] * (
        values
        - jnp.mean(values, axis=1, keepdims=True)
        - hat * jnp.mean(values * hat, axis=1, keepdims=True)
    )
    upper = part.astype(BF)
    lower = (part - upper.astype(F32)).astype(BF)
    sel = select[...]
    out[...] = (middle_grad[...] + dot(upper, sel, 1, 1) + dot(lower, sel, 1, 1)).astype(BF)


def sum_body(parts, own, *refs):
    arrived, outs = refs[: len(refs) - parts], refs[len(refs) - parts :]
    total = own[...].astype(F32)
    if arrived[0].shape[0] < total.shape[0]:
        total = total + jnp.concatenate([ref[...].astype(F32) for ref in arrived], axis=0)
    else:
        for ref in arrived:
            total = total + ref[...].astype(F32)
    size = total.shape[0] // parts
    for index, out in enumerate(outs):
        out[...] = total[index * size : (index + 1) * size, :].astype(out.dtype)


def final_body(width, experts, own, *refs):
    arrived, rest = refs[:-13], refs[-13:]
    w_qkv, gain, *parts, qkv_grad, proj_grad, router_grad, one, two, in_grad, out_grad = rest
    total = own[...]
    for ref in arrived:
        total = total + ref[...].astype(F32)
    qkv = total[:, : 3 * width]
    qkv_grad[...] = qkv
    proj_grad[...] = total[:, 3 * width : 4 * width]
    gain_grad = jnp.sum(qkv * w_qkv[...].astype(F32), axis=1, keepdims=True)
    tail = total[:, 4 * width :]
    share = own.shape[0]
    diagonal = lax.broadcasted_iota(jnp.int32, (share, share), 0) == lane_iota(share, share)

    def turned(column):
        return jnp.sum(jnp.where(diagonal, column, 0.0), axis=0, keepdims=True)

    one[...] = turned(gain_grad) / gain[...].astype(F32)
    two[...] = turned(tail[:, experts + 1 : experts + 2])
    for index in range(experts):
        router_grad[index : index + 1, :] = turned(tail[:, index : index + 1])
    mine, upper, lower, other = parts
    for out, at, beside in (
        (in_grad, slice(0, width), upper),
        (out_grad, slice(width, 2 * width), lower),
    ):
        out[0] = mine[at, :].astype(F32) + beside[...].astype(F32) + other[at, :].astype(F32)


def gather_stages(devices):
    bits = devices.bit_length() - 1
    stages = []
    top = bits - 1
    while top >= 1:
        if top >= 2:
            low, high = 1 << (top - 1), 1 << top
            stages.append([low, high, low | high])
            top -= 2
        else:
            stages.append([1 << top])
            top -= 1
    stages.append([1])
    return stages


def swap(value, devices, mask):
    return lax.ppermute(value, "dp", [(i, i ^ mask) for i in range(devices)])


def reduce_scattered(kept, sent, devices, stages, before, after):
    total = kept
    arrived = [swap(part, devices, stages[-1][0]) for part in sent]
    for level in range(len(stages) - 1, 0, -1):
        masks = stages[level - 1]
        parts = 1 + len(masks)
        dims = (total.shape[0] // parts, total.shape[1])
        outs = [shape(dims, F32)] + [shape(dims, BF)] * (parts - 1)
        if level == 1:
            arrived, before[-1], after = lax.optimization_barrier((arrived, before[-1], after))
        if level == 2:
            arrived, before[:-1] = lax.optimization_barrier((arrived, before[:-1]))
        pieces = call(
            functools.partial(sum_body, parts), outs, [total] + arrived, name=f"sum{level}"
        )
        total = pieces[0]
        arrived = [swap(piece, devices, mask) for piece, mask in zip(pieces[1:], masks)]
    return total, arrived, before, after


def per_device(
    tokens,
    gain_attn,
    w_qkv,
    w_proj,
    gain_moe,
    w_router,
    w_in,
    w_out,
    cotangent,
    image_ids,
    expert_ids,
    slots,
):
    devices = lax.axis_size("dp")
    experts = devices // 4
    rows, width = tokens.shape
    capacity = max(2, 5 * rows // (2 * experts))
    share = width // devices
    span = rows + 2 * HALO
    stages = gather_stages(devices)
    everyone = range(devices)
    half = devices // 2

    ins = [
        w_qkv,
        w_proj,
        w_router.T,
        gain_attn[None, :],
        gain_moe[None, :],
        tokens,
        image_ids.reshape(rows // BLOCK, BLOCK),
    ]
    packed, own, low, high = call(
        functools.partial(pack_body, experts),
        [
            shape((share, 4 * width + LANES), BF),
            shape((rows, width + LANES), BF),
            shape((HALO, width + LANES), BF),
            shape((HALO, width + LANES), BF),
        ],
        ins,
        scratch=[pltpu.VMEM(x.shape, x.dtype) for x in ins]
        + [pltpu.SemaphoreType.DMA((len(ins),))],
        name="pack",
        fetch=True,
    )
    up = [(i, i + 1) for i in range(devices - 1)]
    down = [(i + 1, i) for i in range(devices - 1)]
    low = lax.ppermute(low, "dp", up)
    high = lax.ppermute(high, "dp", down)
    packed, w_in = lax.optimization_barrier((packed, w_in))
    quarter = call(
        functools.partial(quarter_body, width),
        [shape((2 * width, width), BF)],
        [w_in, w_out],
        scratch=[pltpu.SemaphoreType.DMA((2,))],
        name="quarter",
        fetch=True,
    )[0]
    order = [0]
    near = [packed]
    far = None
    for stage in stages:
        order = [a ^ mask for mask in [0] + stage for a in order]
        arrived = [swap(part, devices, mask) for mask in stage for part in near]
        if stage is stages[0]:
            arrived[0], low, high, quarter = lax.optimization_barrier(
                (arrived[0], low, high, quarter)
            )
            arrived[1], quarter_far = lax.optimization_barrier((arrived[1], quarter))
        if stage is stages[-2]:
            *arrived, late_in = lax.optimization_barrier((*arrived, w_in[0]))
        if stage is stages[-1]:
            far = arrived
        else:
            parts = 2 if stage is stages[-2] else 1
            size = near[0].shape[0] * (1 + len(stage)) // parts
            near = call(
                functools.partial(join_body, parts),
                [shape((size, near[0].shape[1]), BF)] * parts,
                [*near, *arrived],
                name="join",
            )
    order = np.stack(
        [
            np.repeat(np.array(order, np.int32), share),
            np.tile(np.arange(share, dtype=np.int32), devices),
        ]
    )

    far_quarter = swap(quarter_far, devices, half)
    near_in = swap(late_in, devices, 2)

    def exchange(parts):
        return [parts[0]] + [
            swap(part, devices, 4 * index) for index, part in enumerate(parts) if index
        ]

    xhat, rstd, select, idcol, idrow, routes, place_row = call(
        functools.partial(prepare_body, width, experts, capacity),
        [
            shape((span, width), F32),
            shape((span, LANES), F32),
            shape((width, width), BF),
            shape((span, LANES), F32),
            shape((8, span), F32),
            shape((rows, LANES), F32),
            shape((8, rows), F32),
        ],
        [own, low, high, jnp.asarray(order), expert_ids.T, slots.T],
        flops=2 * span * width * width,
        name="prepare",
    )
    chips = experts // 2
    half_slots = chips * capacity
    outs = call(
        functools.partial(forward_body, width, experts, capacity),
        [shape((half_slots, 2 * width), BF)]
        + [shape((capacity, 2 * width), BF)] * chips
        + [
            shape((span, 3 * width), BF),
            shape((rows, width), BF),
            shape((8, rows), F32),
            shape((rows, width), F32),
            shape((rows, width), BF),
            shape((rows, LANES), F32),
            shape((span, width), BF),
            shape((width, 3 * width), BF),
            shape((width, width + LANES), BF),
            shape((8, width), F32),
        ],
        [xhat, idcol, idrow, select, own, cotangent, routes, place_row, *near, *far],
        name="forward",
    )
    same_core, other_core, outs = outs[0], outs[1 : 1 + chips], outs[1 + chips :]
    qkv, attended, lse, middle, normed_two, probs, normed, weights, weights_tail, gain = outs

    both = shape((2 * capacity, 2 * width), BF)
    *other_core, near_in = lax.optimization_barrier((*other_core, near_in))
    pieces = call(
        functools.partial(mix_body, capacity),
        [both] * chips,
        [same_core, *[swap(part, devices, 1) for part in other_core]],
        name="mix",
    )
    far_quarter, late_out, piece = lax.optimization_barrier((far_quarter, w_out[0], pieces[0]))
    near_out = swap(late_out, devices, 2)
    arrived = exchange([piece, *pieces[1:]])
    far_half = call(
        halve_body, [shape((width, width), BF)] * 2, [far_quarter], name="halve"
    )
    far_half = [*far_half] + [swap(part, devices, 2) for part in far_half]
    slot_count = experts * capacity
    pair = shape((4 * width, width), BF)
    far_half[-1], *arrived[1:-1] = lax.optimization_barrier((far_half[-1], *arrived[1:-1]))
    kept_pair, *sent_parts = call(
        functools.partial(choose_body, half, width),
        [pair] + [shape((width, width), BF)] * 4,
        [quarter, near_in, near_out, *far_half],
        name="choose",
    )
    expert_weights = [kept_pair] + [swap(part, devices, 1) for part in sent_parts]
    tile = slot_count // 4
    held = pltpu.VMEM((slot_count, 2 * width), BF)
    back, hidden, pre_grad = [], [], []
    for part in (arrived[: chips // 2], arrived[chips // 2 :]):
        half_held = pltpu.VMEM((half_slots, 2 * width), BF)
        outs = call(
            functools.partial(expert_body, width, tile, len(part)),
            [both] * len(part) + [shape((half_slots, 4 * width), BF)] * 2,
            [*part, *expert_weights],
            scratch=[
                half_held,
                half_held,
                pltpu.VMEM((width, 4 * width), BF),
                pltpu.VMEM((4 * width, width), BF),
            ],
            flops=4 * slot_count * width * 4 * width,
            name="expert",
            vmem_mib=16,
        )
        back += outs[: len(part)]
        hidden.append(outs[-2])
        pre_grad.append(outs[-1])
    returned = exchange(back)
    kept_pair, sent_pair = call(
        functools.partial(expert_grad_body, width, chips),
        [pair, pair],
        [*arrived, *hidden, *pre_grad],
        vmem_mib=16,
        flops=4 * slot_count * width * 4 * width,
        name="expert_grad",
    )
    other_pair = swap(sent_pair, devices, 1)
    single = shape((2 * width, width), BF)
    square = shape((width, width), BF)
    home_kept, *home_sent = call(
        functools.partial(split_body, half, 2 * width),
        [single, square, square] * 2 + [shape((width, span), BF)],
        [kept_pair, other_pair, weights, normed],
        name="split",
    )
    home_sent, (away_kept, *away_sent, keys_turned) = home_sent[:2], home_sent[2:]
    away_came = [swap(part, devices, 2) for part in away_sent]
    *home_sent, returned[1] = lax.optimization_barrier((*home_sent, returned[1]))
    home_came = [swap(part, devices, 2) for part in home_sent]
    away = call(
        functools.partial(sum_body, 1), [single], [away_kept, *away_came], name="away"
    )[0]

    returned[-1], away = lax.optimization_barrier((returned[-1], away))
    mine, *theirs = call(
        functools.partial(unmix_body, capacity),
        [shape((half_slots, 2 * width), BF)] + [shape((capacity, 2 * width), BF)] * chips,
        returned,
        name="unmix",
    )
    theirs = [swap(part, devices, 1) for part in theirs]
    mixed, middle_grad, attended_grad, tail_grad = call(
        functools.partial(combine_body, width, experts, capacity),
        [
            shape((rows, width), BF),
            shape((rows, width), F32),
            shape((rows, width), BF),
            shape((width, width + LANES), BF),
        ],
        [
            middle,
            normed_two,
            probs,
            cotangent,
            routes,
            attended,
            weights_tail,
            select,
            mine,
            *theirs,
        ],
        scratch=[pltpu.VMEM((slot_count, 2 * width), BF)],
        flops=6 * rows * slot_count * width,
        name="combine",
    )
    expert_parts = [home_kept, *home_came, swap(away, devices, half)]
    half_rows = width // 2

    dq, rims_low, rims_high, inner, kept, *sent = call(
        functools.partial(backward_body, width),
        [
            shape((rows, width), BF),
            shape((HALO, 2 * width), BF),
            shape((HALO, 2 * width), BF),
            shape((rows, 2 * width), F32),
            shape((half_rows, 4 * width + LANES), F32),
        ]
        + [shape((half_rows // 4, 4 * width + LANES), BF)] * 4,
        [qkv, keys_turned, lse, attended_grad, idcol, idrow, normed, tail_grad],
        scratch=[pltpu.VMEM((span, 2 * width), F32)],
        name="backward",
    )
    total, last, expert_parts, (rims_low, rims_high) = reduce_scattered(
        kept, sent, devices, stages, expert_parts, [rims_low, rims_high]
    )
    from_high = lax.ppermute(rims_low, "dp", down)
    from_low = lax.ppermute(rims_high, "dp", up)
    grad_tokens = call(
        functools.partial(finish_body, width),
        [shape((rows, width), BF)],
        [dq, inner, from_low, from_high, weights, gain, xhat, rstd, select, middle_grad],
        scratch=[pltpu.VMEM((rows, 2 * width), F32)],
        flops=2 * rows * width * 5 * width,
        name="finish",
    )[0]

    last[0], grad_tokens = lax.optimization_barrier((last[0], grad_tokens))
    qkv_grad, proj_grad, router_grad, gain_one_grad, gain_two_grad, in_grad, out_grad = call(
        functools.partial(final_body, width, experts),
        [
            shape((share, 3 * width), F32),
            shape((share, width), F32),
            shape((experts, share), F32),
            shape((1, share), F32),
            shape((1, share), F32),
            shape((1, width, width), F32),
            shape((1, width, width), F32),
        ],
        [total, *last, w_qkv, gain_attn[None, :], *expert_parts],
        name="final",
    )
    return (
        mixed,
        grad_tokens,
        gain_one_grad.reshape(share),
        qkv_grad,
        proj_grad,
        gain_two_grad.reshape(share),
        router_grad.T,
        in_grad,
        out_grad,
    )


def solution(mesh):
    row, line, cube = P("dp", None), P("dp"), P("dp", None, None)
    return jax.shard_map(
        per_device,
        mesh=mesh,
        in_specs=(row, line, row, row, line, row, cube, cube, row, line, row, row),
        out_specs=(row, row, line, row, row, line, row, cube, cube),
        check_vma=False,
    )
```

```python
import functools

import jax
import jax.numpy as jnp
import numpy as np
from jax import lax
from jax.experimental import pallas as pl
from jax.experimental.pallas import tpu as pltpu
from jax.sharding import PartitionSpec as P

HEAD_DIM = 64
LEN = 197
EPSILON = 1e-06
MASKED = -1e30
HALO = 256
BLOCK = 128
WINDOW = BLOCK + 2 * HALO
LANES = 128
SCALE = HEAD_DIM ** (-0.5)
BF = jnp.bfloat16
F32 = jnp.float32
GELU_C = (2.0 / np.pi) ** 0.5
GELU_A = 0.044715


def dot(left, right, left_dim=1, right_dim=0):
    return lax.dot_general(
        left,
        right,
        (((left_dim,), (right_dim,)), ((), ())),
        preferred_element_type=F32,
    )


def call(body, outs, ins, scratch=(), flops=0, name=None, vmem_mib=12, fetch=False):
    vmem = pl.BlockSpec(memory_space=pltpu.VMEM)
    spec = pl.BlockSpec(memory_space=pltpu.HBM) if fetch else vmem
    if fetch:
        ins = [pltpu.with_memory_space_constraint(x, pltpu.HBM) for x in ins]
    return pl.pallas_call(
        body,
        out_shape=tuple(outs),
        in_specs=[spec] * len(ins),
        out_specs=tuple([vmem] * len(outs)),
        scratch_shapes=list(scratch),
        compiler_params=pltpu.CompilerParams(vmem_limit_bytes=vmem_mib * 1024 * 1024),
        cost_estimate=pl.CostEstimate(flops=int(flops), bytes_accessed=1024, transcendentals=0),
        name=name,
    )(*ins)


def shape(dims, dtype):
    return jax.ShapeDtypeStruct(dims, dtype)


def lane_iota(rows, lanes=LANES):
    return lax.broadcasted_iota(jnp.int32, (rows, lanes), 1)


def fetched(refs, held, sems):
    copies = [
        pltpu.make_async_copy(ref, into, sems.at[index])
        for index, (ref, into) in enumerate(zip(refs, held))
    ]
    for copy in copies:
        copy.start()
    for copy in copies:
        copy.wait()


def pack_body(experts, *refs):
    count = 7
    (out, own, low, high), held, sems = refs[count : count + 4], refs[count + 4 : -1], refs[-1]
    fetched(refs[:count], held, sems)
    w_qkv, w_proj, router_turned, gain_attn, gain_moe, tokens, ids = held
    share, cols = w_qkv.shape
    width = cols // 3
    out[:, :cols] = w_qkv[...]
    out[:, cols : 4 * width] = w_proj[...]
    lanes = lane_iota(share)
    diagonal = lax.broadcasted_iota(jnp.int32, (share, share), 0) == lane_iota(share, share)
    pick = lax.broadcasted_iota(jnp.int32, (experts, LANES), 0) == lane_iota(experts)
    tail = dot(router_turned[...], pick.astype(F32).astype(BF), 0, 0)
    for index, gain in enumerate((gain_attn, gain_moe)):
        column = jnp.sum(
            jnp.where(diagonal, gain[...].astype(F32), 0.0), axis=1, keepdims=True
        )
        tail = jnp.where(lanes == experts + index, column, tail)
    out[:, 4 * width :] = tail.astype(BF)
    rows = tokens.shape[0]
    own[:, :width] = tokens[...]
    for index in range(rows // BLOCK):
        line = (ids[index : index + 1, :] + 1).astype(F32)
        column = jnp.broadcast_to(line, (BLOCK, BLOCK)).T
        upper = jnp.floor(column * (1.0 / 256.0))
        lower = column - 256.0 * upper
        own[index * BLOCK : (index + 1) * BLOCK, width:] = jnp.where(
            lane_iota(BLOCK) == 0, upper, lower
        ).astype(BF)
    low[...] = own[rows - HALO :, :]
    high[...] = own[:HALO, :]


def quarter_body(width, w_in, w_out, quarter, sems):
    fetched(
        (w_in.at[0], w_out.at[0]), (quarter.at[:width, :], quarter.at[width:, :]), sems
    )


def join_body(parts, *refs):
    pieces, outs = refs[:-parts], refs[-parts:]
    whole = jnp.concatenate([piece[...].astype(F32) for piece in pieces], axis=0).astype(BF)
    size = whole.shape[0] // parts
    for index, out in enumerate(outs):
        out[...] = whole[index * size : (index + 1) * size, :]


def prepare_body(
    width,
    experts,
    capacity,
    own,
    low,
    high,
    order,
    experts_row,
    slots_row,
    xhat,
    rstd_out,
    select,
    idcol,
    idrow,
    routes,
    place_row,
):
    me = lax.axis_index("dp")
    devices = 4 * experts
    share = width // devices
    target = (me ^ order[0:1, :]) * share + order[1:2, :]
    sel = (lax.broadcasted_iota(jnp.int32, (width, width), 0) == target).astype(F32).astype(BF)
    select[...] = sel
    start = 0
    for ref in (low, own, high):
        rows = ref.shape[0]
        values = dot(ref[:, :width], sel)
        mean = jnp.mean(values, axis=1, keepdims=True)
        centered = values - mean
        rstd = lax.rsqrt(jnp.mean(centered * centered, axis=1, keepdims=True) + EPSILON)
        xhat[start : start + rows, :] = centered * rstd
        rstd_out[start : start + rows, :] = jnp.broadcast_to(rstd, (rows, LANES))
        marks = ref[:, width : width + LANES].astype(F32)
        column = marks[:, 0:1] * 256.0 + marks[:, 1:2]
        idcol[start : start + rows, :] = jnp.broadcast_to(column, (rows, LANES))
        turned = marks.T
        line = turned[0:1, :] * 256.0 + turned[1:2, :]
        idrow[:, start : start + rows] = jnp.broadcast_to(line, (8, rows))
        start += rows
    rows = own.shape[0]
    group = (((me >> 2) & (experts // 2 - 1)) << 1) | (me & 1)
    half_bits = (experts // 2).bit_length() - 1
    expert = experts_row[...]
    slot = slots_row[...]
    holder = ((expert & (experts // 2 - 1)) << 1) | (expert >> half_bits)
    apart = group ^ holder
    index = (apart & 1) * (experts // 2) + (apart >> 1)
    place = jnp.where(slot >= 0, index * capacity + slot, -1).astype(F32)
    lines = jnp.concatenate(
        [place, expert.astype(F32), jnp.zeros((4, rows), F32)], axis=0
    )
    place_row[...] = lines
    routes[...] = jnp.concatenate([lines] * (LANES // 8), axis=0).T


def stacked(values, half):
    zero = jnp.zeros_like(values)
    return jnp.concatenate(
        [jnp.where(half, values, zero), jnp.where(half, zero, values)], axis=0
    )


def forward_body(
    width,
    experts,
    capacity,
    xhat,
    idcol,
    idrow,
    select,
    own,
    cotangent,
    routes,
    place_row,
    near_one,
    near_two,
    far_one,
    far_two,
    *outs,
):
    same_core, other_core, outs = outs[0], outs[1 : 1 + experts // 2], outs[1 + experts // 2 :]
    qkv, attended, lse, middle, normed_two, probs, normed, weights, weights_tail, gain = outs
    rows = own.shape[0]
    span = xhat.shape[0]
    cols = 3 * width
    parts = (near_one, near_two, far_one, far_two)
    size = width // 4
    for index, part in enumerate(parts):
        weights[index * size : (index + 1) * size, :] = part[:, :cols]
    sel = select[...]
    tail = jnp.concatenate([part[:, cols:] for part in parts], axis=0)
    gain_row = tail[:, width:].astype(F32).T[experts : experts + 1, :]
    gain[...] = jnp.broadcast_to(gain_row, (8, width))
    natural = dot(sel, tail)
    weights_tail[...] = natural.astype(BF)
    gain_two = natural[:, width:].T[experts + 1 : experts + 2, :]
    normed[...] = (xhat[...] * gain_row).astype(BF)
    qkv[HALO : HALO + rows, :] = dot(normed[HALO : HALO + rows, :], weights[...]).astype(BF)
    for first in (0, HALO + rows):
        qkv[first : first + HALO, width:] = dot(
            normed[first : first + HALO, :], weights[:, width:]
        ).astype(BF)
    half = lane_iota(BLOCK) < HEAD_DIM

    def attend(block, carry):
        base = pl.multiple_of(block * BLOCK, BLOCK)
        window = pl.ds(base, WINDOW)
        here = pl.ds(base, BLOCK)
        marks = idrow[0:1, pl.ds(base + HALO, BLOCK)]
        same = idcol[window, 0:1] == jnp.concatenate([marks, marks], axis=1)
        for pair in range(width // LANES):
            start = pair * LANES
            queries = qkv[pl.ds(base + HALO, BLOCK), start : start + LANES]
            queries = stacked((queries.astype(F32) * SCALE).astype(BF), half)
            keys = qkv[window, width + start : width + start + LANES]
            values = qkv[window, 2 * width + start : 2 * width + start + LANES]
            scores = jnp.where(same, dot(keys, queries, 1, 1), MASKED)
            peak = jnp.max(scores, axis=0, keepdims=True)
            raised = jnp.exp(scores - peak)
            total = jnp.sum(raised, axis=0, keepdims=True)
            result = dot(raised.astype(BF), values, 0, 0)
            column = jnp.broadcast_to(1.0 / total, (8, 2 * BLOCK)).T[:, 0:1]
            result = result * column
            attended[here, start : start + LANES] = jnp.where(
                half, result[:BLOCK], result[BLOCK:]
            ).astype(BF)
            logs = peak + jnp.log(total)
            lse[2 * pair : 2 * pair + 1, here] = logs[:, :BLOCK]
            lse[2 * pair + 1 : 2 * pair + 2, here] = logs[:, BLOCK:]
        return carry

    lax.fori_loop(0, rows // BLOCK, attend, 0, unroll=4)
    mid = own[:, :width].astype(F32) + dot(attended[...], weights_tail[:, :width])
    middle[...] = mid
    centered = mid - jnp.mean(mid, axis=1, keepdims=True)
    variance = jnp.mean(centered * centered, axis=1, keepdims=True)
    low_two = (centered * lax.rsqrt(variance + EPSILON) * gain_two).astype(BF)
    normed_two[...] = low_two
    lanes = lane_iota(rows)
    logits = jnp.where(lanes < experts, dot(low_two, weights_tail[:, width:]), MASKED)
    raised = jnp.exp(logits - jnp.max(logits, axis=1, keepdims=True))
    share = raised / jnp.sum(raised, axis=1, keepdims=True)
    probs[...] = share
    upstream = cotangent[...].astype(F32)
    wide_lanes = lanes.astype(F32)
    gates = []
    for choice in range(2):
        gate = jnp.sum(
            jnp.where(wide_lanes == routes[:, 2 + choice : 3 + choice], share, 0.0),
            axis=1,
            keepdims=True,
        )
        gates.append(jnp.broadcast_to(gate, (rows, 8)))
    gates = jnp.concatenate(gates + [jnp.zeros((rows, LANES - 16), F32)], axis=1).T
    source = jnp.concatenate([low_two, cotangent[...]], axis=1)
    for index in range(experts):
        if index < experts // 2:
            chunk = same_core.at[index * capacity : (index + 1) * capacity, :]
        else:
            chunk = other_core[index - experts // 2]
        slot = (
            lax.broadcasted_iota(jnp.int32, (capacity, rows), 0) + index * capacity
        ).astype(F32)
        first = slot == place_row[0:1, :]
        second = slot == place_row[1:2, :]
        weight = jnp.where(first, gates[0:1, :], jnp.where(second, gates[8:9, :], 0.0))
        taken = jnp.where(first | second, 1.0, 0.0)
        moved = dot(taken.astype(BF), source)
        chunk[:, :width] = moved[:, :width].astype(BF)
        chunk[:, width:] = (
            moved[:, width:] * jnp.sum(weight, axis=1, keepdims=True)
        ).astype(BF)


def joined(pieces, held):
    capacity = pieces[0].shape[0]
    for index, piece in enumerate(pieces):
        held[index * capacity : (index + 1) * capacity, :] = piece[...]


def expert_body(width, tile, count, *refs):
    pieces, kept, sent, rest = (
        refs[:count],
        refs[count],
        refs[count + 1 : count + 5],
        refs[count + 5 :],
    )
    returns, (hidden_out, grad_out, arrived, back, w_in, w_out) = rest[:count], rest[count:]
    joined(pieces, arrived)
    w_ins = [kept.at[:width, :], kept.at[2 * width : 3 * width, :], sent[0], sent[2]]
    w_outs = [kept.at[width : 2 * width, :], kept.at[3 * width :, :], sent[1], sent[3]]
    for quarter, (first, second) in enumerate(zip(w_ins, w_outs)):
        at = slice(quarter * width, (quarter + 1) * width)
        w_in[:, at] = first[...]
        w_out[at, :] = second[...]
    step_width = 2 * width // 3

    def step(index, carry):
        at = pl.ds(pl.multiple_of(index * tile, tile), tile)
        for start in range(0, 4 * width, step_width):
            columns = slice(start, start + step_width)
            pre = dot(arrived[at, :width], w_in[:, columns])
            hidden_grad = dot(arrived[at, width:], w_out[columns, :], 1, 1)
            square = pre * pre
            bend = jnp.tanh(pre * (GELU_C + (GELU_C * GELU_A) * square))
            scaled = 0.5 * pre
            hidden_out[at, columns] = (scaled + scaled * bend).astype(BF)
            slope = (0.5 + 0.5 * bend) + (
                scaled * (GELU_C + (3.0 * GELU_C * GELU_A) * square)
            ) * (1.0 - bend * bend)
            grad_out[at, columns] = (hidden_grad * slope).astype(BF)
        back[at, :width] = dot(hidden_out[at, :], w_out[...]).astype(BF)
        back[at, width:] = dot(grad_out[at, :], w_in[...], 1, 1).astype(BF)
        return carry

    lax.fori_loop(0, arrived.shape[0] // tile, step, 0)
    capacity = pieces[0].shape[0]
    for index, out in enumerate(returns):
        out[...] = back[index * capacity : (index + 1) * capacity, :]


def expert_grad_body(width, count, *refs):
    pieces, (hidden_one, hidden_two, pre_one, pre_two, kept, sent) = refs[:count], refs[count:]
    size = 2 * width
    outs = (kept.at[:size, :], kept.at[size:, :], sent.at[:size, :], sent.at[size:, :])
    grad_in = grad_out = 0.0
    for part, hidden, pre_grad in (
        (pieces[: count // 2], hidden_one, pre_one),
        (pieces[count // 2 :], hidden_two, pre_two),
    ):
        rows = jnp.concatenate([piece[:, :width] for piece in part], axis=0)
        grads = jnp.concatenate([piece[:, width:] for piece in part], axis=0)
        grad_in = grad_in + dot(rows, pre_grad[...], 0, 0)
        grad_out = grad_out + dot(grads, hidden[...], 0, 0)
    for quarter, out in enumerate(outs):
        columns = slice(quarter * width, (quarter + 1) * width)
        out[:width, :] = grad_in[:, columns].astype(BF)
        out[width:, :] = grad_out[:, columns].T.astype(BF)


def at_home(half):
    me = lax.axis_index("dp")
    return (me >= half) == ((me & 1) == 1)


def halve_body(whole, upper, lower):
    size = upper.shape[0]
    upper[...] = whole[:size, :]
    lower[...] = whole[size:, :]


def choose_body(half, size, near_one, near_in, near_out, *refs):
    far, kept, sent = refs[:4], refs[4], refs[5:]
    near = (near_one.at[:size, :], near_one.at[size:, :], near_in, near_out)

    def place(mine, theirs):
        for index, (one, two) in enumerate(zip(mine, theirs)):
            kept[index * size : (index + 1) * size, :] = one[...]
            sent[index][...] = two[...]

    @pl.when(at_home(half))
    def _():
        place(near, far)

    @pl.when(jnp.logical_not(at_home(half)))
    def _():
        place(far, near)


def mix_body(capacity, mine, *refs):
    theirs, outs = refs[: len(refs) // 2], refs[len(refs) // 2 :]
    for index, (part, out) in enumerate(zip(theirs, outs)):
        out[:capacity, :] = mine[index * capacity : (index + 1) * capacity, :]
        out[capacity:, :] = part[...]


def unmix_body(capacity, *refs):
    count = len(refs) // 2
    pieces, mine, theirs = refs[:count], refs[count], refs[count + 1 :]
    for index, (piece, out) in enumerate(zip(pieces, theirs)):
        mine[index * capacity : (index + 1) * capacity, :] = piece[:capacity, :]
        out[...] = piece[capacity:, :]


def split_body(half, size, mine, theirs, weights, normed, *outs):
    home_one, home_two, home_three, *away, keys_turned = outs
    width = size // 2
    keys_turned[...] = dot(weights[:, width : 2 * width], normed[...], 0, 1).astype(BF)

    def place(home, other):
        home_one[...] = home[:size, :]
        home_two[...], home_three[...] = home[size : 3 * size // 2, :], home[3 * size // 2 :, :]
        away[0][...] = other[:size, :]
        away[1][...], away[2][...] = other[size : 3 * size // 2, :], other[3 * size // 2 :, :]

    @pl.when(at_home(half))
    def _():
        place(mine, theirs)

    @pl.when(jnp.logical_not(at_home(half)))
    def _():
        place(theirs, mine)


def combine_body(
    width,
    experts,
    capacity,
    middle,
    normed_two,
    probs,
    cotangent,
    routes,
    attended,
    weights_tail,
    select,
    *refs,
):
    mixed, middle_grad, attended_grad, tail_grad, held = refs[-5:]
    start = 0
    for ref in refs[:-5]:
        held[start : start + ref.shape[0], :] = ref[...]
        start += ref.shape[0]
    rows = middle.shape[0]
    slots = experts * capacity
    gain_two = weights_tail[:, width:].astype(F32).T[experts + 1 : experts + 2, :]
    gain_grad = jnp.zeros((1, width), F32)
    router_rows = []
    branch_rows = []
    tile = rows
    for start in range(0, rows, tile):
        at = slice(start, start + tile)
        lanes = lane_iota(tile).astype(F32)
        wide = lax.broadcasted_iota(jnp.int32, (tile, slots), 1).astype(F32)
        first = (wide == routes[at, 0:1]).astype(F32)
        second = (wide == routes[at, 1:2]).astype(F32)
        picked = dot(
            jnp.concatenate([first, second], axis=0).astype(BF), held[:, :width]
        )
        grad_two = dot((first + second).astype(BF), held[:, width:])
        upstream = cotangent[at, :].astype(F32)
        share = probs[at, :]
        mid = middle[at, :]
        total = mid
        probs_grad = jnp.zeros((tile, LANES), F32)
        for choice in range(2):
            chosen = lanes == routes[at, 2 + choice : 3 + choice]
            gate = jnp.sum(jnp.where(chosen, share, 0.0), axis=1, keepdims=True)
            one = picked[choice * tile : (choice + 1) * tile, :]
            total = total + gate * one
            gate_grad = jnp.sum(one * upstream, axis=1, keepdims=True)
            probs_grad = probs_grad + jnp.where(chosen, gate_grad, 0.0)
        mixed[at, :] = total.astype(BF)
        logits_grad = (
            share * (probs_grad - jnp.sum(share * probs_grad, axis=1, keepdims=True))
        ).astype(BF)
        router_rows.append(logits_grad)
        grad_two = grad_two + dot(logits_grad, weights_tail[:, width:], 1, 1)
        centered = mid - jnp.mean(mid, axis=1, keepdims=True)
        variance = jnp.mean(centered * centered, axis=1, keepdims=True)
        rstd = lax.rsqrt(variance + EPSILON)
        xhat = centered * rstd
        gain_grad = gain_grad + jnp.sum(grad_two * xhat, axis=0, keepdims=True)
        inner = grad_two * gain_two
        inner_grad = rstd * (
            inner
            - jnp.mean(inner, axis=1, keepdims=True)
            - xhat * jnp.mean(inner * xhat, axis=1, keepdims=True)
        )
        through = upstream + inner_grad
        middle_grad[at, :] = through
        branch = through.astype(BF)
        branch_rows.append(branch)
        attended_grad[at, :] = dot(branch, weights_tail[:, :width], 1, 1).astype(BF)
    sel = select[...]
    logits_grad = jnp.concatenate(router_rows, axis=0)
    branch = jnp.concatenate(branch_rows, axis=0)
    attended_turned = dot(attended[...], sel).astype(BF)
    normed_turned = dot(normed_two[...], sel).astype(BF)
    tail_grad[:, :width] = dot(attended_turned, branch, 0, 0).astype(BF)
    gain_line = jnp.broadcast_to(gain_grad, (8, width))
    upper = gain_line.astype(BF)
    lower = (gain_line - upper.astype(F32)).astype(BF)
    gain_turned = dot(upper, sel) + dot(lower, sel)
    gain_column = jnp.broadcast_to(gain_turned[0:1, :], (LANES, width)).T
    router_grad = dot(normed_turned, logits_grad, 0, 0)
    tail_grad[:, width:] = jnp.where(
        lane_iota(width) == experts + 1, gain_column, router_grad
    ).astype(BF)


def backward_body(
    width,
    qkv,
    keys_turned,
    lse,
    attended_grad,
    idcol,
    idrow,
    normed,
    tail_grad,
    dq,
    rims_low,
    rims_high,
    inner,
    kept,
    *sents,
):
    rows = attended_grad.shape[0]
    half_rows = width // 2
    *sents, acc = sents
    half = lane_iota(BLOCK) < HEAD_DIM
    upper = lax.broadcasted_iota(jnp.int32, (LANES, BLOCK), 0) < HEAD_DIM
    acc[...] = jnp.zeros_like(acc)

    def attend(block, carry):
        base = pl.multiple_of(block * BLOCK, BLOCK)
        window = pl.ds(base, WINDOW)
        here = pl.ds(base, BLOCK)
        marks = idrow[0:1, pl.ds(base + HALO, BLOCK)]
        same = idcol[window, 0:1] == jnp.concatenate([marks, marks], axis=1)
        for pair in range(width // LANES):
            start = pair * LANES
            queries = qkv[pl.ds(base + HALO, BLOCK), start : start + LANES]
            queries = stacked((queries.astype(F32) * SCALE).astype(BF), half)
            grads = stacked(attended_grad[here, start : start + LANES], half)
            keys = qkv[window, width + start : width + start + LANES]
            values = qkv[window, 2 * width + start : 2 * width + start + LANES]
            logs = jnp.concatenate(
                [lse[2 * pair : 2 * pair + 1, here], lse[2 * pair + 1 : 2 * pair + 2, here]], axis=1
            )
            scores = jnp.where(same, dot(keys, queries, 1, 1), MASKED)
            weights = jnp.exp(scores - logs)
            weights_grad = dot(values, grads, 1, 1)
            delta = jnp.sum(weights * weights_grad, axis=0, keepdims=True)
            scores_grad = (weights * (weights_grad - delta)).astype(BF)
            acc[window, start : start + LANES] += dot(scores_grad, queries)
            acc[window, width + start : width + start + LANES] += dot(weights.astype(BF), grads)
            result = dot(keys_turned[start : start + LANES, window], scores_grad) * SCALE
            dq[here, start : start + LANES] = (
                jnp.where(upper, result[:, :BLOCK], result[:, BLOCK:]).T.astype(BF)
            )
        return carry

    lax.fori_loop(0, rows // BLOCK, attend, 0, unroll=2)
    rims_low[...] = acc[:HALO, :].astype(BF)
    rims_high[...] = acc[HALO + rows :, :].astype(BF)
    inner[...] = acc[HALO : HALO + rows, :]
    own = normed[HALO : HALO + rows, :]
    query_part = dot(own, dq[...], 0, 0)
    kept[:, :width] = query_part[:half_rows]
    other_part = dot(normed[...], acc[...].astype(BF), 0, 0)
    kept[:, width : 3 * width] = other_part[:half_rows]
    kept[:, 3 * width :] = tail_grad[:half_rows, :].astype(F32)
    size = half_rows // len(sents)
    for index, sent in enumerate(sents):
        at = slice(half_rows + index * size, half_rows + (index + 1) * size)
        sent[:, :width] = query_part[at].astype(BF)
        sent[:, width : 3 * width] = other_part[at].astype(BF)
        sent[:, 3 * width :] = tail_grad[at, :]


def finish_body(
    width, dq, inner, from_low, from_high, weights, normed_gain, xhat, rstd, select, middle_grad, out, grad
):
    rows = dq.shape[0]
    experts_lane = 0
    grad[...] = inner[...]
    grad[:HALO, :] += from_low[...].astype(F32)
    grad[rows - HALO :, :] += from_high[...].astype(F32)
    values = dot(dq[...], weights[:, :width], 1, 1) + dot(
        grad[...].astype(BF), weights[:, width:], 1, 1
    )
    hat = xhat[HALO : HALO + rows, :]
    values = values * normed_gain[0:1, :]
    part = rstd[HALO : HALO + rows, 0:1] * (
        values
        - jnp.mean(values, axis=1, keepdims=True)
        - hat * jnp.mean(values * hat, axis=1, keepdims=True)
    )
    upper = part.astype(BF)
    lower = (part - upper.astype(F32)).astype(BF)
    sel = select[...]
    out[...] = (middle_grad[...] + dot(upper, sel, 1, 1) + dot(lower, sel, 1, 1)).astype(BF)


def sum_body(parts, own, *refs):
    arrived, outs = refs[: len(refs) - parts], refs[len(refs) - parts :]
    total = own[...].astype(F32)
    if arrived[0].shape[0] < total.shape[0]:
        total = total + jnp.concatenate([ref[...].astype(F32) for ref in arrived], axis=0)
    else:
        for ref in arrived:
            total = total + ref[...].astype(F32)
    size = total.shape[0] // parts
    for index, out in enumerate(outs):
        out[...] = total[index * size : (index + 1) * size, :].astype(out.dtype)


def final_body(width, experts, own, *refs):
    arrived, rest = refs[:-13], refs[-13:]
    w_qkv, gain, *parts, qkv_grad, proj_grad, router_grad, one, two, in_grad, out_grad = rest
    total = own[...]
    for ref in arrived:
        total = total + ref[...].astype(F32)
    qkv = total[:, : 3 * width]
    qkv_grad[...] = qkv
    proj_grad[...] = total[:, 3 * width : 4 * width]
    gain_grad = jnp.sum(qkv * w_qkv[...].astype(F32), axis=1, keepdims=True)
    tail = total[:, 4 * width :]
    share = own.shape[0]
    diagonal = lax.broadcasted_iota(jnp.int32, (share, share), 0) == lane_iota(share, share)

    def turned(column):
        return jnp.sum(jnp.where(diagonal, column, 0.0), axis=0, keepdims=True)

    one[...] = turned(gain_grad) / gain[...].astype(F32)
    two[...] = turned(tail[:, experts + 1 : experts + 2])
    for index in range(experts):
        router_grad[index : index + 1, :] = turned(tail[:, index : index + 1])
    mine, upper, lower, other = parts
    for out, at, beside in (
        (in_grad, slice(0, width), upper),
        (out_grad, slice(width, 2 * width), lower),
    ):
        out[0] = mine[at, :].astype(F32) + beside[...].astype(F32) + other[at, :].astype(F32)


def gather_stages(devices):
    bits = devices.bit_length() - 1
    stages = []
    top = bits - 1
    while top >= 1:
        if top >= 2:
            low, high = 1 << (top - 1), 1 << top
            stages.append([low, high, low | high])
            top -= 2
        else:
            stages.append([1 << top])
            top -= 1
    stages.append([1])
    return stages


def swap(value, devices, mask):
    return lax.ppermute(value, "dp", [(i, i ^ mask) for i in range(devices)])


def reduce_scattered(kept, sent, devices, stages, before, after):
    total = kept
    arrived = [swap(part, devices, stages[-1][0]) for part in sent]
    for level in range(len(stages) - 1, 0, -1):
        masks = stages[level - 1]
        parts = 1 + len(masks)
        dims = (total.shape[0] // parts, total.shape[1])
        outs = [shape(dims, F32)] + [shape(dims, BF)] * (parts - 1)
        if level == 1:
            arrived, before[-1], after = lax.optimization_barrier((arrived, before[-1], after))
        if level == 2:
            arrived, before[:-1] = lax.optimization_barrier((arrived, before[:-1]))
        pieces = call(
            functools.partial(sum_body, parts), outs, [total] + arrived, name=f"sum{level}"
        )
        total = pieces[0]
        arrived = [swap(piece, devices, mask) for piece, mask in zip(pieces[1:], masks)]
    return total, arrived, before, after


def per_device(
    tokens,
    gain_attn,
    w_qkv,
    w_proj,
    gain_moe,
    w_router,
    w_in,
    w_out,
    cotangent,
    image_ids,
    expert_ids,
    slots,
):
    devices = lax.axis_size("dp")
    experts = devices // 4
    rows, width = tokens.shape
    capacity = max(2, 5 * rows // (2 * experts))
    share = width // devices
    span = rows + 2 * HALO
    stages = gather_stages(devices)
    everyone = range(devices)
    half = devices // 2

    ins = [
        w_qkv,
        w_proj,
        w_router.T,
        gain_attn[None, :],
        gain_moe[None, :],
        tokens,
        image_ids.reshape(rows // BLOCK, BLOCK),
    ]
    packed, own, low, high = call(
        functools.partial(pack_body, experts),
        [
            shape((share, 4 * width + LANES), BF),
            shape((rows, width + LANES), BF),
            shape((HALO, width + LANES), BF),
            shape((HALO, width + LANES), BF),
        ],
        ins,
        scratch=[pltpu.VMEM(x.shape, x.dtype) for x in ins]
        + [pltpu.SemaphoreType.DMA((len(ins),))],
        name="pack",
        fetch=True,
    )
    up = [(i, i + 1) for i in range(devices - 1)]
    down = [(i + 1, i) for i in range(devices - 1)]
    low = lax.ppermute(low, "dp", up)
    high = lax.ppermute(high, "dp", down)
    packed, w_in = lax.optimization_barrier((packed, w_in))
    quarter = call(
        functools.partial(quarter_body, width),
        [shape((2 * width, width), BF)],
        [w_in, w_out],
        scratch=[pltpu.SemaphoreType.DMA((2,))],
        name="quarter",
        fetch=True,
    )[0]
    order = [0]
    near = [packed]
    far = None
    for stage in stages:
        order = [a ^ mask for mask in [0] + stage for a in order]
        arrived = [swap(part, devices, mask) for mask in stage for part in near]
        if stage is stages[0]:
            arrived[0], low, high, quarter = lax.optimization_barrier(
                (arrived[0], low, high, quarter)
            )
            arrived[1], quarter_far = lax.optimization_barrier((arrived[1], quarter))
        if stage is stages[-2]:
            *arrived, late_in = lax.optimization_barrier((*arrived, w_in[0]))
        if stage is stages[-1]:
            far = arrived
        else:
            parts = 2 if stage is stages[-2] else 1
            size = near[0].shape[0] * (1 + len(stage)) // parts
            near = call(
                functools.partial(join_body, parts),
                [shape((size, near[0].shape[1]), BF)] * parts,
                [*near, *arrived],
                name="join",
            )
    order = np.stack(
        [
            np.repeat(np.array(order, np.int32), share),
            np.tile(np.arange(share, dtype=np.int32), devices),
        ]
    )

    far_quarter = swap(quarter_far, devices, half)
    near_in = swap(late_in, devices, 2)

    def exchange(parts):
        return [parts[0]] + [
            swap(part, devices, 4 * index) for index, part in enumerate(parts) if index
        ]

    xhat, rstd, select, idcol, idrow, routes, place_row = call(
        functools.partial(prepare_body, width, experts, capacity),
        [
            shape((span, width), F32),
            shape((span, LANES), F32),
            shape((width, width), BF),
            shape((span, LANES), F32),
            shape((8, span), F32),
            shape((rows, LANES), F32),
            shape((8, rows), F32),
        ],
        [own, low, high, jnp.asarray(order), expert_ids.T, slots.T],
        flops=2 * span * width * width,
        name="prepare",
    )
    chips = experts // 2
    half_slots = chips * capacity
    outs = call(
        functools.partial(forward_body, width, experts, capacity),
        [shape((half_slots, 2 * width), BF)]
        + [shape((capacity, 2 * width), BF)] * chips
        + [
            shape((span, 3 * width), BF),
            shape((rows, width), BF),
            shape((8, rows), F32),
            shape((rows, width), F32),
            shape((rows, width), BF),
            shape((rows, LANES), F32),
            shape((span, width), BF),
            shape((width, 3 * width), BF),
            shape((width, width + LANES), BF),
            shape((8, width), F32),
        ],
        [xhat, idcol, idrow, select, own, cotangent, routes, place_row, *near, *far],
        name="forward",
    )
    same_core, other_core, outs = outs[0], outs[1 : 1 + chips], outs[1 + chips :]
    qkv, attended, lse, middle, normed_two, probs, normed, weights, weights_tail, gain = outs

    both = shape((2 * capacity, 2 * width), BF)
    *other_core, near_in = lax.optimization_barrier((*other_core, near_in))
    pieces = call(
        functools.partial(mix_body, capacity),
        [both] * chips,
        [same_core, *[swap(part, devices, 1) for part in other_core]],
        name="mix",
    )
    far_quarter, late_out, piece = lax.optimization_barrier((far_quarter, w_out[0], pieces[0]))
    near_out = swap(late_out, devices, 2)
    arrived = exchange([piece, *pieces[1:]])
    far_half = call(
        halve_body, [shape((width, width), BF)] * 2, [far_quarter], name="halve"
    )
    far_half = [*far_half] + [swap(part, devices, 2) for part in far_half]
    slot_count = experts * capacity
    pair = shape((4 * width, width), BF)
    far_half[-1], *arrived[1:-1] = lax.optimization_barrier((far_half[-1], *arrived[1:-1]))
    kept_pair, *sent_parts = call(
        functools.partial(choose_body, half, width),
        [pair] + [shape((width, width), BF)] * 4,
        [quarter, near_in, near_out, *far_half],
        name="choose",
    )
    expert_weights = [kept_pair] + [swap(part, devices, 1) for part in sent_parts]
    tile = slot_count // 4
    held = pltpu.VMEM((slot_count, 2 * width), BF)
    back, hidden, pre_grad = [], [], []
    for part in (arrived[: chips // 2], arrived[chips // 2 :]):
        half_held = pltpu.VMEM((half_slots, 2 * width), BF)
        outs = call(
            functools.partial(expert_body, width, tile, len(part)),
            [both] * len(part) + [shape((half_slots, 4 * width), BF)] * 2,
            [*part, *expert_weights],
            scratch=[
                half_held,
                half_held,
                pltpu.VMEM((width, 4 * width), BF),
                pltpu.VMEM((4 * width, width), BF),
            ],
            flops=4 * slot_count * width * 4 * width,
            name="expert",
            vmem_mib=16,
        )
        back += outs[: len(part)]
        hidden.append(outs[-2])
        pre_grad.append(outs[-1])
    returned = exchange(back)
    kept_pair, sent_pair = call(
        functools.partial(expert_grad_body, width, chips),
        [pair, pair],
        [*arrived, *hidden, *pre_grad],
        vmem_mib=16,
        flops=4 * slot_count * width * 4 * width,
        name="expert_grad",
    )
    other_pair = swap(sent_pair, devices, 1)
    single = shape((2 * width, width), BF)
    square = shape((width, width), BF)
    home_kept, *home_sent = call(
        functools.partial(split_body, half, 2 * width),
        [single, square, square] * 2 + [shape((width, span), BF)],
        [kept_pair, other_pair, weights, normed],
        name="split",
    )
    home_sent, (away_kept, *away_sent, keys_turned) = home_sent[:2], home_sent[2:]
    away_came = [swap(part, devices, 2) for part in away_sent]
    *home_sent, returned[1] = lax.optimization_barrier((*home_sent, returned[1]))
    home_came = [swap(part, devices, 2) for part in home_sent]
    away = call(
        functools.partial(sum_body, 1), [single], [away_kept, *away_came], name="away"
    )[0]

    returned[-1], away = lax.optimization_barrier((returned[-1], away))
    mine, *theirs = call(
        functools.partial(unmix_body, capacity),
        [shape((half_slots, 2 * width), BF)] + [shape((capacity, 2 * width), BF)] * chips,
        returned,
        name="unmix",
    )
    theirs = [swap(part, devices, 1) for part in theirs]
    mixed, middle_grad, attended_grad, tail_grad = call(
        functools.partial(combine_body, width, experts, capacity),
        [
            shape((rows, width), BF),
            shape((rows, width), F32),
            shape((rows, width), BF),
            shape((width, width + LANES), BF),
        ],
        [
            middle,
            normed_two,
            probs,
            cotangent,
            routes,
            attended,
            weights_tail,
            select,
            mine,
            *theirs,
        ],
        scratch=[pltpu.VMEM((slot_count, 2 * width), BF)],
        flops=6 * rows * slot_count * width,
        name="combine",
    )
    expert_parts = [home_kept, *home_came, swap(away, devices, half)]
    half_rows = width // 2

    dq, rims_low, rims_high, inner, kept, *sent = call(
        functools.partial(backward_body, width),
        [
            shape((rows, width), BF),
            shape((HALO, 2 * width), BF),
            shape((HALO, 2 * width), BF),
            shape((rows, 2 * width), F32),
            shape((half_rows, 4 * width + LANES), F32),
        ]
        + [shape((half_rows // 4, 4 * width + LANES), BF)] * 4,
        [qkv, keys_turned, lse, attended_grad, idcol, idrow, normed, tail_grad],
        scratch=[pltpu.VMEM((span, 2 * width), F32)],
        name="backward",
    )
    total, last, expert_parts, (rims_low, rims_high) = reduce_scattered(
        kept, sent, devices, stages, expert_parts, [rims_low, rims_high]
    )
    from_high = lax.ppermute(rims_low, "dp", down)
    from_low = lax.ppermute(rims_high, "dp", up)
    grad_tokens = call(
        functools.partial(finish_body, width),
        [shape((rows, width), BF)],
        [dq, inner, from_low, from_high, weights, gain, xhat, rstd, select, middle_grad],
        scratch=[pltpu.VMEM((rows, 2 * width), F32)],
        flops=2 * rows * width * 5 * width,
        name="finish",
    )[0]

    last[0], grad_tokens = lax.optimization_barrier((last[0], grad_tokens))
    qkv_grad, proj_grad, router_grad, gain_one_grad, gain_two_grad, in_grad, out_grad = call(
        functools.partial(final_body, width, experts),
        [
            shape((share, 3 * width), F32),
            shape((share, width), F32),
            shape((experts, share), F32),
            shape((1, share), F32),
            shape((1, share), F32),
            shape((1, width, width), F32),
            shape((1, width, width), F32),
        ],
        [total, *last, w_qkv, gain_attn[None, :], *expert_parts],
        name="final",
    )
    return (
        mixed,
        grad_tokens,
        gain_one_grad.reshape(share),
        qkv_grad,
        proj_grad,
        gain_two_grad.reshape(share),
        router_grad.T,
        in_grad,
        out_grad,
    )


def solution(mesh):
    row, line, cube = P("dp", None), P("dp"), P("dp", None, None)
    return jax.shard_map(
        per_device,
        mesh=mesh,
        in_specs=(row, line, row, row, line, row, cube, cube, row, line, row, row),
        out_specs=(row, row, line, row, row, line, row, cube, cube),
        check_vma=False,
    )
```

```python
import functools

import jax
import jax.numpy as jnp
import numpy as np
from jax import lax
from jax.experimental import pallas as pl
from jax.experimental.pallas import tpu as pltpu
from jax.sharding import PartitionSpec as P

HEAD_DIM = 64
LEN = 197
EPSILON = 1e-06
MASKED = -1e30
HALO = 256
BLOCK = 128
WINDOW = BLOCK + 2 * HALO
LANES = 128
SCALE = HEAD_DIM ** (-0.5)
BF = jnp.bfloat16
F32 = jnp.float32
GELU_C = (2.0 / np.pi) ** 0.5
GELU_A = 0.044715


def dot(left, right, left_dim=1, right_dim=0):
    return lax.dot_general(
        left,
        right,
        (((left_dim,), (right_dim,)), ((), ())),
        preferred_element_type=F32,
    )


def call(body, outs, ins, scratch=(), flops=0, name=None, vmem_mib=12, fetch=False):
    vmem = pl.BlockSpec(memory_space=pltpu.VMEM)
    spec = pl.BlockSpec(memory_space=pltpu.HBM) if fetch else vmem
    if fetch:
        ins = [pltpu.with_memory_space_constraint(x, pltpu.HBM) for x in ins]
    return pl.pallas_call(
        body,
        out_shape=tuple(outs),
        in_specs=[spec] * len(ins),
        out_specs=tuple([vmem] * len(outs)),
        scratch_shapes=list(scratch),
        compiler_params=pltpu.CompilerParams(vmem_limit_bytes=vmem_mib * 1024 * 1024),
        cost_estimate=pl.CostEstimate(flops=int(flops), bytes_accessed=1024, transcendentals=0),
        name=name,
    )(*ins)


def shape(dims, dtype):
    return jax.ShapeDtypeStruct(dims, dtype)


def lane_iota(rows, lanes=LANES):
    return lax.broadcasted_iota(jnp.int32, (rows, lanes), 1)


def fetched(refs, held, sems):
    copies = [
        pltpu.make_async_copy(ref, into, sems.at[index])
        for index, (ref, into) in enumerate(zip(refs, held))
    ]
    for copy in copies:
        copy.start()
    for copy in copies:
        copy.wait()


def pack_body(experts, *refs):
    count = 7
    (out, own, low, high), held, sems = refs[count : count + 4], refs[count + 4 : -1], refs[-1]
    fetched(refs[:count], held, sems)
    w_qkv, w_proj, router_turned, gain_attn, gain_moe, tokens, ids = held
    share, cols = w_qkv.shape
    width = cols // 3
    out[:, :cols] = w_qkv[...]
    out[:, cols : 4 * width] = w_proj[...]
    lanes = lane_iota(share)
    diagonal = lax.broadcasted_iota(jnp.int32, (share, share), 0) == lane_iota(share, share)
    pick = lax.broadcasted_iota(jnp.int32, (experts, LANES), 0) == lane_iota(experts)
    tail = dot(router_turned[...], pick.astype(F32).astype(BF), 0, 0)
    for index, gain in enumerate((gain_attn, gain_moe)):
        column = jnp.sum(
            jnp.where(diagonal, gain[...].astype(F32), 0.0), axis=1, keepdims=True
        )
        tail = jnp.where(lanes == experts + index, column, tail)
    out[:, 4 * width :] = tail.astype(BF)
    rows = tokens.shape[0]
    own[:, :width] = tokens[...]
    for index in range(rows // BLOCK):
        line = (ids[index : index + 1, :] + 1).astype(F32)
        column = jnp.broadcast_to(line, (BLOCK, BLOCK)).T
        upper = jnp.floor(column * (1.0 / 256.0))
        lower = column - 256.0 * upper
        own[index * BLOCK : (index + 1) * BLOCK, width:] = jnp.where(
            lane_iota(BLOCK) == 0, upper, lower
        ).astype(BF)
    low[...] = own[rows - HALO :, :]
    high[...] = own[:HALO, :]


def quarter_body(width, w_in, w_out, quarter, sems):
    fetched(
        (w_in.at[0], w_out.at[0]), (quarter.at[:width, :], quarter.at[width:, :]), sems
    )


def join_body(parts, *refs):
    pieces, outs = refs[:-parts], refs[-parts:]
    whole = jnp.concatenate([piece[...].astype(F32) for piece in pieces], axis=0).astype(BF)
    size = whole.shape[0] // parts
    for index, out in enumerate(outs):
        out[...] = whole[index * size : (index + 1) * size, :]


def normed_rows(ref, width, sel):
    values = dot(ref[:, :width], sel)
    centered = values - jnp.mean(values, axis=1, keepdims=True)
    rstd = lax.rsqrt(jnp.mean(centered * centered, axis=1, keepdims=True) + EPSILON)
    return centered * rstd, rstd


def halo_body(width, own, low, high, select, xhat, idcol, idrow):
    sel = select[...]
    xhat[:HALO, :] = normed_rows(low, width, sel)[0]
    xhat[HALO:, :] = normed_rows(high, width, sel)[0]
    start = 0
    for ref in (low, own, high):
        rows = ref.shape[0]
        marks = ref[:, width : width + LANES].astype(F32)
        column = marks[:, 0:1] * 256.0 + marks[:, 1:2]
        idcol[start : start + rows, :] = jnp.broadcast_to(column, (rows, LANES))
        turned = marks.T
        line = turned[0:1, :] * 256.0 + turned[1:2, :]
        idrow[:, start : start + rows] = jnp.broadcast_to(line, (8, rows))
        start += rows


def prepare_body(
    width,
    experts,
    capacity,
    own,
    order,
    experts_row,
    slots_row,
    xhat,
    rstd_out,
    select,
    routes,
    place_row,
):
    me = lax.axis_index("dp")
    devices = 4 * experts
    share = width // devices
    target = (me ^ order[0:1, :]) * share + order[1:2, :]
    sel = (lax.broadcasted_iota(jnp.int32, (width, width), 0) == target).astype(F32).astype(BF)
    select[...] = sel
    xhat[...], rstd = normed_rows(own, width, sel)
    rstd_out[...] = jnp.broadcast_to(rstd, rstd_out.shape)
    rows = own.shape[0]
    group = (((me >> 2) & (experts // 2 - 1)) << 1) | (me & 1)
    half_bits = (experts // 2).bit_length() - 1
    expert = experts_row[...]
    slot = slots_row[...]
    holder = ((expert & (experts // 2 - 1)) << 1) | (expert >> half_bits)
    apart = group ^ holder
    index = (apart & 1) * (experts // 2) + (apart >> 1)
    place = jnp.where(slot >= 0, index * capacity + slot, -1).astype(F32)
    lines = jnp.concatenate(
        [place, expert.astype(F32), jnp.zeros((4, rows), F32)], axis=0
    )
    place_row[...] = lines
    routes[...] = jnp.concatenate([lines] * (LANES // 8), axis=0).T


def stacked(values, half):
    zero = jnp.zeros_like(values)
    return jnp.concatenate(
        [jnp.where(half, values, zero), jnp.where(half, zero, values)], axis=0
    )


def forward_body(
    width,
    experts,
    capacity,
    xhat,
    xhat_halo,
    idcol,
    idrow,
    select,
    own,
    cotangent,
    routes,
    place_row,
    near_one,
    near_two,
    far_one,
    far_two,
    *outs,
):
    same_core, other_core, outs = outs[0], outs[1 : 1 + experts // 2], outs[1 + experts // 2 :]
    qkv, attended, lse, middle, normed_two, probs, normed, weights, weights_tail, gain = outs
    rows = own.shape[0]
    cols = 3 * width
    parts = (near_one, near_two, far_one, far_two)
    size = width // 4
    for index, part in enumerate(parts):
        weights[index * size : (index + 1) * size, :] = part[:, :cols]
    sel = select[...]
    tail = jnp.concatenate([part[:, cols:] for part in parts], axis=0)
    gain_row = tail[:, width:].astype(F32).T[experts : experts + 1, :]
    gain[...] = jnp.broadcast_to(gain_row, (8, width))
    natural = dot(sel, tail)
    weights_tail[...] = natural.astype(BF)
    gain_two = natural[:, width:].T[experts + 1 : experts + 2, :]
    normed[:HALO, :] = (xhat_halo[:HALO, :] * gain_row).astype(BF)
    normed[HALO : HALO + rows, :] = (xhat[...] * gain_row).astype(BF)
    normed[HALO + rows :, :] = (xhat_halo[HALO:, :] * gain_row).astype(BF)
    qkv[HALO : HALO + rows, :] = dot(normed[HALO : HALO + rows, :], weights[...]).astype(BF)
    for first in (0, HALO + rows):
        qkv[first : first + HALO, width:] = dot(
            normed[first : first + HALO, :], weights[:, width:]
        ).astype(BF)
    half = lane_iota(BLOCK) < HEAD_DIM

    def attend(block, carry):
        base = pl.multiple_of(block * BLOCK, BLOCK)
        window = pl.ds(base, WINDOW)
        here = pl.ds(base, BLOCK)
        marks = idrow[0:1, pl.ds(base + HALO, BLOCK)]
        same = idcol[window, 0:1] == jnp.concatenate([marks, marks], axis=1)
        for pair in range(width // LANES):
            start = pair * LANES
            queries = qkv[pl.ds(base + HALO, BLOCK), start : start + LANES]
            queries = stacked((queries.astype(F32) * SCALE).astype(BF), half)
            keys = qkv[window, width + start : width + start + LANES]
            values = qkv[window, 2 * width + start : 2 * width + start + LANES]
            scores = jnp.where(same, dot(keys, queries, 1, 1), MASKED)
            peak = jnp.max(scores, axis=0, keepdims=True)
            raised = jnp.exp(scores - peak)
            total = jnp.sum(raised, axis=0, keepdims=True)
            result = dot(raised.astype(BF), values, 0, 0)
            column = jnp.broadcast_to(1.0 / total, (8, 2 * BLOCK)).T[:, 0:1]
            result = result * column
            attended[here, start : start + LANES] = jnp.where(
                half, result[:BLOCK], result[BLOCK:]
            ).astype(BF)
            logs = peak + jnp.log(total)
            lse[2 * pair : 2 * pair + 1, here] = logs[:, :BLOCK]
            lse[2 * pair + 1 : 2 * pair + 2, here] = logs[:, BLOCK:]
        return carry

    lax.fori_loop(0, rows // BLOCK, attend, 0, unroll=4)
    mid = own[:, :width].astype(F32) + dot(attended[...], weights_tail[:, :width])
    middle[...] = mid
    centered = mid - jnp.mean(mid, axis=1, keepdims=True)
    variance = jnp.mean(centered * centered, axis=1, keepdims=True)
    low_two = (centered * lax.rsqrt(variance + EPSILON) * gain_two).astype(BF)
    normed_two[...] = low_two
    lanes = lane_iota(rows)
    logits = jnp.where(lanes < experts, dot(low_two, weights_tail[:, width:]), MASKED)
    raised = jnp.exp(logits - jnp.max(logits, axis=1, keepdims=True))
    share = raised / jnp.sum(raised, axis=1, keepdims=True)
    probs[...] = share
    upstream = cotangent[...].astype(F32)
    wide_lanes = lanes.astype(F32)
    gates = []
    for choice in range(2):
        gate = jnp.sum(
            jnp.where(wide_lanes == routes[:, 2 + choice : 3 + choice], share, 0.0),
            axis=1,
            keepdims=True,
        )
        gates.append(jnp.broadcast_to(gate, (rows, 8)))
    gates = jnp.concatenate(gates + [jnp.zeros((rows, LANES - 16), F32)], axis=1).T
    source = jnp.concatenate([low_two, cotangent[...]], axis=1)
    for index in range(experts):
        if index < experts // 2:
            chunk = same_core.at[index * capacity : (index + 1) * capacity, :]
        else:
            chunk = other_core[index - experts // 2]
        slot = (
            lax.broadcasted_iota(jnp.int32, (capacity, rows), 0) + index * capacity
        ).astype(F32)
        first = slot == place_row[0:1, :]
        second = slot == place_row[1:2, :]
        weight = jnp.where(first, gates[0:1, :], jnp.where(second, gates[8:9, :], 0.0))
        taken = jnp.where(first | second, 1.0, 0.0)
        moved = dot(taken.astype(BF), source)
        chunk[:, :width] = moved[:, :width].astype(BF)
        chunk[:, width:] = (
            moved[:, width:] * jnp.sum(weight, axis=1, keepdims=True)
        ).astype(BF)


def joined(pieces, held):
    capacity = pieces[0].shape[0]
    for index, piece in enumerate(pieces):
        held[index * capacity : (index + 1) * capacity, :] = piece[...]


def expert_body(width, tile, count, *refs):
    pieces, kept, sent, rest = (
        refs[:count],
        refs[count],
        refs[count + 1 : count + 5],
        refs[count + 5 :],
    )
    returns, (hidden_out, grad_out, arrived, back, w_in, w_out) = rest[:count], rest[count:]
    joined(pieces, arrived)
    w_ins = [kept.at[:width, :], kept.at[2 * width : 3 * width, :], sent[0], sent[2]]
    w_outs = [kept.at[width : 2 * width, :], kept.at[3 * width :, :], sent[1], sent[3]]
    for quarter, (first, second) in enumerate(zip(w_ins, w_outs)):
        at = slice(quarter * width, (quarter + 1) * width)
        w_in[:, at] = first[...]
        w_out[at, :] = second[...]
    step_width = 2 * width // 3

    def step(index, carry):
        at = pl.ds(pl.multiple_of(index * tile, tile), tile)
        for start in range(0, 4 * width, step_width):
            columns = slice(start, start + step_width)
            pre = dot(arrived[at, :width], w_in[:, columns])
            hidden_grad = dot(arrived[at, width:], w_out[columns, :], 1, 1)
            square = pre * pre
            bend = jnp.tanh(pre * (GELU_C + (GELU_C * GELU_A) * square))
            scaled = 0.5 * pre
            hidden_out[at, columns] = (scaled + scaled * bend).astype(BF)
            slope = (0.5 + 0.5 * bend) + (
                scaled * (GELU_C + (3.0 * GELU_C * GELU_A) * square)
            ) * (1.0 - bend * bend)
            grad_out[at, columns] = (hidden_grad * slope).astype(BF)
        back[at, :width] = dot(hidden_out[at, :], w_out[...]).astype(BF)
        back[at, width:] = dot(grad_out[at, :], w_in[...], 1, 1).astype(BF)
        return carry

    lax.fori_loop(0, arrived.shape[0] // tile, step, 0)
    capacity = pieces[0].shape[0]
    for index, out in enumerate(returns):
        out[...] = back[index * capacity : (index + 1) * capacity, :]


def expert_grad_body(width, count, *refs):
    pieces, (hidden_one, hidden_two, pre_one, pre_two, kept, sent) = refs[:count], refs[count:]
    size = 2 * width
    outs = (kept.at[:size, :], kept.at[size:, :], sent.at[:size, :], sent.at[size:, :])
    grad_in = grad_out = 0.0
    for part, hidden, pre_grad in (
        (pieces[: count // 2], hidden_one, pre_one),
        (pieces[count // 2 :], hidden_two, pre_two),
    ):
        rows = jnp.concatenate([piece[:, :width] for piece in part], axis=0)
        grads = jnp.concatenate([piece[:, width:] for piece in part], axis=0)
        grad_in = grad_in + dot(rows, pre_grad[...], 0, 0)
        grad_out = grad_out + dot(grads, hidden[...], 0, 0)
    for quarter, out in enumerate(outs):
        columns = slice(quarter * width, (quarter + 1) * width)
        out[:width, :] = grad_in[:, columns].astype(BF)
        out[width:, :] = grad_out[:, columns].T.astype(BF)


def at_home(half):
    me = lax.axis_index("dp")
    return (me >= half) == ((me & 1) == 1)


def halve_body(whole, upper, lower):
    size = upper.shape[0]
    upper[...] = whole[:size, :]
    lower[...] = whole[size:, :]


def choose_body(half, size, near_one, near_in, near_out, *refs):
    far, kept, sent = refs[:4], refs[4], refs[5:]
    near = (near_one.at[:size, :], near_one.at[size:, :], near_in, near_out)

    def place(mine, theirs):
        for index, (one, two) in enumerate(zip(mine, theirs)):
            kept[index * size : (index + 1) * size, :] = one[...]
            sent[index][...] = two[...]

    @pl.when(at_home(half))
    def _():
        place(near, far)

    @pl.when(jnp.logical_not(at_home(half)))
    def _():
        place(far, near)


def mix_body(capacity, mine, *refs):
    theirs, outs = refs[: len(refs) // 2], refs[len(refs) // 2 :]
    for index, (part, out) in enumerate(zip(theirs, outs)):
        out[:capacity, :] = mine[index * capacity : (index + 1) * capacity, :]
        out[capacity:, :] = part[...]


def unmix_body(capacity, *refs):
    count = len(refs) // 2
    pieces, mine, theirs = refs[:count], refs[count], refs[count + 1 :]
    for index, (piece, out) in enumerate(zip(pieces, theirs)):
        mine[index * capacity : (index + 1) * capacity, :] = piece[:capacity, :]
        out[...] = piece[capacity:, :]


def split_body(half, size, mine, theirs, weights, normed, *outs):
    home_one, home_two, home_three, *away, keys_turned = outs
    width = size // 2
    keys_turned[...] = dot(weights[:, width : 2 * width], normed[...], 0, 1).astype(BF)

    def place(home, other):
        home_one[...] = home[:size, :]
        home_two[...], home_three[...] = home[size : 3 * size // 2, :], home[3 * size // 2 :, :]
        away[0][...] = other[:size, :]
        away[1][...], away[2][...] = other[size : 3 * size // 2, :], other[3 * size // 2 :, :]

    @pl.when(at_home(half))
    def _():
        place(mine, theirs)

    @pl.when(jnp.logical_not(at_home(half)))
    def _():
        place(theirs, mine)


def combine_body(
    width,
    experts,
    capacity,
    middle,
    normed_two,
    probs,
    cotangent,
    routes,
    attended,
    weights_tail,
    select,
    *refs,
):
    mixed, middle_grad, attended_grad, tail_grad, held = refs[-5:]
    start = 0
    for ref in refs[:-5]:
        held[start : start + ref.shape[0], :] = ref[...]
        start += ref.shape[0]
    rows = middle.shape[0]
    slots = experts * capacity
    gain_two = weights_tail[:, width:].astype(F32).T[experts + 1 : experts + 2, :]
    gain_grad = jnp.zeros((1, width), F32)
    router_rows = []
    branch_rows = []
    tile = rows
    for start in range(0, rows, tile):
        at = slice(start, start + tile)
        lanes = lane_iota(tile).astype(F32)
        wide = lax.broadcasted_iota(jnp.int32, (tile, slots), 1).astype(F32)
        first = (wide == routes[at, 0:1]).astype(F32)
        second = (wide == routes[at, 1:2]).astype(F32)
        picked = dot(
            jnp.concatenate([first, second], axis=0).astype(BF), held[:, :width]
        )
        grad_two = dot((first + second).astype(BF), held[:, width:])
        upstream = cotangent[at, :].astype(F32)
        share = probs[at, :]
        mid = middle[at, :]
        total = mid
        probs_grad = jnp.zeros((tile, LANES), F32)
        for choice in range(2):
            chosen = lanes == routes[at, 2 + choice : 3 + choice]
            gate = jnp.sum(jnp.where(chosen, share, 0.0), axis=1, keepdims=True)
            one = picked[choice * tile : (choice + 1) * tile, :]
            total = total + gate * one
            gate_grad = jnp.sum(one * upstream, axis=1, keepdims=True)
            probs_grad = probs_grad + jnp.where(chosen, gate_grad, 0.0)
        mixed[at, :] = total.astype(BF)
        logits_grad = (
            share * (probs_grad - jnp.sum(share * probs_grad, axis=1, keepdims=True))
        ).astype(BF)
        router_rows.append(logits_grad)
        grad_two = grad_two + dot(logits_grad, weights_tail[:, width:], 1, 1)
        centered = mid - jnp.mean(mid, axis=1, keepdims=True)
        variance = jnp.mean(centered * centered, axis=1, keepdims=True)
        rstd = lax.rsqrt(variance + EPSILON)
        xhat = centered * rstd
        gain_grad = gain_grad + jnp.sum(grad_two * xhat, axis=0, keepdims=True)
        inner = grad_two * gain_two
        inner_grad = rstd * (
            inner
            - jnp.mean(inner, axis=1, keepdims=True)
            - xhat * jnp.mean(inner * xhat, axis=1, keepdims=True)
        )
        through = upstream + inner_grad
        middle_grad[at, :] = through
        branch = through.astype(BF)
        branch_rows.append(branch)
        attended_grad[at, :] = dot(branch, weights_tail[:, :width], 1, 1).astype(BF)
    sel = select[...]
    logits_grad = jnp.concatenate(router_rows, axis=0)
    branch = jnp.concatenate(branch_rows, axis=0)
    attended_turned = dot(attended[...], sel).astype(BF)
    normed_turned = dot(normed_two[...], sel).astype(BF)
    tail_grad[:, :width] = dot(attended_turned, branch, 0, 0).astype(BF)
    gain_line = jnp.broadcast_to(gain_grad, (8, width))
    upper = gain_line.astype(BF)
    lower = (gain_line - upper.astype(F32)).astype(BF)
    gain_turned = dot(upper, sel) + dot(lower, sel)
    gain_column = jnp.broadcast_to(gain_turned[0:1, :], (LANES, width)).T
    router_grad = dot(normed_turned, logits_grad, 0, 0)
    tail_grad[:, width:] = jnp.where(
        lane_iota(width) == experts + 1, gain_column, router_grad
    ).astype(BF)


def backward_body(
    width,
    qkv,
    keys_turned,
    lse,
    attended_grad,
    idcol,
    idrow,
    normed,
    tail_grad,
    dq,
    rims_low,
    rims_high,
    inner,
    kept,
    *sents,
):
    rows = attended_grad.shape[0]
    half_rows = width // 2
    *sents, acc = sents
    half = lane_iota(BLOCK) < HEAD_DIM
    upper = lax.broadcasted_iota(jnp.int32, (LANES, BLOCK), 0) < HEAD_DIM
    acc[...] = jnp.zeros_like(acc)

    def attend(block, carry):
        base = pl.multiple_of(block * BLOCK, BLOCK)
        window = pl.ds(base, WINDOW)
        here = pl.ds(base, BLOCK)
        marks = idrow[0:1, pl.ds(base + HALO, BLOCK)]
        same = idcol[window, 0:1] == jnp.concatenate([marks, marks], axis=1)
        for pair in range(width // LANES):
            start = pair * LANES
            queries = qkv[pl.ds(base + HALO, BLOCK), start : start + LANES]
            queries = stacked((queries.astype(F32) * SCALE).astype(BF), half)
            grads = stacked(attended_grad[here, start : start + LANES], half)
            keys = qkv[window, width + start : width + start + LANES]
            values = qkv[window, 2 * width + start : 2 * width + start + LANES]
            logs = jnp.concatenate(
                [lse[2 * pair : 2 * pair + 1, here], lse[2 * pair + 1 : 2 * pair + 2, here]], axis=1
            )
            scores = jnp.where(same, dot(keys, queries, 1, 1), MASKED)
            weights = jnp.exp(scores - logs)
            weights_grad = dot(values, grads, 1, 1)
            delta = jnp.sum(weights * weights_grad, axis=0, keepdims=True)
            scores_grad = (weights * (weights_grad - delta)).astype(BF)
            acc[window, start : start + LANES] += dot(scores_grad, queries)
            acc[window, width + start : width + start + LANES] += dot(weights.astype(BF), grads)
            result = dot(keys_turned[start : start + LANES, window], scores_grad) * SCALE
            dq[here, start : start + LANES] = (
                jnp.where(upper, result[:, :BLOCK], result[:, BLOCK:]).T.astype(BF)
            )
        return carry

    lax.fori_loop(0, rows // BLOCK, attend, 0, unroll=2)
    rims_low[...] = acc[:HALO, :].astype(BF)
    rims_high[...] = acc[HALO + rows :, :].astype(BF)
    inner[...] = acc[HALO : HALO + rows, :]
    own = normed[HALO : HALO + rows, :]
    query_part = dot(own, dq[...], 0, 0)
    kept[:, :width] = query_part[:half_rows]
    other_part = dot(normed[...], acc[...].astype(BF), 0, 0)
    kept[:, width : 3 * width] = other_part[:half_rows]
    kept[:, 3 * width :] = tail_grad[:half_rows, :].astype(F32)
    size = half_rows // len(sents)
    for index, sent in enumerate(sents):
        at = slice(half_rows + index * size, half_rows + (index + 1) * size)
        sent[:, :width] = query_part[at].astype(BF)
        sent[:, width : 3 * width] = other_part[at].astype(BF)
        sent[:, 3 * width :] = tail_grad[at, :]


def finish_body(
    width, dq, inner, from_low, from_high, weights, normed_gain, xhat, rstd, select, middle_grad, out, grad
):
    rows = dq.shape[0]
    experts_lane = 0
    grad[...] = inner[...]
    grad[:HALO, :] += from_low[...].astype(F32)
    grad[rows - HALO :, :] += from_high[...].astype(F32)
    values = dot(dq[...], weights[:, :width], 1, 1) + dot(
        grad[...].astype(BF), weights[:, width:], 1, 1
    )
    hat = xhat[...]
    values = values * normed_gain[0:1, :]
    part = rstd[:, 0:1] * (
        values
        - jnp.mean(values, axis=1, keepdims=True)
        - hat * jnp.mean(values * hat, axis=1, keepdims=True)
    )
    upper = part.astype(BF)
    lower = (part - upper.astype(F32)).astype(BF)
    sel = select[...]
    out[...] = (middle_grad[...] + dot(upper, sel, 1, 1) + dot(lower, sel, 1, 1)).astype(BF)


def sum_body(parts, own, *refs):
    arrived, outs = refs[: len(refs) - parts], refs[len(refs) - parts :]
    total = own[...].astype(F32)
    if arrived[0].shape[0] < total.shape[0]:
        total = total + jnp.concatenate([ref[...].astype(F32) for ref in arrived], axis=0)
    else:
        for ref in arrived:
            total = total + ref[...].astype(F32)
    size = total.shape[0] // parts
    for index, out in enumerate(outs):
        out[...] = total[index * size : (index + 1) * size, :].astype(out.dtype)


def final_body(width, experts, own, *refs):
    arrived, rest = refs[:-13], refs[-13:]
    w_qkv, gain, *parts, qkv_grad, proj_grad, router_grad, one, two, in_grad, out_grad = rest
    total = own[...]
    for ref in arrived:
        total = total + ref[...].astype(F32)
    qkv = total[:, : 3 * width]
    qkv_grad[...] = qkv
    proj_grad[...] = total[:, 3 * width : 4 * width]
    gain_grad = jnp.sum(qkv * w_qkv[...].astype(F32), axis=1, keepdims=True)
    tail = total[:, 4 * width :]
    share = own.shape[0]
    diagonal = lax.broadcasted_iota(jnp.int32, (share, share), 0) == lane_iota(share, share)

    def turned(column):
        return jnp.sum(jnp.where(diagonal, column, 0.0), axis=0, keepdims=True)

    one[...] = turned(gain_grad) / gain[...].astype(F32)
    two[...] = turned(tail[:, experts + 1 : experts + 2])
    for index in range(experts):
        router_grad[index : index + 1, :] = turned(tail[:, index : index + 1])
    mine, upper, lower, other = parts
    for out, at, beside in (
        (in_grad, slice(0, width), upper),
        (out_grad, slice(width, 2 * width), lower),
    ):
        out[0] = mine[at, :].astype(F32) + beside[...].astype(F32) + other[at, :].astype(F32)


def gather_stages(devices):
    bits = devices.bit_length() - 1
    stages = []
    top = bits - 1
    while top >= 1:
        if top >= 2:
            low, high = 1 << (top - 1), 1 << top
            stages.append([low, high, low | high])
            top -= 2
        else:
            stages.append([1 << top])
            top -= 1
    stages.append([1])
    return stages


def swap(value, devices, mask):
    return lax.ppermute(value, "dp", [(i, i ^ mask) for i in range(devices)])


def reduce_scattered(kept, sent, devices, stages, before, after):
    total = kept
    arrived = [swap(part, devices, stages[-1][0]) for part in sent]
    for level in range(len(stages) - 1, 0, -1):
        masks = stages[level - 1]
        parts = 1 + len(masks)
        dims = (total.shape[0] // parts, total.shape[1])
        outs = [shape(dims, F32)] + [shape(dims, BF)] * (parts - 1)
        if level == 1:
            arrived, before[-1], after = lax.optimization_barrier((arrived, before[-1], after))
        if level == 2:
            arrived, before[:-1] = lax.optimization_barrier((arrived, before[:-1]))
        pieces = call(
            functools.partial(sum_body, parts), outs, [total] + arrived, name=f"sum{level}"
        )
        total = pieces[0]
        arrived = [swap(piece, devices, mask) for piece, mask in zip(pieces[1:], masks)]
    return total, arrived, before, after


def per_device(
    tokens,
    gain_attn,
    w_qkv,
    w_proj,
    gain_moe,
    w_router,
    w_in,
    w_out,
    cotangent,
    image_ids,
    expert_ids,
    slots,
):
    devices = lax.axis_size("dp")
    experts = devices // 4
    rows, width = tokens.shape
    capacity = max(2, 5 * rows // (2 * experts))
    share = width // devices
    span = rows + 2 * HALO
    stages = gather_stages(devices)
    everyone = range(devices)
    half = devices // 2

    ins = [
        w_qkv,
        w_proj,
        w_router.T,
        gain_attn[None, :],
        gain_moe[None, :],
        tokens,
        image_ids.reshape(rows // BLOCK, BLOCK),
    ]
    packed, own, low, high = call(
        functools.partial(pack_body, experts),
        [
            shape((share, 4 * width + LANES), BF),
            shape((rows, width + LANES), BF),
            shape((HALO, width + LANES), BF),
            shape((HALO, width + LANES), BF),
        ],
        ins,
        scratch=[pltpu.VMEM(x.shape, x.dtype) for x in ins]
        + [pltpu.SemaphoreType.DMA((len(ins),))],
        name="pack",
        fetch=True,
    )
    up = [(i, i + 1) for i in range(devices - 1)]
    down = [(i + 1, i) for i in range(devices - 1)]
    low = lax.ppermute(low, "dp", up)
    high = lax.ppermute(high, "dp", down)
    packed, w_in = lax.optimization_barrier((packed, w_in))
    quarter = call(
        functools.partial(quarter_body, width),
        [shape((2 * width, width), BF)],
        [w_in, w_out],
        scratch=[pltpu.SemaphoreType.DMA((2,))],
        name="quarter",
        fetch=True,
    )[0]
    order = [0]
    for stage in stages:
        order = [a ^ mask for mask in [0] + stage for a in order]
    order = np.stack(
        [
            np.repeat(np.array(order, np.int32), share),
            np.tile(np.arange(share, dtype=np.int32), devices),
        ]
    )
    packed, own = lax.optimization_barrier((packed, own))
    xhat, rstd, select, routes, place_row = call(
        functools.partial(prepare_body, width, experts, capacity),
        [
            shape((rows, width), F32),
            shape((rows, LANES), F32),
            shape((width, width), BF),
            shape((rows, LANES), F32),
            shape((8, rows), F32),
        ],
        [own, jnp.asarray(order), expert_ids.T, slots.T],
        name="prepare",
    )
    near = [packed]
    far = None
    for stage in stages:
        arrived = [swap(part, devices, mask) for mask in stage for part in near]
        if stage is stages[0]:
            arrived[0], low, high, quarter = lax.optimization_barrier(
                (arrived[0], low, high, quarter)
            )
            arrived[1], quarter_far = lax.optimization_barrier((arrived[1], quarter))
            arrived[2], xhat = lax.optimization_barrier((arrived[2], xhat))
        if stage is stages[-2]:
            *arrived, late_in = lax.optimization_barrier((*arrived, w_in[0]))
        if stage is stages[-1]:
            far = arrived
        else:
            parts = 2 if stage is stages[-2] else 1
            size = near[0].shape[0] * (1 + len(stage)) // parts
            near = call(
                functools.partial(join_body, parts),
                [shape((size, near[0].shape[1]), BF)] * parts,
                [*near, *arrived],
                name="join",
            )
    far_quarter = swap(quarter_far, devices, half)
    near_in = swap(late_in, devices, 2)

    def exchange(parts):
        return [parts[0]] + [
            swap(part, devices, 4 * index) for index, part in enumerate(parts) if index
        ]

    xhat_halo, idcol, idrow = call(
        functools.partial(halo_body, width),
        [
            shape((2 * HALO, width), F32),
            shape((span, LANES), F32),
            shape((8, span), F32),
        ],
        [own, low, high, select],
        name="halo",
    )
    chips = experts // 2
    half_slots = chips * capacity
    outs = call(
        functools.partial(forward_body, width, experts, capacity),
        [shape((half_slots, 2 * width), BF)]
        + [shape((capacity, 2 * width), BF)] * chips
        + [
            shape((span, 3 * width), BF),
            shape((rows, width), BF),
            shape((8, rows), F32),
            shape((rows, width), F32),
            shape((rows, width), BF),
            shape((rows, LANES), F32),
            shape((span, width), BF),
            shape((width, 3 * width), BF),
            shape((width, width + LANES), BF),
            shape((8, width), F32),
        ],
        [xhat, xhat_halo, idcol, idrow, select, own, cotangent, routes, place_row, *near, *far],
        name="forward",
    )
    same_core, other_core, outs = outs[0], outs[1 : 1 + chips], outs[1 + chips :]
    qkv, attended, lse, middle, normed_two, probs, normed, weights, weights_tail, gain = outs

    both = shape((2 * capacity, 2 * width), BF)
    *other_core, near_in = lax.optimization_barrier((*other_core, near_in))
    pieces = call(
        functools.partial(mix_body, capacity),
        [both] * chips,
        [same_core, *[swap(part, devices, 1) for part in other_core]],
        name="mix",
    )
    far_quarter, late_out, piece = lax.optimization_barrier((far_quarter, w_out[0], pieces[0]))
    near_out = swap(late_out, devices, 2)
    arrived = exchange([piece, *pieces[1:]])
    far_half = call(
        halve_body, [shape((width, width), BF)] * 2, [far_quarter], name="halve"
    )
    far_half = [*far_half] + [swap(part, devices, 2) for part in far_half]
    slot_count = experts * capacity
    pair = shape((4 * width, width), BF)
    far_half[-1], *arrived[1:-1] = lax.optimization_barrier((far_half[-1], *arrived[1:-1]))
    kept_pair, *sent_parts = call(
        functools.partial(choose_body, half, width),
        [pair] + [shape((width, width), BF)] * 4,
        [quarter, near_in, near_out, *far_half],
        name="choose",
    )
    expert_weights = [kept_pair] + [swap(part, devices, 1) for part in sent_parts]
    tile = slot_count // 4
    held = pltpu.VMEM((slot_count, 2 * width), BF)
    back, hidden, pre_grad = [], [], []
    for part in (arrived[: chips // 2], arrived[chips // 2 :]):
        half_held = pltpu.VMEM((half_slots, 2 * width), BF)
        outs = call(
            functools.partial(expert_body, width, tile, len(part)),
            [both] * len(part) + [shape((half_slots, 4 * width), BF)] * 2,
            [*part, *expert_weights],
            scratch=[
                half_held,
                half_held,
                pltpu.VMEM((width, 4 * width), BF),
                pltpu.VMEM((4 * width, width), BF),
            ],
            flops=4 * slot_count * width * 4 * width,
            name="expert",
            vmem_mib=16,
        )
        back += outs[: len(part)]
        hidden.append(outs[-2])
        pre_grad.append(outs[-1])
    returned = exchange(back)
    kept_pair, sent_pair = call(
        functools.partial(expert_grad_body, width, chips),
        [pair, pair],
        [*arrived, *hidden, *pre_grad],
        vmem_mib=16,
        flops=4 * slot_count * width * 4 * width,
        name="expert_grad",
    )
    other_pair = swap(sent_pair, devices, 1)
    single = shape((2 * width, width), BF)
    square = shape((width, width), BF)
    home_kept, *home_sent = call(
        functools.partial(split_body, half, 2 * width),
        [single, square, square] * 2 + [shape((width, span), BF)],
        [kept_pair, other_pair, weights, normed],
        name="split",
    )
    home_sent, (away_kept, *away_sent, keys_turned) = home_sent[:2], home_sent[2:]
    away_came = [swap(part, devices, 2) for part in away_sent]
    *home_sent, returned[1] = lax.optimization_barrier((*home_sent, returned[1]))
    home_came = [swap(part, devices, 2) for part in home_sent]
    away = call(
        functools.partial(sum_body, 1), [single], [away_kept, *away_came], name="away"
    )[0]

    returned[-1], away = lax.optimization_barrier((returned[-1], away))
    mine, *theirs = call(
        functools.partial(unmix_body, capacity),
        [shape((half_slots, 2 * width), BF)] + [shape((capacity, 2 * width), BF)] * chips,
        returned,
        name="unmix",
    )
    theirs = [swap(part, devices, 1) for part in theirs]
    mixed, middle_grad, attended_grad, tail_grad = call(
        functools.partial(combine_body, width, experts, capacity),
        [
            shape((rows, width), BF),
            shape((rows, width), F32),
            shape((rows, width), BF),
            shape((width, width + LANES), BF),
        ],
        [
            middle,
            normed_two,
            probs,
            cotangent,
            routes,
            attended,
            weights_tail,
            select,
            mine,
            *theirs,
        ],
        scratch=[pltpu.VMEM((slot_count, 2 * width), BF)],
        flops=6 * rows * slot_count * width,
        name="combine",
    )
    expert_parts = [home_kept, *home_came, swap(away, devices, half)]
    half_rows = width // 2

    dq, rims_low, rims_high, inner, kept, *sent = call(
        functools.partial(backward_body, width),
        [
            shape((rows, width), BF),
            shape((HALO, 2 * width), BF),
            shape((HALO, 2 * width), BF),
            shape((rows, 2 * width), F32),
            shape((half_rows, 4 * width + LANES), F32),
        ]
        + [shape((half_rows // 4, 4 * width + LANES), BF)] * 4,
        [qkv, keys_turned, lse, attended_grad, idcol, idrow, normed, tail_grad],
        scratch=[pltpu.VMEM((span, 2 * width), F32)],
        name="backward",
    )
    total, last, expert_parts, (rims_low, rims_high) = reduce_scattered(
        kept, sent, devices, stages, expert_parts, [rims_low, rims_high]
    )
    from_high = lax.ppermute(rims_low, "dp", down)
    from_low = lax.ppermute(rims_high, "dp", up)
    grad_tokens = call(
        functools.partial(finish_body, width),
        [shape((rows, width), BF)],
        [dq, inner, from_low, from_high, weights, gain, xhat, rstd, select, middle_grad],
        scratch=[pltpu.VMEM((rows, 2 * width), F32)],
        flops=2 * rows * width * 5 * width,
        name="finish",
    )[0]

    last[0], grad_tokens = lax.optimization_barrier((last[0], grad_tokens))
    qkv_grad, proj_grad, router_grad, gain_one_grad, gain_two_grad, in_grad, out_grad = call(
        functools.partial(final_body, width, experts),
        [
            shape((share, 3 * width), F32),
            shape((share, width), F32),
            shape((experts, share), F32),
            shape((1, share), F32),
            shape((1, share), F32),
            shape((1, width, width), F32),
            shape((1, width, width), F32),
        ],
        [total, *last, w_qkv, gain_attn[None, :], *expert_parts],
        name="final",
    )
    return (
        mixed,
        grad_tokens,
        gain_one_grad.reshape(share),
        qkv_grad,
        proj_grad,
        gain_two_grad.reshape(share),
        router_grad.T,
        in_grad,
        out_grad,
    )


def solution(mesh):
    row, line, cube = P("dp", None), P("dp"), P("dp", None, None)
    return jax.shard_map(
        per_device,
        mesh=mesh,
        in_specs=(row, line, row, row, line, row, cube, cube, row, line, row, row),
        out_specs=(row, row, line, row, row, line, row, cube, cube),
        check_vma=False,
    )
```

```python
import functools

import jax
import jax.numpy as jnp
import numpy as np
from jax import lax
from jax.experimental import pallas as pl
from jax.experimental.pallas import tpu as pltpu
from jax.sharding import PartitionSpec as P

HEAD_DIM = 64
LEN = 197
EPSILON = 1e-06
MASKED = -1e30
HALO = 256
RIM = 208
BLOCK = 128
WINDOW = BLOCK + 2 * HALO
LANES = 128
SCALE = HEAD_DIM ** (-0.5)
BF = jnp.bfloat16
F32 = jnp.float32
GELU_C = (2.0 / np.pi) ** 0.5
GELU_A = 0.044715


def dot(left, right, left_dim=1, right_dim=0):
    return lax.dot_general(
        left,
        right,
        (((left_dim,), (right_dim,)), ((), ())),
        preferred_element_type=F32,
    )


def call(body, outs, ins, scratch=(), flops=0, name=None, vmem_mib=12, fetch=False):
    vmem = pl.BlockSpec(memory_space=pltpu.VMEM)
    spec = pl.BlockSpec(memory_space=pltpu.HBM) if fetch else vmem
    if fetch:
        ins = [pltpu.with_memory_space_constraint(x, pltpu.HBM) for x in ins]
    return pl.pallas_call(
        body,
        out_shape=tuple(outs),
        in_specs=[spec] * len(ins),
        out_specs=tuple([vmem] * len(outs)),
        scratch_shapes=list(scratch),
        compiler_params=pltpu.CompilerParams(vmem_limit_bytes=vmem_mib * 1024 * 1024),
        cost_estimate=pl.CostEstimate(flops=int(flops), bytes_accessed=1024, transcendentals=0),
        name=name,
    )(*ins)


def shape(dims, dtype):
    return jax.ShapeDtypeStruct(dims, dtype)


def lane_iota(rows, lanes=LANES):
    return lax.broadcasted_iota(jnp.int32, (rows, lanes), 1)


def fetched(refs, held, sems):
    copies = [
        pltpu.make_async_copy(ref, into, sems.at[index])
        for index, (ref, into) in enumerate(zip(refs, held))
    ]
    for copy in copies:
        copy.start()
    for copy in copies:
        copy.wait()


def pack_body(experts, *refs):
    count = 7
    (out, own, low, high), held, sems = refs[count : count + 4], refs[count + 4 : -1], refs[-1]
    fetched(refs[:count], held, sems)
    w_qkv, w_proj, router_turned, gain_attn, gain_moe, tokens, ids = held
    share, cols = w_qkv.shape
    width = cols // 3
    out[:, :cols] = w_qkv[...]
    out[:, cols : 4 * width] = w_proj[...]
    lanes = lane_iota(share)
    diagonal = lax.broadcasted_iota(jnp.int32, (share, share), 0) == lane_iota(share, share)
    pick = lax.broadcasted_iota(jnp.int32, (experts, LANES), 0) == lane_iota(experts)
    tail = dot(router_turned[...], pick.astype(F32).astype(BF), 0, 0)
    for index, gain in enumerate((gain_attn, gain_moe)):
        column = jnp.sum(
            jnp.where(diagonal, gain[...].astype(F32), 0.0), axis=1, keepdims=True
        )
        tail = jnp.where(lanes == experts + index, column, tail)
    out[:, 4 * width :] = tail.astype(BF)
    rows = tokens.shape[0]
    own[:, :width] = tokens[...]
    for index in range(rows // BLOCK):
        line = (ids[index : index + 1, :] + 1).astype(F32)
        column = jnp.broadcast_to(line, (BLOCK, BLOCK)).T
        upper = jnp.floor(column * (1.0 / 256.0))
        lower = column - 256.0 * upper
        own[index * BLOCK : (index + 1) * BLOCK, width:] = jnp.where(
            lane_iota(BLOCK) == 0, upper, lower
        ).astype(BF)
    low[...] = own[rows - RIM :, :]
    high[...] = own[:RIM, :]


def quarter_body(width, w_in, w_out, quarter, sems):
    fetched(
        (w_in.at[0], w_out.at[0]), (quarter.at[:width, :], quarter.at[width:, :]), sems
    )


def join_body(parts, *refs):
    pieces, outs = refs[:-parts], refs[-parts:]
    whole = jnp.concatenate([piece[...].astype(F32) for piece in pieces], axis=0).astype(BF)
    size = whole.shape[0] // parts
    for index, out in enumerate(outs):
        out[...] = whole[index * size : (index + 1) * size, :]


def prepare_body(
    width,
    experts,
    capacity,
    own,
    low,
    high,
    order,
    experts_row,
    slots_row,
    xhat,
    rstd_out,
    select,
    idcol,
    idrow,
    routes,
    place_row,
):
    me = lax.axis_index("dp")
    devices = 4 * experts
    share = width // devices
    target = (me ^ order[0:1, :]) * share + order[1:2, :]
    sel = (lax.broadcasted_iota(jnp.int32, (width, width), 0) == target).astype(F32).astype(BF)
    select[...] = sel
    start = 0
    blank = jnp.zeros((HALO - RIM, width + LANES), BF)
    for ref in (low, own, high):
        part = ref[...]
        if ref is low:
            part = jnp.concatenate([blank, part], axis=0)
        if ref is high:
            part = jnp.concatenate([part, blank], axis=0)
        rows = part.shape[0]
        values = dot(part[:, :width], sel)
        mean = jnp.mean(values, axis=1, keepdims=True)
        centered = values - mean
        rstd = lax.rsqrt(jnp.mean(centered * centered, axis=1, keepdims=True) + EPSILON)
        xhat[start : start + rows, :] = centered * rstd
        rstd_out[start : start + rows, :] = jnp.broadcast_to(rstd, (rows, LANES))
        marks = part[:, width:].astype(F32)
        column = marks[:, 0:1] * 256.0 + marks[:, 1:2]
        idcol[start : start + rows, :] = jnp.broadcast_to(column, (rows, LANES))
        turned = marks.T
        line = turned[0:1, :] * 256.0 + turned[1:2, :]
        idrow[:, start : start + rows] = jnp.broadcast_to(line, (8, rows))
        start += rows
    rows = own.shape[0]
    group = (((me >> 2) & (experts // 2 - 1)) << 1) | (me & 1)
    half_bits = (experts // 2).bit_length() - 1
    expert = experts_row[...]
    slot = slots_row[...]
    holder = ((expert & (experts // 2 - 1)) << 1) | (expert >> half_bits)
    apart = group ^ holder
    index = (apart & 1) * (experts // 2) + (apart >> 1)
    place = jnp.where(slot >= 0, index * capacity + slot, -1).astype(F32)
    lines = jnp.concatenate(
        [place, expert.astype(F32), jnp.zeros((4, rows), F32)], axis=0
    )
    place_row[...] = lines
    routes[...] = jnp.concatenate([lines] * (LANES // 8), axis=0).T


def stacked(values, half):
    zero = jnp.zeros_like(values)
    return jnp.concatenate(
        [jnp.where(half, values, zero), jnp.where(half, zero, values)], axis=0
    )


def forward_body(
    width,
    experts,
    capacity,
    xhat,
    idcol,
    idrow,
    select,
    own,
    cotangent,
    routes,
    place_row,
    near_one,
    near_two,
    far_one,
    far_two,
    *outs,
):
    same_core, other_core, outs = outs[0], outs[1 : 1 + experts // 2], outs[1 + experts // 2 :]
    qkv, attended, lse, middle, normed_two, probs, normed, weights, weights_tail, gain = outs
    rows = own.shape[0]
    span = xhat.shape[0]
    cols = 3 * width
    parts = (near_one, near_two, far_one, far_two)
    size = width // 4
    for index, part in enumerate(parts):
        weights[index * size : (index + 1) * size, :] = part[:, :cols]
    sel = select[...]
    tail = jnp.concatenate([part[:, cols:] for part in parts], axis=0)
    gain_row = tail[:, width:].astype(F32).T[experts : experts + 1, :]
    gain[...] = jnp.broadcast_to(gain_row, (8, width))
    natural = dot(sel, tail)
    weights_tail[...] = natural.astype(BF)
    gain_two = natural[:, width:].T[experts + 1 : experts + 2, :]
    normed[...] = (xhat[...] * gain_row).astype(BF)
    qkv[HALO : HALO + rows, :] = dot(normed[HALO : HALO + rows, :], weights[...]).astype(BF)
    for first in (0, HALO + rows):
        qkv[first : first + HALO, width:] = dot(
            normed[first : first + HALO, :], weights[:, width:]
        ).astype(BF)
    half = lane_iota(BLOCK) < HEAD_DIM

    def attend(block, carry):
        base = pl.multiple_of(block * BLOCK, BLOCK)
        window = pl.ds(base, WINDOW)
        here = pl.ds(base, BLOCK)
        marks = idrow[0:1, pl.ds(base + HALO, BLOCK)]
        same = idcol[window, 0:1] == jnp.concatenate([marks, marks], axis=1)
        for pair in range(width // LANES):
            start = pair * LANES
            queries = qkv[pl.ds(base + HALO, BLOCK), start : start + LANES]
            queries = stacked((queries.astype(F32) * SCALE).astype(BF), half)
            keys = qkv[window, width + start : width + start + LANES]
            values = qkv[window, 2 * width + start : 2 * width + start + LANES]
            scores = jnp.where(same, dot(keys, queries, 1, 1), MASKED)
            peak = jnp.max(scores, axis=0, keepdims=True)
            raised = jnp.exp(scores - peak)
            total = jnp.sum(raised, axis=0, keepdims=True)
            result = dot(raised.astype(BF), values, 0, 0)
            column = jnp.broadcast_to(1.0 / total, (8, 2 * BLOCK)).T[:, 0:1]
            result = result * column
            attended[here, start : start + LANES] = jnp.where(
                half, result[:BLOCK], result[BLOCK:]
            ).astype(BF)
            logs = peak + jnp.log(total)
            lse[2 * pair : 2 * pair + 1, here] = logs[:, :BLOCK]
            lse[2 * pair + 1 : 2 * pair + 2, here] = logs[:, BLOCK:]
        return carry

    lax.fori_loop(0, rows // BLOCK, attend, 0, unroll=4)
    mid = own[:, :width].astype(F32) + dot(attended[...], weights_tail[:, :width])
    middle[...] = mid
    centered = mid - jnp.mean(mid, axis=1, keepdims=True)
    variance = jnp.mean(centered * centered, axis=1, keepdims=True)
    low_two = (centered * lax.rsqrt(variance + EPSILON) * gain_two).astype(BF)
    normed_two[...] = low_two
    lanes = lane_iota(rows)
    logits = jnp.where(lanes < experts, dot(low_two, weights_tail[:, width:]), MASKED)
    raised = jnp.exp(logits - jnp.max(logits, axis=1, keepdims=True))
    share = raised / jnp.sum(raised, axis=1, keepdims=True)
    probs[...] = share
    upstream = cotangent[...].astype(F32)
    wide_lanes = lanes.astype(F32)
    gates = []
    for choice in range(2):
        gate = jnp.sum(
            jnp.where(wide_lanes == routes[:, 2 + choice : 3 + choice], share, 0.0),
            axis=1,
            keepdims=True,
        )
        gates.append(jnp.broadcast_to(gate, (rows, 8)))
    gates = jnp.concatenate(gates + [jnp.zeros((rows, LANES - 16), F32)], axis=1).T
    source = jnp.concatenate([low_two, cotangent[...]], axis=1)
    for index in range(experts):
        if index < experts // 2:
            chunk = same_core.at[index * capacity : (index + 1) * capacity, :]
        else:
            chunk = other_core[index - experts // 2]
        slot = (
            lax.broadcasted_iota(jnp.int32, (capacity, rows), 0) + index * capacity
        ).astype(F32)
        first = slot == place_row[0:1, :]
        second = slot == place_row[1:2, :]
        weight = jnp.where(first, gates[0:1, :], jnp.where(second, gates[8:9, :], 0.0))
        taken = jnp.where(first | second, 1.0, 0.0)
        moved = dot(taken.astype(BF), source)
        chunk[:, :width] = moved[:, :width].astype(BF)
        chunk[:, width:] = (
            moved[:, width:] * jnp.sum(weight, axis=1, keepdims=True)
        ).astype(BF)


def joined(pieces, held):
    capacity = pieces[0].shape[0]
    for index, piece in enumerate(pieces):
        held[index * capacity : (index + 1) * capacity, :] = piece[...]


def expert_body(width, tile, count, *refs):
    pieces, kept, sent, rest = (
        refs[:count],
        refs[count],
        refs[count + 1 : count + 5],
        refs[count + 5 :],
    )
    returns, (hidden_out, grad_out, arrived, back, w_in, w_out) = rest[:count], rest[count:]
    joined(pieces, arrived)
    w_ins = [kept.at[:width, :], kept.at[2 * width : 3 * width, :], sent[0], sent[2]]
    w_outs = [kept.at[width : 2 * width, :], kept.at[3 * width :, :], sent[1], sent[3]]
    for quarter, (first, second) in enumerate(zip(w_ins, w_outs)):
        at = slice(quarter * width, (quarter + 1) * width)
        w_in[:, at] = first[...]
        w_out[at, :] = second[...]
    step_width = 2 * width // 3

    def step(index, carry):
        at = pl.ds(pl.multiple_of(index * tile, tile), tile)
        for start in range(0, 4 * width, step_width):
            columns = slice(start, start + step_width)
            pre = dot(arrived[at, :width], w_in[:, columns])
            hidden_grad = dot(arrived[at, width:], w_out[columns, :], 1, 1)
            square = pre * pre
            bend = jnp.tanh(pre * (GELU_C + (GELU_C * GELU_A) * square))
            scaled = 0.5 * pre
            hidden_out[at, columns] = (scaled + scaled * bend).astype(BF)
            slope = (0.5 + 0.5 * bend) + (
                scaled * (GELU_C + (3.0 * GELU_C * GELU_A) * square)
            ) * (1.0 - bend * bend)
            grad_out[at, columns] = (hidden_grad * slope).astype(BF)
        back[at, :width] = dot(hidden_out[at, :], w_out[...]).astype(BF)
        back[at, width:] = dot(grad_out[at, :], w_in[...], 1, 1).astype(BF)
        return carry

    lax.fori_loop(0, arrived.shape[0] // tile, step, 0)
    capacity = pieces[0].shape[0]
    for index, out in enumerate(returns):
        out[...] = back[index * capacity : (index + 1) * capacity, :]


def expert_grad_body(width, count, *refs):
    pieces, (hidden_one, hidden_two, pre_one, pre_two, kept, sent) = refs[:count], refs[count:]
    size = 2 * width
    outs = (kept.at[:size, :], kept.at[size:, :], sent.at[:size, :], sent.at[size:, :])
    grad_in = grad_out = 0.0
    for part, hidden, pre_grad in (
        (pieces[: count // 2], hidden_one, pre_one),
        (pieces[count // 2 :], hidden_two, pre_two),
    ):
        rows = jnp.concatenate([piece[:, :width] for piece in part], axis=0)
        grads = jnp.concatenate([piece[:, width:] for piece in part], axis=0)
        grad_in = grad_in + dot(rows, pre_grad[...], 0, 0)
        grad_out = grad_out + dot(grads, hidden[...], 0, 0)
    for quarter, out in enumerate(outs):
        columns = slice(quarter * width, (quarter + 1) * width)
        out[:width, :] = grad_in[:, columns].astype(BF)
        out[width:, :] = grad_out[:, columns].T.astype(BF)


def at_home(half):
    me = lax.axis_index("dp")
    return (me >= half) == ((me & 1) == 1)


def halve_body(whole, upper, lower):
    size = upper.shape[0]
    upper[...] = whole[:size, :]
    lower[...] = whole[size:, :]


def choose_body(half, size, near_one, near_in, near_out, *refs):
    far, kept, sent = refs[:4], refs[4], refs[5:]
    near = (near_one.at[:size, :], near_one.at[size:, :], near_in, near_out)

    def place(mine, theirs):
        for index, (one, two) in enumerate(zip(mine, theirs)):
            kept[index * size : (index + 1) * size, :] = one[...]
            sent[index][...] = two[...]

    @pl.when(at_home(half))
    def _():
        place(near, far)

    @pl.when(jnp.logical_not(at_home(half)))
    def _():
        place(far, near)


def mix_body(capacity, mine, *refs):
    theirs, outs = refs[: len(refs) // 2], refs[len(refs) // 2 :]
    for index, (part, out) in enumerate(zip(theirs, outs)):
        out[:capacity, :] = mine[index * capacity : (index + 1) * capacity, :]
        out[capacity:, :] = part[...]


def unmix_body(capacity, *refs):
    count = len(refs) // 2
    pieces, mine, theirs = refs[:count], refs[count], refs[count + 1 :]
    for index, (piece, out) in enumerate(zip(pieces, theirs)):
        mine[index * capacity : (index + 1) * capacity, :] = piece[:capacity, :]
        out[...] = piece[capacity:, :]


def split_body(half, size, mine, theirs, weights, normed, *outs):
    home_one, home_two, home_three, *away, keys_turned = outs
    width = size // 2
    keys_turned[...] = dot(weights[:, width : 2 * width], normed[...], 0, 1).astype(BF)

    def place(home, other):
        home_one[...] = home[:size, :]
        home_two[...], home_three[...] = home[size : 3 * size // 2, :], home[3 * size // 2 :, :]
        away[0][...] = other[:size, :]
        away[1][...], away[2][...] = other[size : 3 * size // 2, :], other[3 * size // 2 :, :]

    @pl.when(at_home(half))
    def _():
        place(mine, theirs)

    @pl.when(jnp.logical_not(at_home(half)))
    def _():
        place(theirs, mine)


def combine_body(
    width,
    experts,
    capacity,
    middle,
    normed_two,
    probs,
    cotangent,
    routes,
    attended,
    weights_tail,
    select,
    *refs,
):
    mixed, middle_grad, attended_grad, tail_grad, held = refs[-5:]
    start = 0
    for ref in refs[:-5]:
        held[start : start + ref.shape[0], :] = ref[...]
        start += ref.shape[0]
    rows = middle.shape[0]
    slots = experts * capacity
    gain_two = weights_tail[:, width:].astype(F32).T[experts + 1 : experts + 2, :]
    gain_grad = jnp.zeros((1, width), F32)
    router_rows = []
    branch_rows = []
    tile = rows
    for start in range(0, rows, tile):
        at = slice(start, start + tile)
        lanes = lane_iota(tile).astype(F32)
        wide = lax.broadcasted_iota(jnp.int32, (tile, slots), 1).astype(F32)
        first = (wide == routes[at, 0:1]).astype(F32)
        second = (wide == routes[at, 1:2]).astype(F32)
        picked = dot(
            jnp.concatenate([first, second], axis=0).astype(BF), held[:, :width]
        )
        grad_two = dot((first + second).astype(BF), held[:, width:])
        upstream = cotangent[at, :].astype(F32)
        share = probs[at, :]
        mid = middle[at, :]
        total = mid
        probs_grad = jnp.zeros((tile, LANES), F32)
        for choice in range(2):
            chosen = lanes == routes[at, 2 + choice : 3 + choice]
            gate = jnp.sum(jnp.where(chosen, share, 0.0), axis=1, keepdims=True)
            one = picked[choice * tile : (choice + 1) * tile, :]
            total = total + gate * one
            gate_grad = jnp.sum(one * upstream, axis=1, keepdims=True)
            probs_grad = probs_grad + jnp.where(chosen, gate_grad, 0.0)
        mixed[at, :] = total.astype(BF)
        logits_grad = (
            share * (probs_grad - jnp.sum(share * probs_grad, axis=1, keepdims=True))
        ).astype(BF)
        router_rows.append(logits_grad)
        grad_two = grad_two + dot(logits_grad, weights_tail[:, width:], 1, 1)
        centered = mid - jnp.mean(mid, axis=1, keepdims=True)
        variance = jnp.mean(centered * centered, axis=1, keepdims=True)
        rstd = lax.rsqrt(variance + EPSILON)
        xhat = centered * rstd
        gain_grad = gain_grad + jnp.sum(grad_two * xhat, axis=0, keepdims=True)
        inner = grad_two * gain_two
        inner_grad = rstd * (
            inner
            - jnp.mean(inner, axis=1, keepdims=True)
            - xhat * jnp.mean(inner * xhat, axis=1, keepdims=True)
        )
        through = upstream + inner_grad
        middle_grad[at, :] = through
        branch = through.astype(BF)
        branch_rows.append(branch)
        attended_grad[at, :] = dot(branch, weights_tail[:, :width], 1, 1).astype(BF)
    sel = select[...]
    logits_grad = jnp.concatenate(router_rows, axis=0)
    branch = jnp.concatenate(branch_rows, axis=0)
    attended_turned = dot(attended[...], sel).astype(BF)
    normed_turned = dot(normed_two[...], sel).astype(BF)
    tail_grad[:, :width] = dot(attended_turned, branch, 0, 0).astype(BF)
    gain_line = jnp.broadcast_to(gain_grad, (8, width))
    upper = gain_line.astype(BF)
    lower = (gain_line - upper.astype(F32)).astype(BF)
    gain_turned = dot(upper, sel) + dot(lower, sel)
    gain_column = jnp.broadcast_to(gain_turned[0:1, :], (LANES, width)).T
    router_grad = dot(normed_turned, logits_grad, 0, 0)
    tail_grad[:, width:] = jnp.where(
        lane_iota(width) == experts + 1, gain_column, router_grad
    ).astype(BF)


def backward_body(
    width,
    qkv,
    keys_turned,
    lse,
    attended_grad,
    idcol,
    idrow,
    normed,
    tail_grad,
    dq,
    rims_low,
    rims_high,
    inner,
    kept,
    *sents,
):
    rows = attended_grad.shape[0]
    half_rows = width // 2
    *sents, acc = sents
    half = lane_iota(BLOCK) < HEAD_DIM
    upper = lax.broadcasted_iota(jnp.int32, (LANES, BLOCK), 0) < HEAD_DIM
    acc[...] = jnp.zeros_like(acc)

    def attend(block, carry):
        base = pl.multiple_of(block * BLOCK, BLOCK)
        window = pl.ds(base, WINDOW)
        here = pl.ds(base, BLOCK)
        marks = idrow[0:1, pl.ds(base + HALO, BLOCK)]
        same = idcol[window, 0:1] == jnp.concatenate([marks, marks], axis=1)
        for pair in range(width // LANES):
            start = pair * LANES
            queries = qkv[pl.ds(base + HALO, BLOCK), start : start + LANES]
            queries = stacked((queries.astype(F32) * SCALE).astype(BF), half)
            grads = stacked(attended_grad[here, start : start + LANES], half)
            keys = qkv[window, width + start : width + start + LANES]
            values = qkv[window, 2 * width + start : 2 * width + start + LANES]
            logs = jnp.concatenate(
                [lse[2 * pair : 2 * pair + 1, here], lse[2 * pair + 1 : 2 * pair + 2, here]], axis=1
            )
            scores = jnp.where(same, dot(keys, queries, 1, 1), MASKED)
            weights = jnp.exp(scores - logs)
            weights_grad = dot(values, grads, 1, 1)
            delta = jnp.sum(weights * weights_grad, axis=0, keepdims=True)
            scores_grad = (weights * (weights_grad - delta)).astype(BF)
            acc[window, start : start + LANES] += dot(scores_grad, queries)
            acc[window, width + start : width + start + LANES] += dot(weights.astype(BF), grads)
            result = dot(keys_turned[start : start + LANES, window], scores_grad) * SCALE
            dq[here, start : start + LANES] = (
                jnp.where(upper, result[:, :BLOCK], result[:, BLOCK:]).T.astype(BF)
            )
        return carry

    lax.fori_loop(0, rows // BLOCK, attend, 0, unroll=2)
    rims_low[...] = acc[HALO - RIM : HALO, :].astype(BF)
    rims_high[...] = acc[HALO + rows : HALO + rows + RIM, :].astype(BF)
    inner[...] = acc[HALO : HALO + rows, :]
    own = normed[HALO : HALO + rows, :]
    query_part = dot(own, dq[...], 0, 0)
    kept[:, :width] = query_part[:half_rows]
    other_part = dot(normed[...], acc[...].astype(BF), 0, 0)
    kept[:, width : 3 * width] = other_part[:half_rows]
    kept[:, 3 * width :] = tail_grad[:half_rows, :].astype(F32)
    size = half_rows // len(sents)
    for index, sent in enumerate(sents):
        at = slice(half_rows + index * size, half_rows + (index + 1) * size)
        sent[:, :width] = query_part[at].astype(BF)
        sent[:, width : 3 * width] = other_part[at].astype(BF)
        sent[:, 3 * width :] = tail_grad[at, :]


def finish_body(
    width, dq, inner, from_low, from_high, weights, normed_gain, xhat, rstd, select, middle_grad, out, grad
):
    rows = dq.shape[0]
    experts_lane = 0
    grad[...] = inner[...]
    grad[:RIM, :] += from_low[...].astype(F32)
    grad[rows - RIM :, :] += from_high[...].astype(F32)
    values = dot(dq[...], weights[:, :width], 1, 1) + dot(
        grad[...].astype(BF), weights[:, width:], 1, 1
    )
    hat = xhat[HALO : HALO + rows, :]
    values = values * normed_gain[0:1, :]
    part = rstd[HALO : HALO + rows, 0:1] * (
        values
        - jnp.mean(values, axis=1, keepdims=True)
        - hat * jnp.mean(values * hat, axis=1, keepdims=True)
    )
    upper = part.astype(BF)
    lower = (part - upper.astype(F32)).astype(BF)
    sel = select[...]
    out[...] = (middle_grad[...] + dot(upper, sel, 1, 1) + dot(lower, sel, 1, 1)).astype(BF)


def sum_body(parts, own, *refs):
    arrived, outs = refs[: len(refs) - parts], refs[len(refs) - parts :]
    total = own[...].astype(F32)
    if arrived[0].shape[0] < total.shape[0]:
        total = total + jnp.concatenate([ref[...].astype(F32) for ref in arrived], axis=0)
    else:
        for ref in arrived:
            total = total + ref[...].astype(F32)
    size = total.shape[0] // parts
    for index, out in enumerate(outs):
        out[...] = total[index * size : (index + 1) * size, :].astype(out.dtype)


def final_body(width, experts, own, *refs):
    arrived, rest = refs[:-13], refs[-13:]
    w_qkv, gain, *parts, qkv_grad, proj_grad, router_grad, one, two, in_grad, out_grad = rest
    total = own[...]
    for ref in arrived:
        total = total + ref[...].astype(F32)
    qkv = total[:, : 3 * width]
    qkv_grad[...] = qkv
    proj_grad[...] = total[:, 3 * width : 4 * width]
    gain_grad = jnp.sum(qkv * w_qkv[...].astype(F32), axis=1, keepdims=True)
    tail = total[:, 4 * width :]
    share = own.shape[0]
    diagonal = lax.broadcasted_iota(jnp.int32, (share, share), 0) == lane_iota(share, share)

    def turned(column):
        return jnp.sum(jnp.where(diagonal, column, 0.0), axis=0, keepdims=True)

    one[...] = turned(gain_grad) / gain[...].astype(F32)
    two[...] = turned(tail[:, experts + 1 : experts + 2])
    for index in range(experts):
        router_grad[index : index + 1, :] = turned(tail[:, index : index + 1])
    mine, upper, lower, other = parts
    for out, at, beside in (
        (in_grad, slice(0, width), upper),
        (out_grad, slice(width, 2 * width), lower),
    ):
        out[0] = mine[at, :].astype(F32) + beside[...].astype(F32) + other[at, :].astype(F32)


def gather_stages(devices):
    bits = devices.bit_length() - 1
    stages = []
    top = bits - 1
    while top >= 1:
        if top >= 2:
            low, high = 1 << (top - 1), 1 << top
            stages.append([low, high, low | high])
            top -= 2
        else:
            stages.append([1 << top])
            top -= 1
    stages.append([1])
    return stages


def swap(value, devices, mask):
    return lax.ppermute(value, "dp", [(i, i ^ mask) for i in range(devices)])


def reduce_scattered(kept, sent, devices, stages, before, after):
    total = kept
    arrived = [swap(part, devices, stages[-1][0]) for part in sent]
    for level in range(len(stages) - 1, 0, -1):
        masks = stages[level - 1]
        parts = 1 + len(masks)
        dims = (total.shape[0] // parts, total.shape[1])
        outs = [shape(dims, F32)] + [shape(dims, BF)] * (parts - 1)
        if level == 1:
            arrived, before[-1], after = lax.optimization_barrier((arrived, before[-1], after))
        if level == 2:
            arrived, before[:-1] = lax.optimization_barrier((arrived, before[:-1]))
        pieces = call(
            functools.partial(sum_body, parts), outs, [total] + arrived, name=f"sum{level}"
        )
        total = pieces[0]
        arrived = [swap(piece, devices, mask) for piece, mask in zip(pieces[1:], masks)]
    return total, arrived, before, after


def per_device(
    tokens,
    gain_attn,
    w_qkv,
    w_proj,
    gain_moe,
    w_router,
    w_in,
    w_out,
    cotangent,
    image_ids,
    expert_ids,
    slots,
):
    devices = lax.axis_size("dp")
    experts = devices // 4
    rows, width = tokens.shape
    capacity = max(2, 5 * rows // (2 * experts))
    share = width // devices
    span = rows + 2 * HALO
    stages = gather_stages(devices)
    everyone = range(devices)
    half = devices // 2

    ins = [
        w_qkv,
        w_proj,
        w_router.T,
        gain_attn[None, :],
        gain_moe[None, :],
        tokens,
        image_ids.reshape(rows // BLOCK, BLOCK),
    ]
    packed, own, low, high = call(
        functools.partial(pack_body, experts),
        [
            shape((share, 4 * width + LANES), BF),
            shape((rows, width + LANES), BF),
            shape((RIM, width + LANES), BF),
            shape((RIM, width + LANES), BF),
        ],
        ins,
        scratch=[pltpu.VMEM(x.shape, x.dtype) for x in ins]
        + [pltpu.SemaphoreType.DMA((len(ins),))],
        name="pack",
        fetch=True,
    )
    up = [(i, i + 1) for i in range(devices - 1)]
    down = [(i + 1, i) for i in range(devices - 1)]
    low = lax.ppermute(low, "dp", up)
    high = lax.ppermute(high, "dp", down)
    packed, w_in = lax.optimization_barrier((packed, w_in))
    quarter = call(
        functools.partial(quarter_body, width),
        [shape((2 * width, width), BF)],
        [w_in, w_out],
        scratch=[pltpu.SemaphoreType.DMA((2,))],
        name="quarter",
        fetch=True,
    )[0]
    order = [0]
    near = [packed]
    far = None
    for stage in stages:
        order = [a ^ mask for mask in [0] + stage for a in order]
        arrived = [swap(part, devices, mask) for mask in stage for part in near]
        if stage is stages[0]:
            arrived[0], low, high, quarter = lax.optimization_barrier(
                (arrived[0], low, high, quarter)
            )
            arrived[1], quarter_far = lax.optimization_barrier((arrived[1], quarter))
        if stage is stages[-2]:
            *arrived, late_in = lax.optimization_barrier((*arrived, w_in[0]))
        if stage is stages[-1]:
            far = arrived
        else:
            parts = 2 if stage is stages[-2] else 1
            size = near[0].shape[0] * (1 + len(stage)) // parts
            near = call(
                functools.partial(join_body, parts),
                [shape((size, near[0].shape[1]), BF)] * parts,
                [*near, *arrived],
                name="join",
            )
    order = np.stack(
        [
            np.repeat(np.array(order, np.int32), share),
            np.tile(np.arange(share, dtype=np.int32), devices),
        ]
    )

    far_quarter = swap(quarter_far, devices, half)
    near_in = swap(late_in, devices, 2)

    def exchange(parts):
        return [parts[0]] + [
            swap(part, devices, 4 * index) for index, part in enumerate(parts) if index
        ]

    xhat, rstd, select, idcol, idrow, routes, place_row = call(
        functools.partial(prepare_body, width, experts, capacity),
        [
            shape((span, width), F32),
            shape((span, LANES), F32),
            shape((width, width), BF),
            shape((span, LANES), F32),
            shape((8, span), F32),
            shape((rows, LANES), F32),
            shape((8, rows), F32),
        ],
        [own, low, high, jnp.asarray(order), expert_ids.T, slots.T],
        flops=2 * span * width * width,
        name="prepare",
    )
    chips = experts // 2
    half_slots = chips * capacity
    outs = call(
        functools.partial(forward_body, width, experts, capacity),
        [shape((half_slots, 2 * width), BF)]
        + [shape((capacity, 2 * width), BF)] * chips
        + [
            shape((span, 3 * width), BF),
            shape((rows, width), BF),
            shape((8, rows), F32),
            shape((rows, width), F32),
            shape((rows, width), BF),
            shape((rows, LANES), F32),
            shape((span, width), BF),
            shape((width, 3 * width), BF),
            shape((width, width + LANES), BF),
            shape((8, width), F32),
        ],
        [xhat, idcol, idrow, select, own, cotangent, routes, place_row, *near, *far],
        name="forward",
    )
    same_core, other_core, outs = outs[0], outs[1 : 1 + chips], outs[1 + chips :]
    qkv, attended, lse, middle, normed_two, probs, normed, weights, weights_tail, gain = outs

    both = shape((2 * capacity, 2 * width), BF)
    *other_core, near_in = lax.optimization_barrier((*other_core, near_in))
    pieces = call(
        functools.partial(mix_body, capacity),
        [both] * chips,
        [same_core, *[swap(part, devices, 1) for part in other_core]],
        name="mix",
    )
    far_quarter, late_out, piece = lax.optimization_barrier((far_quarter, w_out[0], pieces[0]))
    near_out = swap(late_out, devices, 2)
    arrived = exchange([piece, *pieces[1:]])
    far_half = call(
        halve_body, [shape((width, width), BF)] * 2, [far_quarter], name="halve"
    )
    far_half = [*far_half] + [swap(part, devices, 2) for part in far_half]
    slot_count = experts * capacity
    pair = shape((4 * width, width), BF)
    far_half[-1], *arrived[1:-1] = lax.optimization_barrier((far_half[-1], *arrived[1:-1]))
    kept_pair, *sent_parts = call(
        functools.partial(choose_body, half, width),
        [pair] + [shape((width, width), BF)] * 4,
        [quarter, near_in, near_out, *far_half],
        name="choose",
    )
    expert_weights = [kept_pair] + [swap(part, devices, 1) for part in sent_parts]
    tile = slot_count // 4
    held = pltpu.VMEM((slot_count, 2 * width), BF)
    back, hidden, pre_grad = [], [], []
    for part in (arrived[: chips // 2], arrived[chips // 2 :]):
        half_held = pltpu.VMEM((half_slots, 2 * width), BF)
        outs = call(
            functools.partial(expert_body, width, tile, len(part)),
            [both] * len(part) + [shape((half_slots, 4 * width), BF)] * 2,
            [*part, *expert_weights],
            scratch=[
                half_held,
                half_held,
                pltpu.VMEM((width, 4 * width), BF),
                pltpu.VMEM((4 * width, width), BF),
            ],
            flops=4 * slot_count * width * 4 * width,
            name="expert",
            vmem_mib=16,
        )
        back += outs[: len(part)]
        hidden.append(outs[-2])
        pre_grad.append(outs[-1])
    returned = exchange(back)
    kept_pair, sent_pair = call(
        functools.partial(expert_grad_body, width, chips),
        [pair, pair],
        [*arrived, *hidden, *pre_grad],
        vmem_mib=16,
        flops=4 * slot_count * width * 4 * width,
        name="expert_grad",
    )
    other_pair = swap(sent_pair, devices, 1)
    single = shape((2 * width, width), BF)
    square = shape((width, width), BF)
    home_kept, *home_sent = call(
        functools.partial(split_body, half, 2 * width),
        [single, square, square] * 2 + [shape((width, span), BF)],
        [kept_pair, other_pair, weights, normed],
        name="split",
    )
    home_sent, (away_kept, *away_sent, keys_turned) = home_sent[:2], home_sent[2:]
    away_came = [swap(part, devices, 2) for part in away_sent]
    *home_sent, returned[1] = lax.optimization_barrier((*home_sent, returned[1]))
    home_came = [swap(part, devices, 2) for part in home_sent]
    away = call(
        functools.partial(sum_body, 1), [single], [away_kept, *away_came], name="away"
    )[0]

    returned[-1], away = lax.optimization_barrier((returned[-1], away))
    mine, *theirs = call(
        functools.partial(unmix_body, capacity),
        [shape((half_slots, 2 * width), BF)] + [shape((capacity, 2 * width), BF)] * chips,
        returned,
        name="unmix",
    )
    theirs = [swap(part, devices, 1) for part in theirs]
    mixed, middle_grad, attended_grad, tail_grad = call(
        functools.partial(combine_body, width, experts, capacity),
        [
            shape((rows, width), BF),
            shape((rows, width), F32),
            shape((rows, width), BF),
            shape((width, width + LANES), BF),
        ],
        [
            middle,
            normed_two,
            probs,
            cotangent,
            routes,
            attended,
            weights_tail,
            select,
            mine,
            *theirs,
        ],
        scratch=[pltpu.VMEM((slot_count, 2 * width), BF)],
        flops=6 * rows * slot_count * width,
        name="combine",
    )
    expert_parts = [home_kept, *home_came, swap(away, devices, half)]
    half_rows = width // 2

    dq, rims_low, rims_high, inner, kept, *sent = call(
        functools.partial(backward_body, width),
        [
            shape((rows, width), BF),
            shape((RIM, 2 * width), BF),
            shape((RIM, 2 * width), BF),
            shape((rows, 2 * width), F32),
            shape((half_rows, 4 * width + LANES), F32),
        ]
        + [shape((half_rows // 4, 4 * width + LANES), BF)] * 4,
        [qkv, keys_turned, lse, attended_grad, idcol, idrow, normed, tail_grad],
        scratch=[pltpu.VMEM((span, 2 * width), F32)],
        name="backward",
    )
    total, last, expert_parts, (rims_low, rims_high) = reduce_scattered(
        kept, sent, devices, stages, expert_parts, [rims_low, rims_high]
    )
    from_high = lax.ppermute(rims_low, "dp", down)
    from_low = lax.ppermute(rims_high, "dp", up)
    grad_tokens = call(
        functools.partial(finish_body, width),
        [shape((rows, width), BF)],
        [dq, inner, from_low, from_high, weights, gain, xhat, rstd, select, middle_grad],
        scratch=[pltpu.VMEM((rows, 2 * width), F32)],
        flops=2 * rows * width * 5 * width,
        name="finish",
    )[0]

    last[0], grad_tokens = lax.optimization_barrier((last[0], grad_tokens))
    qkv_grad, proj_grad, router_grad, gain_one_grad, gain_two_grad, in_grad, out_grad = call(
        functools.partial(final_body, width, experts),
        [
            shape((share, 3 * width), F32),
            shape((share, width), F32),
            shape((experts, share), F32),
            shape((1, share), F32),
            shape((1, share), F32),
            shape((1, width, width), F32),
            shape((1, width, width), F32),
        ],
        [total, *last, w_qkv, gain_attn[None, :], *expert_parts],
        name="final",
    )
    return (
        mixed,
        grad_tokens,
        gain_one_grad.reshape(share),
        qkv_grad,
        proj_grad,
        gain_two_grad.reshape(share),
        router_grad.T,
        in_grad,
        out_grad,
    )


def solution(mesh):
    row, line, cube = P("dp", None), P("dp"), P("dp", None, None)
    return jax.shard_map(
        per_device,
        mesh=mesh,
        in_specs=(row, line, row, row, line, row, cube, cube, row, line, row, row),
        out_specs=(row, row, line, row, row, line, row, cube, cube),
        check_vma=False,
    )
```
